32 devices in a mesh: dp: 4 (over y, x), mp: 8 (over z, core).
Axes of the slice: x: 2, y: 2, z: 4, core: 2. Of those that a mesh axis runs over, the one named last changes fastest.
Arguments:
- image_a: bfloat16 [1024, 9216], P('dp', 'mp'), may hold values from -6 to 6
- image_b: bfloat16 [1024, 9216], P('dp', 'mp'), may hold values from -6 to 6
- image_group: int32 [1024], P('dp'), may hold values from 0 to 1
- position_mask: int32 [2, 36], replicated, may hold values 0 or 1
- weight_a: bfloat16 [9216, 4096], P(None, 'mp'), may hold values from -0.0625 to 0.0625
- weight_b: bfloat16 [9216, 4096], P(None, 'mp'), may hold values from -0.0625 to 0.0625
- tower_bias: float32 [2, 4096], P(None, 'mp'), may hold values from -3 to 3
- stitch: float32 [4, 4096], P(None, 'mp'), may hold values from 0.2 to 1
- cotan_a: bfloat16 [1024, 4096], P('dp', 'mp'), may hold values from -6 to 6
- cotan_b: bfloat16 [1024, 4096], P('dp', 'mp'), may hold values from -6 to 6
Outputs:
- stitched_a: bfloat16 [1024, 4096], P('dp')
- stitched_b: bfloat16 [1024, 4096], P('dp')
- grad_image_a: bfloat16 [9216, 1024], P('mp', 'dp')
- grad_image_b: bfloat16 [9216, 1024], P('mp', 'dp')
- grad_weight_a: float32 [9216, 4096], P('dp', 'mp')
- grad_weight_b: float32 [9216, 4096], P('dp', 'mp')
- grad_bias: float32 [2, 4096], P(None, 'mp')
- grad_stitch: float32 [4, 4096], P(None, 'mp')
The draws below stay inside these ranges and needn't reach their ends.
All inputs are finite; a program needn't handle non-finite values.
Results may differ from the reference program's by a relative error of at most 0.005.
Values may be sent and summed in bfloat16 or wider, within the bound.
No kernel may reach another device: no remote copies, remote signals or barrier semaphores. Data moves between devices by JAX's collectives and lax.ppermute only.
A program may use at most 256 MiB of HBM per device.

```python
import jax
import jax.numpy as jnp
from jax import lax

CH = 256
POS = 36
FC = 4096
FEAT = 9216
IMAGES = 1024


def plant(values, key, smallest, high):
    spot = [jax.random.randint(jax.random.fold_in(key, axis), (), 0, length) for axis, length in enumerate(values.shape)]
    longest = values.shape.index(max(values.shape))
    beside = spot[:longest] + [(spot[longest] + 1) % values.shape[longest]] + spot[longest + 1:]
    return values.at[tuple(spot)].set(smallest).at[tuple(beside)].set(high)


def block_scale(own_key, extent, split, low, high):
    loudness = 1.0
    for axis_at, parts in split:
        steps = jax.random.uniform(jax.random.fold_in(jax.random.fold_in(own_key, 6), axis_at), (parts,), jnp.float32, low / len(split), high / len(split))
        loudness = loudness * jnp.repeat(jnp.exp(steps), extent[axis_at] // parts).reshape((-1,) + (1,) * (len(extent) - 1 - axis_at))
    return loudness


def bell_draw(stream_key, dims, spread, limit, shards=(), dtype=jnp.bfloat16):
    result = jax.random.normal(stream_key, dims, jnp.float32) * spread
    if len(shards) > 0:
        result = block_scale(stream_key, dims, shards, -0.22, 0.18) * result
    return jnp.clip(result, min=-limit, max=limit).astype(dtype)


def setup_inputs(seed: int = 0) -> dict:
    seeds = jax.random.split(jax.random.key(seed), 11)
    image_a = bell_draw(seeds[0], (IMAGES, FEAT), 1.0, 6.0, ((0, 4), (1, 8)))
    image_b = bell_draw(seeds[1], (IMAGES, FEAT), 1.0, 6.0, ((0, 4), (1, 8)))
    image_group = plant(jax.random.randint(seeds[2], (IMAGES,), 0, 2), jax.random.fold_in(seeds[2], 1), 0, 1).astype(jnp.int32)
    position_mask = plant((jax.random.randint(seeds[3], (2, POS), 0, 6) < 5).astype(jnp.int32), jax.random.fold_in(seeds[3], 1), 0, 1)
    weight_a = bell_draw(seeds[4], (FEAT, FC), FEAT ** -0.5, 0.0625, ((1, 8),))
    weight_b = bell_draw(seeds[5], (FEAT, FC), FEAT ** -0.5, 0.0625, ((1, 8),))
    tower_bias = bell_draw(seeds[6], (2, FC), 0.5, 3.0, ((1, 8),), jnp.float32)
    stitch = jnp.clip(0.2 + 0.8 * jax.random.uniform(seeds[7], (4, FC), jnp.float32) ** block_scale(seeds[7], (4, FC), ((1, 8),), -0.2, 0.2), 0.2, 1.0)
    cotan_a = bell_draw(seeds[8], (IMAGES, FC), 1.0, 6.0, ((0, 4), (1, 8)))
    cotan_b = bell_draw(seeds[9], (IMAGES, FC), 1.0, 6.0, ((0, 4), (1, 8)))
    return dict(image_a=image_a, image_b=image_b, image_group=image_group, position_mask=position_mask, weight_a=weight_a, weight_b=weight_b, tower_bias=tower_bias, stitch=stitch, cotan_a=cotan_a, cotan_b=cotan_b)


@jax.custom_vjp
def low(v):
    return lax.optimization_barrier(v.astype(jnp.bfloat16)).astype(jnp.float32)

@jax.custom_vjp
def low_back(v):
    return v

def low_keep(v):
    return (low(v), None)

def low_pass(kept, grad):
    return (grad,)

def back_keep(v):
    return (v, None)

def back_low(kept, grad):
    return (low(grad),)
low.defvjp(low_keep, low_pass)
low_back.defvjp(back_keep, back_low)

def reference(image_a, image_b, image_group, position_mask, weight_a, weight_b, tower_bias, stitch, cotan_a, cotan_b):
    mask_f = position_mask.astype(jnp.float32)
    per_image = jnp.where(image_group[:, None] == 1, mask_f[1][None, :], mask_f[0][None, :])
    keep_full = jnp.repeat(per_image, CH, axis=1)

    def forward(feat_a, feat_b, mat_a, mat_b, biases, units):
        masked_a = feat_a * keep_full
        masked_b = feat_b * keep_full
        pre_a = low_back(jnp.dot(masked_a, mat_a, precision=lax.Precision.HIGHEST)) + biases[0][None, :]
        pre_b = low_back(jnp.dot(masked_b, mat_b, precision=lax.Precision.HIGHEST)) + biases[1][None, :]
        hid_a = jax.nn.silu(pre_a)
        hid_b = jax.nn.silu(pre_b)
        out_a = low(units[0][None, :] * hid_a + units[1][None, :] * hid_b)
        out_b = low(units[2][None, :] * hid_a + units[3][None, :] * hid_b)
        return (out_a, out_b)
    outputs, vjp_fn = jax.vjp(forward, image_a.astype(jnp.float32), image_b.astype(jnp.float32), weight_a.astype(jnp.float32), weight_b.astype(jnp.float32), tower_bias, stitch)
    grads = vjp_fn((cotan_a.astype(jnp.float32), cotan_b.astype(jnp.float32)))
    return (outputs[0].astype(jnp.bfloat16), outputs[1].astype(jnp.bfloat16), grads[0].T.astype(jnp.bfloat16), grads[1].T.astype(jnp.bfloat16), grads[2], grads[3], grads[4], grads[5])
```

```python
import functools

import jax
import jax.numpy as jnp
from jax import lax
from jax.experimental import pallas as pl
from jax.experimental.pallas import tpu as pltpu
from jax.sharding import PartitionSpec as P

CH = 256
POS = 36


def keep_block(image_group, position_mask, first_col, cols):
    positions = (first_col + lax.iota(jnp.int32, cols)) // CH
    onehot = (positions[:, None] == lax.iota(jnp.int32, POS)[None, :]).astype(jnp.float32)
    per_position = jnp.dot(onehot, position_mask.astype(jnp.float32).T)
    return jnp.where(
        image_group[:, None] == 1, per_position[:, 1][None, :], per_position[:, 0][None, :]
    )


def general_shards(
    image_a,
    image_b,
    image_group,
    position_mask,
    weight_a,
    weight_b,
    tower_bias,
    stitch,
    cotan_a,
    cotan_b,
):
    batch_rows = image_a.shape[0]
    shard_cols = image_a.shape[1]
    first_col = lax.axis_index("mp") * shard_cols
    keep_mask = keep_block(image_group, position_mask, first_col, shard_cols)
    keep_low = keep_mask.astype(jnp.bfloat16)
    contract_rows = (((0,), (0,)), ((), ()))
    contract_units = (((1,), (1,)), ((), ()))
    full_a = lax.all_gather(image_a * keep_low, "mp", axis=1, tiled=True)
    full_b = lax.all_gather(image_b * keep_low, "mp", axis=1, tiled=True)
    pre_a = jnp.dot(full_a, weight_a, preferred_element_type=jnp.float32) + tower_bias[0][None, :]
    pre_b = jnp.dot(full_b, weight_b, preferred_element_type=jnp.float32) + tower_bias[1][None, :]
    sigma_a = jax.nn.sigmoid(pre_a)
    sigma_b = jax.nn.sigmoid(pre_b)
    hidden_a = pre_a * sigma_a
    hidden_b = pre_b * sigma_b
    local_a = (stitch[0][None, :] * hidden_a + stitch[1][None, :] * hidden_b).astype(jnp.bfloat16)
    local_b = (stitch[2][None, :] * hidden_a + stitch[3][None, :] * hidden_b).astype(jnp.bfloat16)
    stitched_a = lax.all_gather(local_a, "mp", axis=1, tiled=True)
    stitched_b = lax.all_gather(local_b, "mp", axis=1, tiled=True)
    upper_a = cotan_a.astype(jnp.float32)
    upper_b = cotan_b.astype(jnp.float32)
    dhid_a = stitch[0][None, :] * upper_a + stitch[2][None, :] * upper_b
    dhid_b = stitch[1][None, :] * upper_a + stitch[3][None, :] * upper_b
    dpre_a = dhid_a * (sigma_a * (1.0 + pre_a * (1.0 - sigma_a)))
    dpre_b = dhid_b * (sigma_b * (1.0 + pre_b * (1.0 - sigma_b)))
    bias_terms = jnp.stack([jnp.sum(dpre_a, axis=0), jnp.sum(dpre_b, axis=0)])
    stitch_terms = jnp.stack(
        [
            jnp.sum(upper_a * hidden_a, axis=0),
            jnp.sum(upper_a * hidden_b, axis=0),
            jnp.sum(upper_b * hidden_a, axis=0),
            jnp.sum(upper_b * hidden_b, axis=0),
        ]
    )
    grad_bias, grad_stitch = lax.psum((bias_terms, stitch_terms), "dp")
    dlow_a = dpre_a.astype(jnp.bfloat16)
    dlow_b = dpre_b.astype(jnp.bfloat16)
    block_a = lax.dot_general(full_a, dlow_a, contract_rows, preferred_element_type=jnp.float32)
    block_b = lax.dot_general(full_b, dlow_b, contract_rows, preferred_element_type=jnp.float32)
    grad_weight_a = lax.psum_scatter(block_a, "dp", scatter_dimension=0, tiled=True)
    grad_weight_b = lax.psum_scatter(block_b, "dp", scatter_dimension=0, tiled=True)
    part_a = lax.dot_general(weight_a, dlow_a, contract_units, preferred_element_type=jnp.float32)
    part_b = lax.dot_general(weight_b, dlow_b, contract_units, preferred_element_type=jnp.float32)
    summed = lax.psum_scatter(
        jnp.concatenate([part_a, part_b], axis=1), "mp", scatter_dimension=0, tiled=True
    )
    keep_cols = keep_mask.T
    grad_image_a = (summed[:, :batch_rows] * keep_cols).astype(jnp.bfloat16)
    grad_image_b = (summed[:, batch_rows:] * keep_cols).astype(jnp.bfloat16)
    return (
        stitched_a,
        stitched_b,
        grad_image_a,
        grad_image_b,
        grad_weight_a,
        grad_weight_b,
        grad_bias,
        grad_stitch,
    )


SWAP_CORE = [(d, d ^ 1) for d in range(8)]
FLIP_X = [(d, d ^ 1) for d in range(4)]
FLIP_Y = [(d, d ^ 2) for d in range(4)]
FLIP_XY = [(d, d ^ 3) for d in range(4)]
ENDS_IN = [(0, 2), (1, 3), (6, 4), (7, 5)]
MIDS = [(2, 4), (3, 5), (4, 2), (5, 3)]
ENDS_OUT = [(2, 0), (3, 1), (4, 6), (5, 7)]
SLOTS = ((3, 2, 1, 0), (3, 2, 0, 1), (0, 1, 3, 2), (0, 1, 2, 3))


def part_kernel(where, w_ref, wo_ref, dz_ref, dzo_ref, out_ref):
    total = lax.dot_general(
        w_ref[...], dz_ref[...], (((1,), (1,)), ((), ())), preferred_element_type=jnp.float32
    )
    total += lax.dot_general(
        wo_ref[...], dzo_ref[...], (((1,), (1,)), ((), ())), preferred_element_type=jnp.float32
    )
    out_ref[...] = total.astype(jnp.bfloat16)


def part_block(block, core, weight, weight_other, dz, dz_other, cols):
    rows, units = dz.shape
    tile = cols // 3
    steps = cols // tile
    where = jnp.stack([2 * block + core, block]).astype(jnp.int32)
    return pl.pallas_call(
        part_kernel,
        out_shape=jax.ShapeDtypeStruct((cols, rows), jnp.bfloat16),
        grid_spec=pltpu.PrefetchScalarGridSpec(
            num_scalar_prefetch=1,
            grid=(steps,),
            in_specs=[
                pl.BlockSpec((tile, units), lambda t, where: (where[0] * steps + t, 0)),
                pl.BlockSpec((tile, units), lambda t, where: (where[1] * steps + t, 0)),
                pl.BlockSpec((rows, units), lambda t, where: (0, 0)),
                pl.BlockSpec((rows, units), lambda t, where: (0, 0)),
            ],
            out_specs=pl.BlockSpec((tile, rows), lambda t, where: (t, 0)),
        ),
        cost_estimate=pl.CostEstimate(
            flops=4 * cols * rows * units, bytes_accessed=2 * cols * (2 * units + rows), transcendentals=0
        ),
        name="part_block",
    )(where, weight, weight_other, dz, dz_other)


def weight_kernel(where, own, px, py, pd, qx, qy, qd, dz0, dzx, dzy, dzd, out_ref):
    def dots(pieces):
        total = None
        for image, dz in zip(pieces, (dz0, dzx, dzy, dzd)):
            term = lax.dot_general(
                image[...], dz[...], (((0,), (0,)), ((), ())), preferred_element_type=jnp.float32
            )
            total = term if total is None else total + term
        out_ref[...] = total

    same = pl.program_id(0) == where[1]

    @pl.when(same)
    def _():
        dots((own, px, py, pd))

    @pl.when(jnp.logical_not(same))
    def _():
        dots((own, qx, qy, qd))


def weight_grad(quarter, core, full, near, far, dzs):
    rows, units = dzs[0].shape
    cols = near[0].shape[1]
    tile = cols // 3
    steps = cols // tile
    where = jnp.stack([quarter, core]).astype(jnp.int32)
    own = pl.BlockSpec((rows, tile), lambda p, t, where: (0, (2 * where[0] + p) * steps + t))
    mine = pl.BlockSpec((rows, tile), lambda p, t, where: (0, jnp.where(p == where[1], t, 0)))
    other = pl.BlockSpec((rows, tile), lambda p, t, where: (0, jnp.where(p == where[1], 0, t)))
    whole = pl.BlockSpec((rows, units), lambda p, t, where: (0, 0))
    return pl.pallas_call(
        weight_kernel,
        out_shape=jax.ShapeDtypeStruct((2 * cols, units), jnp.float32),
        grid_spec=pltpu.PrefetchScalarGridSpec(
            num_scalar_prefetch=1,
            grid=(2, steps),
            in_specs=[own] + [mine] * 3 + [other] * 3 + [whole] * 4,
            out_specs=pl.BlockSpec((tile, units), lambda p, t, where: (p * steps + t, 0)),
        ),
        cost_estimate=pl.CostEstimate(
            flops=16 * cols * rows * units,
            bytes_accessed=16 * cols * rows + 8 * cols * units,
            transcendentals=0,
        ),
        name="weight_grad",
    )(where, full, *near, *far, *dzs)


def fast_shards(
    image_a,
    image_b,
    image_group,
    position_mask,
    weight_a,
    weight_b,
    tower_bias,
    stitch,
    cotan_a,
    cotan_b,
):
    rows, cols = image_a.shape
    units = weight_a.shape[1]
    place = lax.axis_index("mp")
    z = place // 2
    core = place % 2
    quarter = lax.axis_index("dp")
    keep_mask = keep_block(image_group, position_mask, place * cols, cols)
    keep_low = keep_mask.astype(jnp.bfloat16)
    masked_a = image_a * keep_low
    masked_b = image_b * keep_low
    full_a = lax.all_gather(masked_a, "mp", axis=1, tiled=True)
    full_b = lax.all_gather(masked_b, "mp", axis=1, tiled=True)
    slots = jnp.take(jnp.asarray(SLOTS, jnp.int32), z, axis=0)

    def other_weight(weight):
        blocks = weight.reshape(4, 2, cols, units)
        send = lax.dynamic_index_in_dim(blocks, 1 - core, axis=1, keepdims=False)
        return lax.ppermute(send.reshape(4 * cols, units), "mp", SWAP_CORE)

    upper_a = cotan_a.astype(jnp.float32)
    upper_b = cotan_b.astype(jnp.float32)

    def tower(full, weight, bias, unit_a, unit_b):
        pre = jnp.dot(full, weight, preferred_element_type=jnp.float32) + bias[None, :]
        sigma = jax.nn.sigmoid(pre)
        hidden = pre * sigma
        dhid = unit_a[None, :] * upper_a + unit_b[None, :] * upper_b
        dpre = dhid * (sigma * (1.0 + pre * (1.0 - sigma)))
        sums = jnp.stack(
            [
                jnp.sum(dpre, axis=0),
                jnp.sum(upper_a * hidden, axis=0),
                jnp.sum(upper_b * hidden, axis=0),
            ]
        )
        return hidden, dpre.astype(jnp.bfloat16), sums

    def image_grad(weight, weight_other, dz):
        dz_other = lax.ppermute(dz, "mp", SWAP_CORE)
        first, second, third, kept = [
            part_block(slots[k], core, weight, weight_other, dz, dz_other, cols) for k in range(4)
        ]

        def add(*terms):
            total = terms[0].astype(jnp.float32)
            for term in terms[1:]:
                total = total + term.astype(jnp.float32)
            return total

        got_first = lax.ppermute(first, "mp", ENDS_IN)
        got_second = lax.ppermute(second, "mp", ENDS_IN)
        got_third = lax.ppermute(third, "mp", ENDS_IN)
        cross_first = lax.ppermute(add(first, got_first).astype(jnp.bfloat16), "mp", MIDS)
        cross_second = lax.ppermute(add(second, got_second).astype(jnp.bfloat16), "mp", MIDS)
        last = lax.ppermute(add(third, cross_first).astype(jnp.bfloat16), "mp", ENDS_OUT)
        total = add(kept, last, got_third, cross_second)
        return (total * keep_mask.T).astype(jnp.bfloat16)

    def spread(full):
        near = []
        far = []
        for step, flip in ((1, FLIP_X), (2, FLIP_Y), (3, FLIP_XY)):
            block = 2 * (quarter ^ step) + core
            send = lax.dynamic_slice_in_dim(full, block * cols, cols, axis=1)
            got = lax.ppermute(send, "dp", flip)
            near.append(got)
            far.append(lax.ppermute(got, "mp", SWAP_CORE))
        return near, far

    def around(x):
        return [x] + [lax.ppermute(x, "dp", flip) for flip in (FLIP_X, FLIP_Y, FLIP_XY)]

    other_a = other_weight(weight_a)
    other_b = other_weight(weight_b)
    hidden_a, dz_a, sums_a = tower(full_a, weight_a, tower_bias[0], stitch[0], stitch[2])
    grad_image_a = image_grad(weight_a, other_a, dz_a)
    near_a, far_a = spread(full_a)
    grad_weight_a = weight_grad(quarter, core, full_a, near_a, far_a, around(dz_a))

    hidden_b, dz_b, sums_b = tower(full_b, weight_b, tower_bias[1], stitch[1], stitch[3])
    local_a = (stitch[0][None, :] * hidden_a + stitch[1][None, :] * hidden_b).astype(jnp.bfloat16)
    local_b = (stitch[2][None, :] * hidden_a + stitch[3][None, :] * hidden_b).astype(jnp.bfloat16)
    stitched = lax.all_gather(jnp.concatenate([local_a, local_b]), "mp", axis=1, tiled=True)
    grad_image_b = image_grad(weight_b, other_b, dz_b)
    near_b, far_b = spread(full_b)
    grad_weight_b = weight_grad(quarter, core, full_b, near_b, far_b, around(dz_b))

    own, by_x, by_y, by_xy = around(jnp.concatenate([sums_a, sums_b]))
    sums = (own + by_x) + (by_y + by_xy)
    grad_bias = jnp.stack([sums[0], sums[3]])
    grad_stitch = jnp.stack([sums[1], sums[4], sums[2], sums[5]])
    return (
        stitched[:rows],
        stitched[rows:],
        grad_image_a,
        grad_image_b,
        grad_weight_a,
        grad_weight_b,
        grad_bias,
        grad_stitch,
    )


def solution(mesh):
    placed = (
        P("dp", "mp"),
        P("dp", "mp"),
        P("dp"),
        P(),
        P(None, "mp"),
        P(None, "mp"),
        P(None, "mp"),
        P(None, "mp"),
        P("dp", "mp"),
        P("dp", "mp"),
    )
    fits = mesh.shape["dp"] == 4 and mesh.shape["mp"] == 8
    return jax.shard_map(
        fast_shards if fits else general_shards,
        mesh=mesh,
        in_specs=placed,
        out_specs=(
            P("dp", None),
            P("dp", None),
            P("mp", "dp"),
            P("mp", "dp"),
            P("dp", "mp"),
            P("dp", "mp"),
            P(None, "mp"),
            P(None, "mp"),
        ),
        check_vma=False,
    )
```

```python
import functools

import jax
import jax.numpy as jnp
from jax import lax
from jax.experimental import pallas as pl
from jax.experimental.pallas import tpu as pltpu
from jax.sharding import PartitionSpec as P

CH = 256
POS = 36


def keep_block(image_group, position_mask, first_col, cols):
    positions = (first_col + lax.iota(jnp.int32, cols)) // CH
    onehot = (positions[:, None] == lax.iota(jnp.int32, POS)[None, :]).astype(jnp.float32)
    per_position = jnp.dot(onehot, position_mask.astype(jnp.float32).T)
    return jnp.where(
        image_group[:, None] == 1, per_position[:, 1][None, :], per_position[:, 0][None, :]
    )


def general_shards(
    image_a,
    image_b,
    image_group,
    position_mask,
    weight_a,
    weight_b,
    tower_bias,
    stitch,
    cotan_a,
    cotan_b,
):
    batch_rows = image_a.shape[0]
    shard_cols = image_a.shape[1]
    first_col = lax.axis_index("mp") * shard_cols
    keep_mask = keep_block(image_group, position_mask, first_col, shard_cols)
    keep_low = keep_mask.astype(jnp.bfloat16)
    contract_rows = (((0,), (0,)), ((), ()))
    contract_units = (((1,), (1,)), ((), ()))
    full_a = lax.all_gather(image_a * keep_low, "mp", axis=1, tiled=True)
    full_b = lax.all_gather(image_b * keep_low, "mp", axis=1, tiled=True)
    pre_a = jnp.dot(full_a, weight_a, preferred_element_type=jnp.float32) + tower_bias[0][None, :]
    pre_b = jnp.dot(full_b, weight_b, preferred_element_type=jnp.float32) + tower_bias[1][None, :]
    sigma_a = jax.nn.sigmoid(pre_a)
    sigma_b = jax.nn.sigmoid(pre_b)
    hidden_a = pre_a * sigma_a
    hidden_b = pre_b * sigma_b
    local_a = (stitch[0][None, :] * hidden_a + stitch[1][None, :] * hidden_b).astype(jnp.bfloat16)
    local_b = (stitch[2][None, :] * hidden_a + stitch[3][None, :] * hidden_b).astype(jnp.bfloat16)
    stitched_a = lax.all_gather(local_a, "mp", axis=1, tiled=True)
    stitched_b = lax.all_gather(local_b, "mp", axis=1, tiled=True)
    upper_a = cotan_a.astype(jnp.float32)
    upper_b = cotan_b.astype(jnp.float32)
    dhid_a = stitch[0][None, :] * upper_a + stitch[2][None, :] * upper_b
    dhid_b = stitch[1][None, :] * upper_a + stitch[3][None, :] * upper_b
    dpre_a = dhid_a * (sigma_a * (1.0 + pre_a * (1.0 - sigma_a)))
    dpre_b = dhid_b * (sigma_b * (1.0 + pre_b * (1.0 - sigma_b)))
    bias_terms = jnp.stack([jnp.sum(dpre_a, axis=0), jnp.sum(dpre_b, axis=0)])
    stitch_terms = jnp.stack(
        [
            jnp.sum(upper_a * hidden_a, axis=0),
            jnp.sum(upper_a * hidden_b, axis=0),
            jnp.sum(upper_b * hidden_a, axis=0),
            jnp.sum(upper_b * hidden_b, axis=0),
        ]
    )
    grad_bias, grad_stitch = lax.psum((bias_terms, stitch_terms), "dp")
    dlow_a = dpre_a.astype(jnp.bfloat16)
    dlow_b = dpre_b.astype(jnp.bfloat16)
    block_a = lax.dot_general(full_a, dlow_a, contract_rows, preferred_element_type=jnp.float32)
    block_b = lax.dot_general(full_b, dlow_b, contract_rows, preferred_element_type=jnp.float32)
    grad_weight_a = lax.psum_scatter(block_a, "dp", scatter_dimension=0, tiled=True)
    grad_weight_b = lax.psum_scatter(block_b, "dp", scatter_dimension=0, tiled=True)
    part_a = lax.dot_general(weight_a, dlow_a, contract_units, preferred_element_type=jnp.float32)
    part_b = lax.dot_general(weight_b, dlow_b, contract_units, preferred_element_type=jnp.float32)
    summed = lax.psum_scatter(
        jnp.concatenate([part_a, part_b], axis=1), "mp", scatter_dimension=0, tiled=True
    )
    keep_cols = keep_mask.T
    grad_image_a = (summed[:, :batch_rows] * keep_cols).astype(jnp.bfloat16)
    grad_image_b = (summed[:, batch_rows:] * keep_cols).astype(jnp.bfloat16)
    return (
        stitched_a,
        stitched_b,
        grad_image_a,
        grad_image_b,
        grad_weight_a,
        grad_weight_b,
        grad_bias,
        grad_stitch,
    )


SWAP_CORE = [(d, d ^ 1) for d in range(8)]
FLIPS = [[(d, d ^ k) for d in range(4)] for k in range(4)]
NEAR_Z = [(d, d ^ 2) for d in range(8)]
FAR_Z = [(d, d ^ 4) for d in range(8)]
ENDS_IN = [(0, 2), (1, 3), (6, 4), (7, 5)]
MIDS = [(2, 4), (3, 5), (4, 2), (5, 3)]
ENDS_OUT = [(2, 0), (3, 1), (4, 6), (5, 7)]
SLOTS = ((3, 2, 1, 0), (3, 2, 0, 1), (0, 1, 3, 2), (0, 1, 2, 3))
LANES = 128
VMEM_LIMIT = 40 * 1024 * 1024


def after(x, *deps):
    return lax.optimization_barrier((x,) + deps)[0]


def params(**kwargs):
    return pltpu.CompilerParams(vmem_limit_bytes=VMEM_LIMIT, **kwargs)


def low(x):
    return x.astype(jnp.bfloat16)


def wide(x):
    return x.astype(jnp.float32)


def mask_kernel(place, marks, group, image, out):
    second = group[...] == 1
    cols = image.shape[1]
    for chunk in range(cols // LANES):
        position = (place[0] * cols + chunk * LANES) // CH
        keep = wide(jnp.where(second, marks[1, position], marks[0, position]))
        lanes = slice(chunk * LANES, (chunk + 1) * LANES)
        out[:, lanes] = low(wide(image[:, lanes]) * keep)


def mask_image(place, marks, group, image):
    return pl.pallas_call(
        mask_kernel,
        out_shape=jax.ShapeDtypeStruct(image.shape, jnp.bfloat16),
        in_specs=[
            pl.BlockSpec(memory_space=pltpu.SMEM),
            pl.BlockSpec(memory_space=pltpu.SMEM),
            pl.BlockSpec(memory_space=pltpu.VMEM),
            pl.BlockSpec(memory_space=pltpu.VMEM),
        ],
        out_specs=pl.BlockSpec(memory_space=pltpu.VMEM),
        compiler_params=params(),
        cost_estimate=pl.CostEstimate(
            flops=image.size, bytes_accessed=4 * image.size, transcendentals=0
        ),
        name="mask_image",
    )(place, marks, group, image)


def forward_kernel(where, p0, p1, p2, p3, p4, mine, other, out, sent, keep_acc, send_acc):
    k = pl.program_id(0)
    t = pl.program_id(1)

    @pl.when((k == 0) & (t == 0))
    def _():
        keep_acc[...] = jnp.zeros_like(keep_acc)
        send_acc[...] = jnp.zeros_like(send_acc)

    def step(piece):
        keep_acc[...] += jnp.dot(piece[...], mine[...], preferred_element_type=jnp.float32)
        send_acc[...] += jnp.dot(piece[...], other[...], preferred_element_type=jnp.float32)

    for index, piece in enumerate((p0, p1, p2)):
        pl.when(k == index)(functools.partial(step, piece))
    pl.when((k == 3) & (where[2] == 0))(functools.partial(step, p3))
    pl.when((k == 3) & (where[2] == 1))(functools.partial(step, p4))

    @pl.when((k == pl.num_programs(0) - 1) & (t == pl.num_programs(1) - 1))
    def _():
        out[...] = keep_acc[...]
        sent[...] = send_acc[...]


def forward(where, pieces, weight, weight_other):
    rows, cols = pieces[0].shape
    units = weight.shape[1]
    tile = cols // 3
    steps = cols // tile

    def piece_spec(index):
        return pl.BlockSpec(
            (rows, tile),
            lambda k, t, where: (0, jnp.where(k < index, 0, jnp.where(k > index, steps - 1, t))),
        )

    rows_of = pl.BlockSpec(
        (tile, units), lambda k, t, where: ((2 * (where[0] ^ k) + where[1]) * steps + t, 0)
    )
    whole = pl.BlockSpec((rows, units), lambda k, t, where: (0, 0))
    return pl.pallas_call(
        forward_kernel,
        out_shape=[jax.ShapeDtypeStruct((rows, units), jnp.float32)] * 2,
        grid_spec=pltpu.PrefetchScalarGridSpec(
            num_scalar_prefetch=1,
            grid=(4, steps),
            in_specs=[piece_spec(min(k, 3)) for k in range(5)] + [rows_of, rows_of],
            out_specs=[whole, whole],
            scratch_shapes=[pltpu.VMEM((rows, units), jnp.float32)] * 2,
        ),
        compiler_params=params(),
        cost_estimate=pl.CostEstimate(
            flops=16 * rows * cols * units,
            bytes_accessed=8 * cols * (rows + 2 * units) + 8 * rows * units,
            transcendentals=0,
        ),
        name="forward",
    )(where, *pieces, weight, weight_other)


def tower_math(own, got, bias, unit_a, unit_b, upper_a, upper_b, dz, sums):
    pre = own[...] + got[...] + bias[...]
    sigma = jax.nn.sigmoid(pre)
    hidden = pre * sigma
    cot_a = wide(upper_a[...])
    cot_b = wide(upper_b[...])
    dhid = unit_a[...] * cot_a + unit_b[...] * cot_b
    dpre = dhid * (sigma * (1.0 + pre * (1.0 - sigma)))
    dz[...] = low(dpre)
    sums[0:1, :] = jnp.sum(dpre, axis=0, keepdims=True)
    sums[1:2, :] = jnp.sum(cot_a * hidden, axis=0, keepdims=True)
    sums[2:3, :] = jnp.sum(cot_b * hidden, axis=0, keepdims=True)
    sums[3:4, :] = jnp.zeros_like(sums[3:4, :])
    return hidden


def first_kernel(own, got, bias, unit_a, unit_b, upper_a, upper_b, dz, sums, hidden):
    hidden[...] = tower_math(own, got, bias, unit_a, unit_b, upper_a, upper_b, dz, sums)


def second_kernel(
    own, got, bias, unit_a, unit_b, upper_a, upper_b, earlier, stitch, dz, sums, local
):
    hidden = tower_math(own, got, bias, unit_a, unit_b, upper_a, upper_b, dz, sums)
    rows = hidden.shape[0]
    before = earlier[...]
    local[0:rows, :] = low(stitch[0:1, :] * before + stitch[1:2, :] * hidden)
    local[rows : 2 * rows, :] = low(stitch[2:3, :] * before + stitch[3:4, :] * hidden)


def tower(kernel, name, last, *operands):
    rows, units = operands[0].shape
    return pl.pallas_call(
        kernel,
        out_shape=[
            jax.ShapeDtypeStruct((rows, units), jnp.bfloat16),
            jax.ShapeDtypeStruct((4, units), jnp.float32),
            last,
        ],
        in_specs=[pl.BlockSpec(memory_space=pltpu.VMEM)] * len(operands),
        out_specs=[pl.BlockSpec(memory_space=pltpu.VMEM)] * 3,
        compiler_params=params(),
        cost_estimate=pl.CostEstimate(
            flops=30 * rows * units, bytes_accessed=20 * rows * units, transcendentals=rows * units
        ),
        name=name,
    )(*operands)


def part_kernel(where, mine, other, dz, dzo, first, second, third, kept, dz_t, dzo_t):
    k = pl.program_id(0)

    @pl.when((k == 0) & (pl.program_id(1) == 0))
    def _():
        dz_t[...] = dz[...].T
        dzo_t[...] = dzo[...].T

    total = jnp.dot(mine[...], dz_t[...], preferred_element_type=jnp.float32)
    total += jnp.dot(other[...], dzo_t[...], preferred_element_type=jnp.float32)

    def put(ref):
        ref[...] = total.astype(ref.dtype)

    for index, ref in enumerate((first, second, third, kept)):
        pl.when(k == index)(functools.partial(put, ref))


def parts(where, weight, weight_other, dz, dz_other, cols):
    rows, units = dz.shape
    tile = cols // 3
    steps = cols // tile

    def out_spec(index):
        return pl.BlockSpec(
            (tile, rows),
            lambda k, t, where: (jnp.where(k < index, 0, jnp.where(k > index, steps - 1, t)), 0),
        )

    rows_of = pl.BlockSpec(
        (tile, units), lambda k, t, where: ((2 * where[3 + k] + where[1]) * steps + t, 0)
    )
    whole = pl.BlockSpec((rows, units), lambda k, t, where: (0, 0))
    return pl.pallas_call(
        part_kernel,
        out_shape=[jax.ShapeDtypeStruct((cols, rows), jnp.bfloat16)] * 3
        + [jax.ShapeDtypeStruct((cols, rows), jnp.float32)],
        grid_spec=pltpu.PrefetchScalarGridSpec(
            num_scalar_prefetch=1,
            grid=(4, steps),
            in_specs=[rows_of, rows_of, whole, whole],
            out_specs=[out_spec(k) for k in range(4)],
            scratch_shapes=[pltpu.VMEM((units, rows), jnp.bfloat16)] * 2,
        ),
        compiler_params=params(),
        cost_estimate=pl.CostEstimate(
            flops=16 * cols * rows * units,
            bytes_accessed=16 * cols * units + 10 * cols * rows,
            transcendentals=0,
        ),
        name="parts",
    )(where, weight, weight_other, dz, dz_other)


def finish_kernel(place, marks, group, kept, third, cross, last, out):
    second = group[...] == 1
    cols = out.shape[0]
    for chunk in range(cols // LANES):
        position = (place[0] * cols + chunk * LANES) // CH
        keep = wide(jnp.where(second, marks[1, position], marks[0, position]))
        rows = slice(chunk * LANES, (chunk + 1) * LANES)
        total = kept[rows, :] + wide(third[rows, :]) + wide(cross[rows, :]) + wide(last[rows, :])
        out[rows, :] = low(total * keep)


def finish(place, marks, group, kept, third, cross, last):
    return pl.pallas_call(
        finish_kernel,
        out_shape=jax.ShapeDtypeStruct(kept.shape, jnp.bfloat16),
        in_specs=[
            pl.BlockSpec(memory_space=pltpu.SMEM),
            pl.BlockSpec(memory_space=pltpu.SMEM),
        ]
        + [pl.BlockSpec(memory_space=pltpu.VMEM)] * 5,
        out_specs=pl.BlockSpec(memory_space=pltpu.VMEM),
        compiler_params=params(),
        cost_estimate=pl.CostEstimate(
            flops=4 * kept.size, bytes_accessed=12 * kept.size, transcendentals=0
        ),
        name="finish",
    )(place, marks, group, kept, third, cross, last)


def pick_kernel(where, p0, p1, p2, p3, p4, o0, o1, o2, o3, sems):
    outs = (o0, o1, o2, o3)
    for s, out in enumerate(outs):
        k = where[0] ^ where[7] ^ s
        for index, piece in enumerate((p0, p1, p2)):
            pl.when(k == index)(pltpu.make_async_copy(piece, out, sems.at[s]).start)
        pl.when((k == 3) & (where[2] == 0))(pltpu.make_async_copy(p3, out, sems.at[s]).start)
        pl.when((k == 3) & (where[2] == 1))(pltpu.make_async_copy(p4, out, sems.at[s]).start)
    for s, out in enumerate(outs):
        pltpu.make_async_copy(p0, out, sems.at[s]).wait()


def pick(where, pieces):
    return pl.pallas_call(
        pick_kernel,
        out_shape=[jax.ShapeDtypeStruct(pieces[0].shape, pieces[0].dtype)] * 4,
        in_specs=[pl.BlockSpec(memory_space=pltpu.SMEM)] + [pl.BlockSpec(memory_space=pl.ANY)] * 5,
        out_specs=[pl.BlockSpec(memory_space=pl.ANY)] * 4,
        scratch_shapes=[pltpu.SemaphoreType.DMA((4,))],
        compiler_params=params(),
        cost_estimate=pl.CostEstimate(
            flops=0, bytes_accessed=16 * pieces[0].size, transcendentals=0
        ),
        name="pick",
    )(where, *pieces)


def lay_kernel(where, *refs):
    sources = refs[:12]
    out_a, out_b, sems = refs[12:]
    rows = out_a.shape[0]
    units = sources[0].shape[1]
    for side in range(2):
        for k in range(4):
            block = 2 * (where[0] ^ k) + (where[1] ^ side)
            lanes = pl.ds(pl.multiple_of(block * units, units), units)
            for half, out in enumerate((out_a, out_b)):
                sem = sems.at[side * 8 + k * 2 + half]
                part = pl.ds(half * rows, rows)

                def go(source):
                    pltpu.make_async_copy(source.at[part, :], out.at[:, lanes], sem).start()

                if k < 2:
                    go(sources[side * 6 + k])
                else:
                    at = side * 6 + 2 * k - 2
                    pl.when(where[2] == 0)(functools.partial(go, sources[at]))
                    pl.when(where[2] == 1)(functools.partial(go, sources[at + 1]))
    for side in range(2):
        for k in range(4):
            for half, out in enumerate((out_a, out_b)):
                pltpu.make_async_copy(
                    sources[0].at[pl.ds(0, rows), :],
                    out.at[:, pl.ds(0, units)],
                    sems.at[side * 8 + k * 2 + half],
                ).wait()


def lay_out(where, near, far, rows):
    units = near[0].shape[1]
    return pl.pallas_call(
        lay_kernel,
        out_shape=[jax.ShapeDtypeStruct((rows, 8 * units), jnp.bfloat16)] * 2,
        in_specs=[pl.BlockSpec(memory_space=pltpu.SMEM)]
        + [pl.BlockSpec(memory_space=pl.ANY)] * 12,
        out_specs=[pl.BlockSpec(memory_space=pl.ANY)] * 2,
        scratch_shapes=[pltpu.SemaphoreType.DMA((16,))],
        compiler_params=params(),
        cost_estimate=pl.CostEstimate(
            flops=0, bytes_accessed=64 * rows * units, transcendentals=0
        ),
        name="lay_out",
    )(where, *near, *far)


def weight_kernel(where, *refs):
    near, far, dzs, out = refs[0:4], refs[4:8], refs[8:12], refs[12]

    def dots(pieces):
        total = None
        for image, dz in zip(pieces, dzs):
            term = lax.dot_general(
                image[...], dz[...], (((0,), (0,)), ((), ())), preferred_element_type=jnp.float32
            )
            total = term if total is None else total + term
        out[...] = total

    same = pl.program_id(0) == where[1]
    pl.when(same)(functools.partial(dots, near))
    pl.when(jnp.logical_not(same))(functools.partial(dots, far))


def weight_grad(where, near, far, dzs):
    rows, units = dzs[0].shape
    cols = near[0].shape[1]
    tile = cols // 3
    steps = cols // tile
    mine = pl.BlockSpec((rows, tile), lambda p, t, where: (0, jnp.where(p == where[1], t, 0)))
    other = pl.BlockSpec((rows, tile), lambda p, t, where: (0, jnp.where(p == where[1], 0, t)))
    whole = pl.BlockSpec((rows, units), lambda p, t, where: (0, 0))
    return pl.pallas_call(
        weight_kernel,
        out_shape=jax.ShapeDtypeStruct((2 * cols, units), jnp.float32),
        grid_spec=pltpu.PrefetchScalarGridSpec(
            num_scalar_prefetch=1,
            grid=(2, steps),
            in_specs=[mine] * 4 + [other] * 4 + [whole] * 4,
            out_specs=pl.BlockSpec((tile, units), lambda p, t, where: (p * steps + t, 0)),
        ),
        compiler_params=params(),
        cost_estimate=pl.CostEstimate(
            flops=16 * cols * rows * units,
            bytes_accessed=16 * cols * rows + 8 * cols * units,
            transcendentals=0,
        ),
        name="weight_grad",
    )(where, *near, *far, *dzs)


def swap(x):
    return lax.ppermute(x, "mp", SWAP_CORE)


def fast_shards(
    image_a,
    image_b,
    image_group,
    position_mask,
    weight_a,
    weight_b,
    tower_bias,
    stitch,
    cotan_a,
    cotan_b,
):
    rows, cols = image_a.shape
    units = weight_a.shape[1]
    place = lax.axis_index("mp").astype(jnp.int32)
    z = place // 2
    core = place % 2
    quarter = lax.axis_index("dp").astype(jnp.int32)
    middle = ((z == 1) | (z == 2)).astype(jnp.int32)
    slots = jnp.take(jnp.asarray(SLOTS, jnp.int32), z, axis=0)
    where = jnp.concatenate(
        [jnp.stack([z, core, middle]), slots, jnp.stack([quarter])]
    ).astype(jnp.int32)
    spot = place[None]
    group_col = image_group[:, None]
    group_row = image_group[None, :]

    def along(x):
        return lax.ppermute(x, "mp", NEAR_Z)

    a0 = mask_image(spot, position_mask, group_col, image_a)
    a1 = along(a0)
    a2 = lax.ppermute(a0, "mp", FAR_Z)
    b0 = mask_image(spot, position_mask, group_col, after(image_b, a0))
    b2 = lax.ppermute(b0, "mp", FAR_Z)
    other_a = swap(after(weight_a, b0))
    other_b = swap(after(weight_b, other_a))
    a3 = along(a2)
    b0_late = after(b0, a2)
    b1 = along(b0_late)
    b_mid = lax.ppermute(b0_late, "mp", MIDS)
    b_end = lax.ppermute(b2, "mp", ENDS_OUT)
    pieces_a = [a0, a1, a2, a3, a3]
    pieces_b = [b0, b1, b2, b_end, b_mid]

    def around(x):
        return [x] + [lax.ppermute(x, "dp", FLIPS[k]) for k in (1, 2, 3)]

    def spread(pieces):
        own, *send = pick(where, pieces)
        near = [own] + [lax.ppermute(x, "dp", FLIPS[k + 1]) for k, x in enumerate(send)]
        return near, [swap(x) for x in near]

    def add(*terms):
        total = wide(terms[0])
        for term in terms[1:]:
            total = total + wide(term)
        return low(total)

    def image_grad(weight, weight_other, dz):
        dz_other = swap(dz)
        first, second, third, kept = parts(where, weight, weight_other, dz, dz_other, cols)
        got_first = lax.ppermute(first, "mp", ENDS_IN)
        got_second = lax.ppermute(second, "mp", ENDS_IN)
        got_third = lax.ppermute(third, "mp", ENDS_IN)
        cross_first = lax.ppermute(add(first, got_first), "mp", MIDS)
        cross_second = lax.ppermute(add(second, got_second), "mp", MIDS)
        last = lax.ppermute(add(third, cross_first), "mp", ENDS_OUT)
        result = finish(spot, position_mask, group_row, kept, got_third, cross_second, last)
        return result, first

    own_a, sent_a = forward(where, pieces_a, weight_a, other_a)
    dz_a, sums_a, hidden_a = tower(
        first_kernel,
        "tower_a",
        jax.ShapeDtypeStruct((rows, units), jnp.float32),
        own_a,
        swap(sent_a),
        tower_bias[0:1],
        stitch[0:1],
        stitch[2:3],
        cotan_a,
        cotan_b,
    )
    grad_image_a, part_a = image_grad(weight_a, other_a, dz_a)
    near_a, far_a = spread([after(pieces_a[0], part_a)] + pieces_a[1:])
    dzs_a = around(after(dz_a, part_a))

    own_b, sent_b = forward(where, [after(pieces_b[0], part_a)] + pieces_b[1:], weight_b, other_b)
    dz_b, sums_b, local = tower(
        second_kernel,
        "tower_b",
        jax.ShapeDtypeStruct((2 * rows, units), jnp.bfloat16),
        own_b,
        swap(sent_b),
        tower_bias[1:2],
        stitch[1:2],
        stitch[3:4],
        cotan_a,
        cotan_b,
        hidden_a,
        stitch,
    )
    s1 = along(local)
    s_mid = lax.ppermute(local, "mp", MIDS)
    grad_image_b, part_b = image_grad(weight_b, other_b, dz_b)
    s_out = lax.ppermute(s_mid, "mp", ENDS_OUT)
    s_far = lax.ppermute(s1, "mp", MIDS)
    s_last = lax.ppermute(s_far, "mp", ENDS_OUT)
    line = [local, s1, s_out, s_far, s_last, s_mid]
    line_far = [swap(x) for x in line]
    stitched_a, stitched_b = lay_out(where, line, line_far, rows)

    near_b, far_b = spread([after(pieces_b[0], part_b)] + pieces_b[1:])
    dzs_b = around(after(dz_b, part_b))
    grad_weight_a = weight_grad(where, near_a, far_a, dzs_a)
    grad_weight_b = weight_grad(where, near_b, far_b, dzs_b)

    own, by_x, by_y, by_xy = around(jnp.concatenate([sums_a, sums_b]))
    sums = (own + by_x) + (by_y + by_xy)
    grad_bias = jnp.stack([sums[0], sums[4]])
    grad_stitch = jnp.stack([sums[1], sums[5], sums[2], sums[6]])
    return (
        stitched_a,
        stitched_b,
        grad_image_a,
        grad_image_b,
        grad_weight_a,
        grad_weight_b,
        grad_bias,
        grad_stitch,
    )


def solution(mesh):
    placed = (
        P("dp", "mp"),
        P("dp", "mp"),
        P("dp"),
        P(),
        P(None, "mp"),
        P(None, "mp"),
        P(None, "mp"),
        P(None, "mp"),
        P("dp", "mp"),
        P("dp", "mp"),
    )
    fits = mesh.shape["dp"] == 4 and mesh.shape["mp"] == 8
    return jax.shard_map(
        fast_shards if fits else general_shards,
        mesh=mesh,
        in_specs=placed,
        out_specs=(
            P("dp", None),
            P("dp", None),
            P("mp", "dp"),
            P("mp", "dp"),
            P("dp", "mp"),
            P("dp", "mp"),
            P(None, "mp"),
            P(None, "mp"),
        ),
        check_vma=False,
    )
```

```python
import functools

import jax
import jax.numpy as jnp
from jax import lax
from jax.experimental import pallas as pl
from jax.experimental.pallas import tpu as pltpu
from jax.sharding import PartitionSpec as P

CH = 256
POS = 36


def keep_block(image_group, position_mask, first_col, cols):
    positions = (first_col + lax.iota(jnp.int32, cols)) // CH
    onehot = (positions[:, None] == lax.iota(jnp.int32, POS)[None, :]).astype(jnp.float32)
    per_position = jnp.dot(onehot, position_mask.astype(jnp.float32).T)
    return jnp.where(
        image_group[:, None] == 1, per_position[:, 1][None, :], per_position[:, 0][None, :]
    )


def general_shards(
    image_a,
    image_b,
    image_group,
    position_mask,
    weight_a,
    weight_b,
    tower_bias,
    stitch,
    cotan_a,
    cotan_b,
):
    batch_rows = image_a.shape[0]
    shard_cols = image_a.shape[1]
    first_col = lax.axis_index("mp") * shard_cols
    keep_mask = keep_block(image_group, position_mask, first_col, shard_cols)
    keep_low = keep_mask.astype(jnp.bfloat16)
    contract_rows = (((0,), (0,)), ((), ()))
    contract_units = (((1,), (1,)), ((), ()))
    full_a = lax.all_gather(image_a * keep_low, "mp", axis=1, tiled=True)
    full_b = lax.all_gather(image_b * keep_low, "mp", axis=1, tiled=True)
    pre_a = jnp.dot(full_a, weight_a, preferred_element_type=jnp.float32) + tower_bias[0][None, :]
    pre_b = jnp.dot(full_b, weight_b, preferred_element_type=jnp.float32) + tower_bias[1][None, :]
    sigma_a = jax.nn.sigmoid(pre_a)
    sigma_b = jax.nn.sigmoid(pre_b)
    hidden_a = pre_a * sigma_a
    hidden_b = pre_b * sigma_b
    local_a = (stitch[0][None, :] * hidden_a + stitch[1][None, :] * hidden_b).astype(jnp.bfloat16)
    local_b = (stitch[2][None, :] * hidden_a + stitch[3][None, :] * hidden_b).astype(jnp.bfloat16)
    stitched_a = lax.all_gather(local_a, "mp", axis=1, tiled=True)
    stitched_b = lax.all_gather(local_b, "mp", axis=1, tiled=True)
    upper_a = cotan_a.astype(jnp.float32)
    upper_b = cotan_b.astype(jnp.float32)
    dhid_a = stitch[0][None, :] * upper_a + stitch[2][None, :] * upper_b
    dhid_b = stitch[1][None, :] * upper_a + stitch[3][None, :] * upper_b
    dpre_a = dhid_a * (sigma_a * (1.0 + pre_a * (1.0 - sigma_a)))
    dpre_b = dhid_b * (sigma_b * (1.0 + pre_b * (1.0 - sigma_b)))
    bias_terms = jnp.stack([jnp.sum(dpre_a, axis=0), jnp.sum(dpre_b, axis=0)])
    stitch_terms = jnp.stack(
        [
            jnp.sum(upper_a * hidden_a, axis=0),
            jnp.sum(upper_a * hidden_b, axis=0),
            jnp.sum(upper_b * hidden_a, axis=0),
            jnp.sum(upper_b * hidden_b, axis=0),
        ]
    )
    grad_bias, grad_stitch = lax.psum((bias_terms, stitch_terms), "dp")
    dlow_a = dpre_a.astype(jnp.bfloat16)
    dlow_b = dpre_b.astype(jnp.bfloat16)
    block_a = lax.dot_general(full_a, dlow_a, contract_rows, preferred_element_type=jnp.float32)
    block_b = lax.dot_general(full_b, dlow_b, contract_rows, preferred_element_type=jnp.float32)
    grad_weight_a = lax.psum_scatter(block_a, "dp", scatter_dimension=0, tiled=True)
    grad_weight_b = lax.psum_scatter(block_b, "dp", scatter_dimension=0, tiled=True)
    part_a = lax.dot_general(weight_a, dlow_a, contract_units, preferred_element_type=jnp.float32)
    part_b = lax.dot_general(weight_b, dlow_b, contract_units, preferred_element_type=jnp.float32)
    summed = lax.psum_scatter(
        jnp.concatenate([part_a, part_b], axis=1), "mp", scatter_dimension=0, tiled=True
    )
    keep_cols = keep_mask.T
    grad_image_a = (summed[:, :batch_rows] * keep_cols).astype(jnp.bfloat16)
    grad_image_b = (summed[:, batch_rows:] * keep_cols).astype(jnp.bfloat16)
    return (
        stitched_a,
        stitched_b,
        grad_image_a,
        grad_image_b,
        grad_weight_a,
        grad_weight_b,
        grad_bias,
        grad_stitch,
    )


SWAP_CORE = [(d, d ^ 1) for d in range(8)]
NEAR_Z = [(d, d ^ 2) for d in range(8)]
FAR_Z = [(d, d ^ 4) for d in range(8)]
ENDS_IN = [(0, 2), (1, 3), (6, 4), (7, 5)]
MIDS = [(2, 4), (3, 5), (4, 2), (5, 3)]
ENDS_OUT = [(2, 0), (3, 1), (4, 6), (5, 7)]
SLOTS = ((3, 2, 1, 0), (3, 2, 0, 1), (0, 1, 3, 2), (0, 1, 2, 3))
LANES = 128
EXTRA = 16
VMEM_LIMIT = 24 * 1024 * 1024
SMEM = pl.BlockSpec(memory_space=pltpu.SMEM)
VMEM = pl.BlockSpec(memory_space=pltpu.VMEM)
HBM = pl.BlockSpec(memory_space=pltpu.HBM)
LITTLE = pl.CostEstimate(flops=1, bytes_accessed=1, transcendentals=0)


def low(x):
    return x.astype(jnp.bfloat16)


def wide(x):
    return x.astype(jnp.float32)


def array(shape, dtype):
    return jax.ShapeDtypeStruct(shape, dtype)


def call(kernel, out_shape, in_specs, out_specs, name, scratch=()):
    return pl.pallas_call(
        kernel,
        out_shape=out_shape,
        in_specs=in_specs,
        out_specs=out_specs,
        scratch_shapes=scratch,
        compiler_params=pltpu.CompilerParams(vmem_limit_bytes=VMEM_LIMIT),
        cost_estimate=LITTLE,
        name=name,
    )


def marks_of(marks, where, cols, chunk):
    position = (where[8] * cols + chunk * LANES) // CH
    return marks[0, position], marks[1, position]


def mask_kernel(where, marks, group, image, out):
    rows, cols = image.shape
    second = jnp.broadcast_to(jnp.where(group[...] == 1, 1.0, 0.0), (8, rows)).T[:, 0:1] > 0.5
    for chunk in range(cols // LANES):
        zero, one = marks_of(marks, where, cols, chunk)
        keep = wide(jnp.where(second, one, zero))
        lanes = slice(chunk * LANES, (chunk + 1) * LANES)
        out[:, lanes] = low(wide(image[:, lanes]) * keep)


def mask_image(where, marks, group, image):
    return call(
        mask_kernel, array(image.shape, jnp.bfloat16), [SMEM, SMEM, VMEM, VMEM], VMEM, "mask_image"
    )(where, marks, group, image)


def load_kernel(flip, where, weight, out, sems):
    cols = out.shape[0] // 4
    copies = []
    for k in range(4):
        block = 2 * (where[0] ^ k) + (where[1] ^ flip)
        copies.append(
            pltpu.make_async_copy(
                weight.at[pl.ds(pl.multiple_of(block * cols, cols), cols), :],
                out.at[pl.ds(k * cols, cols), :],
                sems.at[k],
            )
        )
    for copy in copies:
        copy.start()
    for copy in copies:
        copy.wait()


def load(flip, where, weight):
    rows, units = weight.shape
    return call(
        functools.partial(load_kernel, flip),
        pltpu.VMEM((rows // 2, units), weight.dtype),
        [SMEM, HBM],
        VMEM,
        "load_weight",
        [pltpu.SemaphoreType.DMA((4,))],
    )(where, weight)


def open_kernel(p0, p1, p2, mine, other, keep, send):
    cols = p0.shape[1]
    for weight, out in ((mine, keep), (other, send)):
        total = None
        for k, piece in enumerate((p0, p1, p2)):
            term = jnp.dot(
                piece[...],
                weight[k * cols : (k + 1) * cols, :],
                preferred_element_type=jnp.float32,
            )
            total = term if total is None else total + term
        out[...] = total


def forward_open(p0, p1, p2, mine, other):
    shape = (p0.shape[0], mine.shape[1])
    return call(
        open_kernel, [pltpu.VMEM(shape, jnp.float32)] * 2, [VMEM] * 5, [VMEM] * 2, "forward_open"
    )(p0, p1, p2, mine, other)


def close_kernel(where, *refs):
    pieces, (mine, other, keep, send, out, sent) = refs[:-6], refs[-6:]
    cols = pieces[0].shape[1]

    def go(piece):
        sent[...] = send[...] + jnp.dot(
            piece[...], other[3 * cols :, :], preferred_element_type=jnp.float32
        )
        out[...] = keep[...] + jnp.dot(
            piece[...], mine[3 * cols :, :], preferred_element_type=jnp.float32
        )

    if len(pieces) == 1:
        go(pieces[0])
    else:
        pl.when(where[2] == 0)(functools.partial(go, pieces[0]))
        pl.when(where[2] == 1)(functools.partial(go, pieces[1]))


def forward_close(where, *operands):
    shape = operands[-1].shape
    return call(
        close_kernel,
        [array(shape, jnp.float32)] * 2,
        [SMEM] + [VMEM] * len(operands),
        [VMEM] * 2,
        "forward_close",
    )(where, *operands)


def tower_math(own, got, bias, unit_a, unit_b, upper_a, upper_b, dz, dz_t, sums):
    pre = own[...] + got[...] + bias[...]
    sigma = jax.nn.sigmoid(pre)
    hidden = pre * sigma
    cot_a = wide(upper_a[...])
    cot_b = wide(upper_b[...])
    dhid = unit_a[...] * cot_a + unit_b[...] * cot_b
    dpre = dhid * (sigma * (1.0 + pre * (1.0 - sigma)))
    dz[...] = low(dpre)
    dz_t[...] = low(dpre).T
    sums[0:1, :] = jnp.sum(dpre, axis=0, keepdims=True)
    sums[1:2, :] = jnp.sum(cot_a * hidden, axis=0, keepdims=True)
    sums[2:3, :] = jnp.sum(cot_b * hidden, axis=0, keepdims=True)
    sums[3:4, :] = jnp.zeros_like(sums[3:4, :])
    return hidden


def first_kernel(own, got, bias, unit_a, unit_b, upper_a, upper_b, dz, dz_t, sums, hidden):
    hidden[...] = tower_math(own, got, bias, unit_a, unit_b, upper_a, upper_b, dz, dz_t, sums)


def second_kernel(
    own, got, bias, unit_a, unit_b, upper_a, upper_b, earlier, stitch, dz, dz_t, sums, local
):
    hidden = tower_math(own, got, bias, unit_a, unit_b, upper_a, upper_b, dz, dz_t, sums)
    rows = hidden.shape[0]
    before = earlier[...]
    local[0:rows, :] = low(stitch[0:1, :] * before + stitch[1:2, :] * hidden)
    local[rows : 2 * rows, :] = low(stitch[2:3, :] * before + stitch[3:4, :] * hidden)


def tower(kernel, name, last, *operands):
    rows, units = operands[0].shape
    return call(
        kernel,
        [
            array((rows, units), jnp.bfloat16),
            array((units, rows), jnp.bfloat16),
            array((4, units), jnp.float32),
            last,
        ],
        [VMEM] * len(operands),
        [VMEM] * 4,
        name,
    )(*operands)


def part_kernel(first, where, mine, other, dz_t, dzo_t, *outs):
    cols = outs[0].shape[0]
    for k, out in enumerate(outs):
        rows = pl.ds(pl.multiple_of(where[3 + first + k] * cols, cols), cols)
        total = jnp.dot(mine[rows, :], dz_t[...], preferred_element_type=jnp.float32)
        total += jnp.dot(other[rows, :], dzo_t[...], preferred_element_type=jnp.float32)
        out[...] = total.astype(out.dtype)


def parts(first, dtypes, where, mine, other, dz_t, dzo_t):
    shape = (mine.shape[0] // 4, dz_t.shape[1])
    return call(
        functools.partial(part_kernel, first),
        [array(shape, dtype) for dtype in dtypes],
        [SMEM] + [VMEM] * 4,
        [VMEM] * len(dtypes),
        "parts",
    )(where, mine, other, dz_t, dzo_t)


def finish_kernel(where, marks, group, kept, third, cross, last, out):
    second = group[...] == 1
    cols = out.shape[0]
    for chunk in range(cols // LANES):
        zero, one = marks_of(marks, where, cols, chunk)
        keep = wide(jnp.where(second, one, zero))
        rows = slice(chunk * LANES, (chunk + 1) * LANES)
        total = kept[rows, :] + wide(third[rows, :]) + wide(cross[rows, :]) + wide(last[rows, :])
        out[rows, :] = low(total * keep)


def finish(where, marks, group, kept, third, cross, last):
    return call(
        finish_kernel,
        array(kept.shape, jnp.bfloat16),
        [SMEM, SMEM] + [VMEM] * 5,
        VMEM,
        "finish",
    )(where, marks, group, kept, third, cross, last)


def pack_kernel(where, p0, p1, p2, p3, p4, dz, sums, out, extra, sems):
    rows, cols = p0.shape
    units = dz.shape[1]
    copies = []
    for q in range(4):
        block = out.at[q, pl.ds(0, rows), pl.ds(0, cols)]
        k = where[0] ^ q
        for index, piece in enumerate((p0, p1, p2)):
            pl.when(k == index)(pltpu.make_async_copy(piece, block, sems.at[q]).start)
        pl.when((k == 3) & (where[2] == 0))(pltpu.make_async_copy(p3, block, sems.at[q]).start)
        pl.when((k == 3) & (where[2] == 1))(pltpu.make_async_copy(p4, block, sems.at[q]).start)
        copies.append(pltpu.make_async_copy(p0, block, sems.at[q]))
        copy = pltpu.make_async_copy(
            dz, out.at[q, pl.ds(0, rows), pl.ds(cols, units)], sems.at[4 + q]
        )
        copy.start()
        copies.append(copy)
    extra[...] = jnp.zeros_like(extra)
    for k in range(3):
        rest = sums[k : k + 1, :]
        for term in range(3):
            piece = low(rest)
            extra[term : term + 1, k * units : (k + 1) * units] = piece
            rest = rest - wide(piece)
    for q in range(4):
        copy = pltpu.make_async_copy(
            extra, out.at[q, pl.ds(rows, extra.shape[0]), :], sems.at[8 + q]
        )
        copy.start()
        copies.append(copy)
    for copy in copies:
        copy.wait()


def pack(where, *operands):
    rows, cols = operands[0].shape
    units = operands[5].shape[1]
    return call(
        pack_kernel,
        array((4, rows + EXTRA, cols + units), jnp.bfloat16),
        [SMEM] + [HBM] * 6 + [VMEM],
        HBM,
        "pack",
        [pltpu.VMEM((EXTRA, cols + units), jnp.bfloat16), pltpu.SemaphoreType.DMA((12,))],
    )(where, *operands)


def lay_kernel(where, own, next_one, rest, own_far, rest_far, out_a, out_b, sems):
    rows = out_a.shape[0]
    units = own.shape[1]
    copies = []
    for side in range(2):
        for k in range(4):
            block = 2 * (where[0] ^ k) + (where[1] ^ side)
            lanes = pl.ds(pl.multiple_of(block * units, units), units)
            if side == 0 and k < 2:
                source, start = (own, next_one)[k], 0
            else:
                source = ((None, rest), (own_far, rest_far))[side][k // 2]
                start = 2 * rows * (k % 2)
            for half, out in enumerate((out_a, out_b)):
                part = pl.ds(start + half * rows, rows)
                sem = sems.at[side * 8 + k * 2 + half]
                copies.append(pltpu.make_async_copy(source.at[part, :], out.at[:, lanes], sem))
    for copy in copies:
        copy.start()
    for copy in copies:
        copy.wait()


def lay_out(where, *sources):
    rows, units = sources[0].shape
    return call(
        lay_kernel,
        [array((rows // 2, 8 * units), jnp.bfloat16)] * 2,
        [SMEM] + [HBM] * 5,
        [HBM] * 2,
        "lay_out",
        [pltpu.SemaphoreType.DMA((16,))],
    )(where, *sources)


def weight_kernel(where, near, far, out, tiles, sems):
    units = out.shape[1]
    cols = out.shape[0] // 2
    rows = near.shape[1] - EXTRA
    tile = tiles.shape[1]
    steps = cols // tile

    def copy(p, t):
        slot = p * steps + t
        return pltpu.make_async_copy(
            tiles.at[slot], out.at[pl.ds(slot * tile, tile), :], sems.at[slot]
        )

    def dots(p, images):
        for t in range(steps):
            total = None
            for q in range(4):
                term = lax.dot_general(
                    images[q, 0:rows, t * tile : (t + 1) * tile],
                    near[q, 0:rows, cols : cols + units],
                    (((0,), (0,)), ((), ())),
                    preferred_element_type=jnp.float32,
                )
                total = term if total is None else total + term
            tiles[p * steps + t] = total
            copy(p, t).start()

    for p in range(2):
        pl.when(where[1] == p)(functools.partial(dots, p, near))
        pl.when(where[1] != p)(functools.partial(dots, p, far))
    for p in range(2):
        for t in range(steps):
            copy(p, t).wait()


def weight_grad(where, near, far, units):
    cols = near.shape[2] - units
    tile = cols // 3
    return call(
        weight_kernel,
        array((2 * cols, units), jnp.float32),
        [SMEM, VMEM, VMEM],
        HBM,
        "weight_grad",
        [pltpu.VMEM((6, tile, units), jnp.float32), pltpu.SemaphoreType.DMA((6,))],
    )(where, near, far)


def total_sums(got, units):
    terms = wide(got[:, got.shape[1] - EXTRA : got.shape[1] - EXTRA + 3, 0 : 3 * units])
    each = (terms[:, 2] + terms[:, 1]) + terms[:, 0]
    return ((each[0] + each[1]) + (each[2] + each[3])).reshape(3, units)


def add(*terms):
    total = wide(terms[0])
    for term in terms[1:]:
        total = total + wide(term)
    return low(total)


class Line:
    def __init__(self, token):
        self.token = token

    def __call__(self, step, *operands):
        *operands, _ = lax.optimization_barrier((*operands, self.token))
        result = step(*operands)
        self.token = result[0] if isinstance(result, (list, tuple)) else result
        return result


def swap(x):
    return lax.ppermute(x, "mp", SWAP_CORE)


def along(x):
    return lax.ppermute(x, "mp", NEAR_Z)


def across(x):
    return lax.ppermute(x, "mp", FAR_Z)


def inward(x):
    return lax.ppermute(x, "mp", ENDS_IN)


def between(x):
    return lax.ppermute(x, "mp", MIDS)


def outward(x):
    return lax.ppermute(x, "mp", ENDS_OUT)


def exchange(x):
    return lax.all_to_all(x, "dp", 0, 0)


def after(x, *deps):
    return lax.optimization_barrier((x,) + deps)[0]


def fast_shards(
    image_a,
    image_b,
    image_group,
    position_mask,
    weight_a,
    weight_b,
    tower_bias,
    stitch,
    cotan_a,
    cotan_b,
):
    rows, cols = image_a.shape
    units = weight_a.shape[1]
    place = lax.axis_index("mp").astype(jnp.int32)
    z = place // 2
    core = place % 2
    quarter = lax.axis_index("dp").astype(jnp.int32)
    middle = ((z == 1) | (z == 2)).astype(jnp.int32)
    slots = jnp.take(jnp.asarray(SLOTS, jnp.int32), z, axis=0) ^ z
    where = jnp.concatenate(
        [jnp.stack([z, core, middle]), slots, jnp.stack([quarter, place])]
    ).astype(jnp.int32)
    group = image_group[None, :]
    line = Line(where)

    bf16, f32 = jnp.bfloat16, jnp.float32

    a0 = line(mask_image, where, position_mask, group, image_a)
    a2 = across(a0)
    a1 = along(a0)
    b0 = line(mask_image, where, position_mask, group, image_b)
    b2 = across(b0)
    other_a = swap(line(functools.partial(load, 1), where, weight_a))
    mine_a = line(functools.partial(load, 0), where, weight_a)
    other_b = swap(line(functools.partial(load, 1), where, weight_b))
    mine_b = line(functools.partial(load, 0), where, weight_b)
    keep_a, give_a = line(forward_open, a0, a1, a2, mine_a, other_a)
    a3 = along(a2)
    b0_late = after(b0, a2, other_b)
    b1 = along(b0_late)
    b_mid = between(b0_late)
    own_a, sent_a = line(forward_close, where, a3, mine_a, other_a, keep_a, give_a)
    dz_a, dzt_a, sums_a, hidden_a = line(
        functools.partial(tower, first_kernel, "tower_a", array((rows, units), f32)),
        own_a,
        swap(sent_a),
        tower_bias[0:1],
        stitch[0:1],
        stitch[2:3],
        cotan_a,
        cotan_b,
    )
    dzo_a = swap(dzt_a)
    (first_a,) = line(functools.partial(parts, 0, [bf16]), where, mine_a, other_a, dzt_a, dzo_a)
    in1_a = inward(first_a)
    second_a, third_a, kept_a = line(
        functools.partial(parts, 1, [bf16, bf16, f32]), where, mine_a, other_a, dzt_a, dzo_a
    )
    in2_a = inward(second_a)
    b2 = after(b2, second_a)
    b_end = outward(b2)
    got_a = exchange(line(pack, where, a0, a1, a2, a3, a3, dz_a, sums_a))
    keep_b, give_b = line(forward_open, b0, b1, b2, mine_b, other_b)
    mid1_a = between(line(add, first_a, in1_a))
    own_b, sent_b = line(forward_close, where, b_end, b_mid, mine_b, other_b, keep_b, give_b)
    dz_b, dzt_b, sums_b, local = line(
        functools.partial(tower, second_kernel, "tower_b", array((2 * rows, units), bf16)),
        own_b,
        swap(sent_b),
        tower_bias[1:2],
        stitch[1:2],
        stitch[3:4],
        cotan_a,
        cotan_b,
        hidden_a,
        stitch,
    )
    dzo_b = swap(dzt_b)
    s1 = along(local)
    s_mid = between(local)
    (first_b,) = line(functools.partial(parts, 0, [bf16]), where, mine_b, other_b, dzt_b, dzo_b)
    in1_b = inward(first_b)
    mid2_a = between(line(add, second_a, in2_a))
    second_b, third_b, kept_b = line(
        functools.partial(parts, 1, [bf16, bf16, f32]), where, mine_b, other_b, dzt_b, dzo_b
    )
    got_b = exchange(line(pack, where, b0, b1, b2, b_end, b_mid, dz_b, sums_b))
    in2_b = inward(after(second_b, mid1_a))
    out_a = outward(after(line(add, third_a, mid1_a), s1))
    s_out = outward(s_mid)
    s_far = between(after(s1, mid2_a))
    mid1_b = between(line(add, first_b, in1_b))
    far_a = swap(after(got_a, out_a))
    grad_weight_a = line(functools.partial(weight_grad, units=units), where, got_a, far_a)
    in3_a = inward(after(third_a, s_out))
    s_last = outward(s_far)
    in3_b = inward(after(third_b, s_far))
    mid2_b = between(line(add, second_b, in2_b))
    out_b = outward(line(add, third_b, mid1_b))
    grad_image_a = line(finish, where, position_mask, group, kept_a, in3_a, mid2_a, out_a)
    near_far = swap(after(jnp.concatenate([local, s1]), in3_a))
    far_b = swap(after(got_b, s_last))
    at_end = middle == 0
    rest = jnp.concatenate(
        [jnp.where(at_end, s_out, s_far), jnp.where(at_end, s_last, s_mid)]
    )
    rest_far = swap(rest)
    grad_weight_b = line(functools.partial(weight_grad, units=units), where, got_b, far_b)
    stitched_a, stitched_b = line(lay_out, where, local, s1, rest, near_far, rest_far)
    grad_image_b = line(finish, where, position_mask, group, kept_b, in3_b, mid2_b, out_b)
    sums_a = total_sums(got_a, units)
    sums_b = total_sums(got_b, units)
    grad_bias = jnp.stack([sums_a[0], sums_b[0]])
    grad_stitch = jnp.stack([sums_a[1], sums_b[1], sums_a[2], sums_b[2]])
    return (
        stitched_a,
        stitched_b,
        grad_image_a,
        grad_image_b,
        grad_weight_a,
        grad_weight_b,
        grad_bias,
        grad_stitch,
    )


def solution(mesh):
    placed = (
        P("dp", "mp"),
        P("dp", "mp"),
        P("dp"),
        P(),
        P(None, "mp"),
        P(None, "mp"),
        P(None, "mp"),
        P(None, "mp"),
        P("dp", "mp"),
        P("dp", "mp"),
    )
    fits = mesh.shape["dp"] == 4 and mesh.shape["mp"] == 8
    return jax.shard_map(
        fast_shards if fits else general_shards,
        mesh=mesh,
        in_specs=placed,
        out_specs=(
            P("dp", None),
            P("dp", None),
            P("mp", "dp"),
            P("mp", "dp"),
            P("dp", "mp"),
            P("dp", "mp"),
            P(None, "mp"),
            P(None, "mp"),
        ),
        check_vma=False,
    )
```

```python
import functools

import jax
import jax.numpy as jnp
from jax import lax
from jax.experimental import pallas as pl
from jax.experimental.pallas import tpu as pltpu
from jax.sharding import PartitionSpec as P

CH = 256
POS = 36


def keep_block(image_group, position_mask, first_col, cols):
    positions = (first_col + lax.iota(jnp.int32, cols)) // CH
    onehot = (positions[:, None] == lax.iota(jnp.int32, POS)[None, :]).astype(jnp.float32)
    per_position = jnp.dot(onehot, position_mask.astype(jnp.float32).T)
    return jnp.where(
        image_group[:, None] == 1, per_position[:, 1][None, :], per_position[:, 0][None, :]
    )


def general_shards(
    image_a,
    image_b,
    image_group,
    position_mask,
    weight_a,
    weight_b,
    tower_bias,
    stitch,
    cotan_a,
    cotan_b,
):
    batch_rows = image_a.shape[0]
    shard_cols = image_a.shape[1]
    first_col = lax.axis_index("mp") * shard_cols
    keep_mask = keep_block(image_group, position_mask, first_col, shard_cols)
    keep_low = keep_mask.astype(jnp.bfloat16)
    contract_rows = (((0,), (0,)), ((), ()))
    contract_units = (((1,), (1,)), ((), ()))
    full_a = lax.all_gather(image_a * keep_low, "mp", axis=1, tiled=True)
    full_b = lax.all_gather(image_b * keep_low, "mp", axis=1, tiled=True)
    pre_a = jnp.dot(full_a, weight_a, preferred_element_type=jnp.float32) + tower_bias[0][None, :]
    pre_b = jnp.dot(full_b, weight_b, preferred_element_type=jnp.float32) + tower_bias[1][None, :]
    sigma_a = jax.nn.sigmoid(pre_a)
    sigma_b = jax.nn.sigmoid(pre_b)
    hidden_a = pre_a * sigma_a
    hidden_b = pre_b * sigma_b
    local_a = (stitch[0][None, :] * hidden_a + stitch[1][None, :] * hidden_b).astype(jnp.bfloat16)
    local_b = (stitch[2][None, :] * hidden_a + stitch[3][None, :] * hidden_b).astype(jnp.bfloat16)
    stitched_a = lax.all_gather(local_a, "mp", axis=1, tiled=True)
    stitched_b = lax.all_gather(local_b, "mp", axis=1, tiled=True)
    upper_a = cotan_a.astype(jnp.float32)
    upper_b = cotan_b.astype(jnp.float32)
    dhid_a = stitch[0][None, :] * upper_a + stitch[2][None, :] * upper_b
    dhid_b = stitch[1][None, :] * upper_a + stitch[3][None, :] * upper_b
    dpre_a = dhid_a * (sigma_a * (1.0 + pre_a * (1.0 - sigma_a)))
    dpre_b = dhid_b * (sigma_b * (1.0 + pre_b * (1.0 - sigma_b)))
    bias_terms = jnp.stack([jnp.sum(dpre_a, axis=0), jnp.sum(dpre_b, axis=0)])
    stitch_terms = jnp.stack(
        [
            jnp.sum(upper_a * hidden_a, axis=0),
            jnp.sum(upper_a * hidden_b, axis=0),
            jnp.sum(upper_b * hidden_a, axis=0),
            jnp.sum(upper_b * hidden_b, axis=0),
        ]
    )
    grad_bias, grad_stitch = lax.psum((bias_terms, stitch_terms), "dp")
    dlow_a = dpre_a.astype(jnp.bfloat16)
    dlow_b = dpre_b.astype(jnp.bfloat16)
    block_a = lax.dot_general(full_a, dlow_a, contract_rows, preferred_element_type=jnp.float32)
    block_b = lax.dot_general(full_b, dlow_b, contract_rows, preferred_element_type=jnp.float32)
    grad_weight_a = lax.psum_scatter(block_a, "dp", scatter_dimension=0, tiled=True)
    grad_weight_b = lax.psum_scatter(block_b, "dp", scatter_dimension=0, tiled=True)
    part_a = lax.dot_general(weight_a, dlow_a, contract_units, preferred_element_type=jnp.float32)
    part_b = lax.dot_general(weight_b, dlow_b, contract_units, preferred_element_type=jnp.float32)
    summed = lax.psum_scatter(
        jnp.concatenate([part_a, part_b], axis=1), "mp", scatter_dimension=0, tiled=True
    )
    keep_cols = keep_mask.T
    grad_image_a = (summed[:, :batch_rows] * keep_cols).astype(jnp.bfloat16)
    grad_image_b = (summed[:, batch_rows:] * keep_cols).astype(jnp.bfloat16)
    return (
        stitched_a,
        stitched_b,
        grad_image_a,
        grad_image_b,
        grad_weight_a,
        grad_weight_b,
        grad_bias,
        grad_stitch,
    )


SWAP_CORE = [(d, d ^ 1) for d in range(8)]
NEAR_Z = [(d, d ^ 2) for d in range(8)]
FAR_Z = [(d, d ^ 4) for d in range(8)]
ENDS_IN = [(0, 2), (1, 3), (6, 4), (7, 5)]
MIDS = [(2, 4), (3, 5), (4, 2), (5, 3)]
ENDS_OUT = [(2, 0), (3, 1), (4, 6), (5, 7)]
SLOTS = ((3, 2, 1, 0), (3, 2, 0, 1), (0, 1, 3, 2), (0, 1, 2, 3))
LANES = 128
EXTRA = 16
VMEM_LIMIT = 24 * 1024 * 1024
SMEM = pl.BlockSpec(memory_space=pltpu.SMEM)
VMEM = pl.BlockSpec(memory_space=pltpu.VMEM)
HBM = pl.BlockSpec(memory_space=pltpu.HBM)
ANY = pl.BlockSpec(memory_space=pl.ANY)
LITTLE = pl.CostEstimate(flops=1, bytes_accessed=1, transcendentals=0)


def low(x):
    return x.astype(jnp.bfloat16)


def wide(x):
    return x.astype(jnp.float32)


def array(shape, dtype):
    return jax.ShapeDtypeStruct(shape, dtype)


class Line:
    def __init__(self):
        self.before = []

    def __call__(self, step, *operands):
        result = step(*operands)
        self.before = [result[0] if isinstance(result, (list, tuple)) else result]
        return result

    def wait(self, *arrived):
        self.before = [*self.before, *arrived]

    def send(self, move, x):
        x, *self.before = lax.optimization_barrier((x, *self.before))
        return move(x)


line = Line()


def call(kernel, out_shape, in_specs, out_specs, name, scratch=()):
    before = list(line.before)
    first = len(in_specs)

    def body(*refs):
        kernel(*refs[:first], *refs[first + len(before) :])

    run = pl.pallas_call(
        body,
        out_shape=out_shape,
        in_specs=[*in_specs, *[pl.BlockSpec(memory_space=pl.ANY)] * len(before)],
        out_specs=out_specs,
        scratch_shapes=scratch,
        compiler_params=pltpu.CompilerParams(vmem_limit_bytes=VMEM_LIMIT),
        cost_estimate=LITTLE,
        name=name,
    )
    return lambda *operands: run(*operands, *before)


def marks_of(marks, where, cols, chunk):
    position = (where[8] * cols + chunk * LANES) // CH
    return marks[0, position], marks[1, position]


def mask_kernel(where, marks, group, image, out):
    rows, cols = image.shape
    second = jnp.broadcast_to(jnp.where(group[...] == 1, 1.0, 0.0), (8, rows)).T[:, 0:1] > 0.5
    for chunk in range(cols // LANES):
        zero, one = marks_of(marks, where, cols, chunk)
        keep = wide(jnp.where(second, one, zero))
        lanes = slice(chunk * LANES, (chunk + 1) * LANES)
        out[:, lanes] = low(wide(image[:, lanes]) * keep)


def mask_image(where, marks, group, image):
    return call(
        mask_kernel, array(image.shape, jnp.bfloat16), [SMEM, SMEM, VMEM, VMEM], VMEM, "mask_image"
    )(where, marks, group, image)


def load_kernel(flip, where, weight, out, sems):
    cols = out.shape[0] // 4
    copies = []
    for k in range(4):
        block = 2 * (where[0] ^ k) + (where[1] ^ flip)
        copies.append(
            pltpu.make_async_copy(
                weight.at[pl.ds(pl.multiple_of(block * cols, cols), cols), :],
                out.at[pl.ds(k * cols, cols), :],
                sems.at[k],
            )
        )
    for copy in copies:
        copy.start()
    for copy in copies:
        copy.wait()


def load(flip, where, weight):
    rows, units = weight.shape
    return call(
        functools.partial(load_kernel, flip),
        pltpu.VMEM((rows // 2, units), weight.dtype),
        [SMEM, HBM],
        VMEM,
        "load_weight",
        [pltpu.SemaphoreType.DMA((4,))],
    )(where, weight)


def whole_kernel(weight, out, sems):
    rows = out.shape[0] // 8
    copies = [
        pltpu.make_async_copy(
            weight.at[pl.ds(k * rows, rows), :], out.at[pl.ds(k * rows, rows), :], sems.at[k]
        )
        for k in range(8)
    ]
    for copy in copies:
        copy.start()
    for copy in copies:
        copy.wait()


def load_whole(weight):
    return call(
        whole_kernel,
        pltpu.VMEM(weight.shape, weight.dtype),
        [HBM],
        VMEM,
        "load_whole",
        [pltpu.SemaphoreType.DMA((8,))],
    )(weight)


def full_kernel(image, weight, out, chunks, sems):
    steps, _, cols = chunks.shape

    def copy(k):
        return pltpu.make_async_copy(
            image.at[:, pl.ds(k * cols, cols)], chunks.at[k], sems.at[k]
        )

    for k in range(steps):
        copy(k).start()
    total = None
    for k in range(steps):
        copy(k).wait()
        term = jnp.dot(
            chunks[k], weight[k * cols : (k + 1) * cols, :], preferred_element_type=jnp.float32
        )
        total = term if total is None else total + term
    out[...] = total


def forward_full(image, weight):
    rows = image.shape[0]
    cols = image.shape[1] // 8
    return call(
        full_kernel,
        array((rows, weight.shape[1]), jnp.float32),
        [HBM, VMEM],
        VMEM,
        "forward_full",
        [pltpu.VMEM((8, rows, cols), jnp.bfloat16), pltpu.SemaphoreType.DMA((8,))],
    )(image, weight)


def open_kernel(p0, p1, p2, mine, other, keep, send):
    cols = p0.shape[1]
    for weight, out in ((mine, keep), (other, send)):
        total = None
        for k, piece in enumerate((p0, p1, p2)):
            term = jnp.dot(
                piece[...],
                weight[k * cols : (k + 1) * cols, :],
                preferred_element_type=jnp.float32,
            )
            total = term if total is None else total + term
        out[...] = total


def forward_open(p0, p1, p2, mine, other):
    shape = (p0.shape[0], mine.shape[1])
    return call(
        open_kernel, [pltpu.VMEM(shape, jnp.float32)] * 2, [VMEM] * 5, [VMEM] * 2, "forward_open"
    )(p0, p1, p2, mine, other)


def close_kernel(where, *refs):
    pieces, (mine, other, keep, send, out, sent) = refs[:-6], refs[-6:]
    cols = pieces[0].shape[1]

    def go(piece):
        sent[...] = send[...] + jnp.dot(
            piece[...], other[3 * cols :, :], preferred_element_type=jnp.float32
        )
        out[...] = keep[...] + jnp.dot(
            piece[...], mine[3 * cols :, :], preferred_element_type=jnp.float32
        )

    if len(pieces) == 1:
        go(pieces[0])
    else:
        pl.when(where[2] == 0)(functools.partial(go, pieces[0]))
        pl.when(where[2] == 1)(functools.partial(go, pieces[1]))


def forward_close(where, *operands):
    shape = operands[-1].shape
    return call(
        close_kernel,
        [array(shape, jnp.float32)] * 2,
        [SMEM] + [VMEM] * len(operands),
        [VMEM] * 2,
        "forward_close",
    )(where, *operands)


def tower_math(pre, bias, unit_a, unit_b, upper_a, upper_b, dz, dz_t, sums):
    pre = pre + bias[...]
    sigma = jax.nn.sigmoid(pre)
    hidden = pre * sigma
    cot_a = wide(upper_a[...])
    cot_b = wide(upper_b[...])
    dhid = unit_a[...] * cot_a + unit_b[...] * cot_b
    dpre = dhid * (sigma * (1.0 + pre * (1.0 - sigma)))
    dz[...] = low(dpre)
    dz_t[...] = low(dpre).T
    sums[0:1, :] = jnp.sum(dpre, axis=0, keepdims=True)
    sums[1:2, :] = jnp.sum(cot_a * hidden, axis=0, keepdims=True)
    sums[2:3, :] = jnp.sum(cot_b * hidden, axis=0, keepdims=True)
    sums[3:4, :] = jnp.zeros_like(sums[3:4, :])
    return hidden


def first_kernel(own, got, bias, unit_a, unit_b, upper_a, upper_b, dz, dz_t, sums, hidden):
    hidden[...] = tower_math(own[...] + got[...], bias, unit_a, unit_b, upper_a, upper_b, dz, dz_t, sums)


def second_kernel(
    own, bias, unit_a, unit_b, upper_a, upper_b, earlier, stitch, dz, dz_t, sums, local
):
    hidden = tower_math(own[...], bias, unit_a, unit_b, upper_a, upper_b, dz, dz_t, sums)
    rows = hidden.shape[0]
    before = earlier[...]
    local[0:rows, :] = low(stitch[0:1, :] * before + stitch[1:2, :] * hidden)
    local[rows : 2 * rows, :] = low(stitch[2:3, :] * before + stitch[3:4, :] * hidden)


def tower(kernel, name, last, *operands):
    rows, units = operands[0].shape
    return call(
        kernel,
        [
            array((rows, units), jnp.bfloat16),
            array((units, rows), jnp.bfloat16),
            array((4, units), jnp.float32),
            last,
        ],
        [VMEM] * len(operands),
        [VMEM] * 4,
        name,
    )(*operands)


def part_kernel(first, where, mine, other, dz_t, dzo_t, *outs):
    cols = outs[0].shape[0]
    for k, out in enumerate(outs):
        slot = where[3 + first + k]
        rows = pl.ds(pl.multiple_of(slot * cols, cols), cols)
        place = slot
        if mine.shape[0] > other.shape[0]:
            place = 2 * (slot ^ where[0]) + where[1]
        own = pl.ds(pl.multiple_of(place * cols, cols), cols)
        total = jnp.dot(mine[own, :], dz_t[...], preferred_element_type=jnp.float32)
        total += jnp.dot(other[rows, :], dzo_t[...], preferred_element_type=jnp.float32)
        out[...] = total.astype(out.dtype)


def parts(first, dtypes, where, mine, other, dz_t, dzo_t):
    shape = (other.shape[0] // 4, dz_t.shape[1])
    return call(
        functools.partial(part_kernel, first),
        [array(shape, dtype) for dtype in dtypes],
        [SMEM] + [VMEM] * 4,
        [VMEM] * len(dtypes),
        "parts",
    )(where, mine, other, dz_t, dzo_t)


def finish_kernel(where, marks, group, kept, third, cross, last, out):
    second = group[...] == 1
    cols = out.shape[0]
    for chunk in range(cols // LANES):
        zero, one = marks_of(marks, where, cols, chunk)
        keep = wide(jnp.where(second, one, zero))
        rows = slice(chunk * LANES, (chunk + 1) * LANES)
        total = kept[rows, :] + wide(third[rows, :]) + wide(cross[rows, :]) + wide(last[rows, :])
        out[rows, :] = low(total * keep)


def finish(where, marks, group, kept, third, cross, last):
    return call(
        finish_kernel,
        array(kept.shape, jnp.bfloat16),
        [SMEM, SMEM] + [VMEM] * 5,
        VMEM,
        "finish",
    )(where, marks, group, kept, third, cross, last)


def sum_rows(sums, extra, start, units):
    extra[...] = jnp.zeros_like(extra)
    for k in range(3):
        rest = sums[k : k + 1, :]
        for term in range(3):
            piece = low(rest)
            extra[3 * k + term : 3 * k + term + 1, start : start + units] = piece
            rest = rest - wide(piece)


def images_kernel(where, p0, p1, p2, p3, out, sems):
    for q in range(4):
        k = where[0] ^ q
        for index, piece in enumerate((p0, p1, p2, p3)):
            pl.when(k == index)(pltpu.make_async_copy(piece, out.at[q], sems.at[q]).start)
    for q in range(4):
        pltpu.make_async_copy(p0, out.at[q], sems.at[q]).wait()


def pack_images(where, *pieces):
    rows, cols = pieces[0].shape
    return call(
        images_kernel,
        array((4, rows, cols), jnp.bfloat16),
        [SMEM] + [ANY] * 4,
        HBM,
        "pack_images",
        [pltpu.SemaphoreType.DMA((4,))],
    )(where, *pieces)


def dz_kernel(dz, sums, out, extra, sems):
    rows, units = dz.shape
    copies = [
        pltpu.make_async_copy(dz, out.at[q, pl.ds(0, rows), :], sems.at[q]) for q in range(4)
    ]
    for copy in copies:
        copy.start()
    sum_rows(sums, extra, 0, units)
    more = [
        pltpu.make_async_copy(extra, out.at[q, pl.ds(rows, EXTRA), :], sems.at[4 + q])
        for q in range(4)
    ]
    for copy in more:
        copy.start()
    for copy in copies + more:
        copy.wait()


def pack_dz(dz, sums):
    rows, units = dz.shape
    return call(
        dz_kernel,
        array((4, rows + EXTRA, units), jnp.bfloat16),
        [ANY, VMEM],
        HBM,
        "pack_dz",
        [pltpu.VMEM((EXTRA, units), jnp.bfloat16), pltpu.SemaphoreType.DMA((8,))],
    )(dz, sums)


def both_kernel(where, image, dz, sums, out, extra, sems):
    rows, units = dz.shape
    cols = out.shape[2] - units
    copies = []
    for q in range(4):
        block = pl.ds(pl.multiple_of((2 * q + where[1]) * cols, cols), cols)
        copies.append(
            pltpu.make_async_copy(
                image.at[:, block], out.at[q, pl.ds(0, rows), pl.ds(0, cols)], sems.at[q]
            )
        )
        copies.append(
            pltpu.make_async_copy(
                dz, out.at[q, pl.ds(0, rows), pl.ds(cols, units)], sems.at[4 + q]
            )
        )
    for copy in copies:
        copy.start()
    sum_rows(sums, extra, cols, units)
    more = [
        pltpu.make_async_copy(extra, out.at[q, pl.ds(rows, EXTRA), :], sems.at[8 + q])
        for q in range(4)
    ]
    for copy in more:
        copy.start()
    for copy in copies + more:
        copy.wait()


def pack_both(where, image, dz, sums):
    rows, units = dz.shape
    cols = image.shape[1] // 8
    return call(
        both_kernel,
        array((4, rows + EXTRA, cols + units), jnp.bfloat16),
        [SMEM, HBM, ANY, VMEM],
        HBM,
        "pack_both",
        [pltpu.VMEM((EXTRA, cols + units), jnp.bfloat16), pltpu.SemaphoreType.DMA((12,))],
    )(where, image, dz, sums)


def weight_kernel(at, where, near, dz, *refs):
    *far, out, tiles, sems = refs
    units = out.shape[1]
    cols = out.shape[0] // 2
    rows = dz.shape[1] - EXTRA
    tile = tiles.shape[1]
    steps = cols // tile

    def copy(p, t):
        slot = p * steps + t
        return pltpu.make_async_copy(
            tiles.at[slot], out.at[pl.ds(slot * tile, tile), :], sems.at[slot]
        )

    def block(images, q, lanes):
        if len(images) == 4:
            return images[q][0:rows, lanes]
        return images[0][q, 0:rows, lanes]

    def dots(p, images):
        for t in range(steps):
            total = None
            for q in range(4):
                term = lax.dot_general(
                    block(images, q, slice(t * tile, (t + 1) * tile)),
                    dz[q, 0:rows, at : at + units],
                    (((0,), (0,)), ((), ())),
                    preferred_element_type=jnp.float32,
                )
                total = term if total is None else total + term
            tiles[p * steps + t] = total
            copy(p, t).start()

    for p in range(2):
        pl.when(where[1] == p)(functools.partial(dots, p, [near]))
        pl.when(where[1] != p)(functools.partial(dots, p, far))
    for p in range(2):
        for t in range(steps):
            copy(p, t).wait()


def weight_grad(cols, units, at, where, near, dz, *far):
    tile = cols // 3
    return call(
        functools.partial(weight_kernel, at),
        array((2 * cols, units), jnp.float32),
        [SMEM] + [VMEM] * (2 + len(far)),
        HBM,
        "weight_grad",
        [pltpu.VMEM((6, tile, units), jnp.float32), pltpu.SemaphoreType.DMA((6,))],
    )(where, near, dz, *far)


def total_sums(got, start, units):
    end = got.shape[1] - EXTRA
    terms = wide(got[:, end : end + 9, start : start + units]).reshape(4, 3, 3, units)
    each = (terms[:, :, 2] + terms[:, :, 1]) + terms[:, :, 0]
    return (each[0] + each[1]) + (each[2] + each[3])


def add_kernel(one, two, out):
    out[...] = low(wide(one[...]) + wide(two[...]))


def add(one, two):
    return call(add_kernel, array(one.shape, jnp.bfloat16), [VMEM, VMEM], VMEM, "add")(one, two)


def swap(x):
    return lax.ppermute(x, "mp", SWAP_CORE)


def along(x):
    return lax.ppermute(x, "mp", NEAR_Z)


def across(x):
    return lax.ppermute(x, "mp", FAR_Z)


def inward(x):
    return lax.ppermute(x, "mp", ENDS_IN)


def between(x):
    return lax.ppermute(x, "mp", MIDS)


def outward(x):
    return lax.ppermute(x, "mp", ENDS_OUT)


def exchange(x):
    return lax.all_to_all(x, "dp", 0, 0)


def after(x, *deps):
    return lax.optimization_barrier((x,) + deps)[0]


def fast_shards(
    image_a,
    image_b,
    image_group,
    position_mask,
    weight_a,
    weight_b,
    tower_bias,
    stitch,
    cotan_a,
    cotan_b,
):
    rows, cols = image_a.shape
    units = weight_a.shape[1]
    place = lax.axis_index("mp").astype(jnp.int32)
    z = place // 2
    core = place % 2
    quarter = lax.axis_index("dp").astype(jnp.int32)
    middle = ((z == 1) | (z == 2)).astype(jnp.int32)
    slots = jnp.take(jnp.asarray(SLOTS, jnp.int32), z, axis=0) ^ z
    where = jnp.concatenate(
        [jnp.stack([z, core, middle]), slots, jnp.stack([quarter, place])]
    ).astype(jnp.int32)
    group = image_group[None, :]
    line.before = []

    bf16, f32 = jnp.bfloat16, jnp.float32
    send, wait = line.send, line.wait

    def first_part(mine, other, dz_t, dzo_t):
        return line(functools.partial(parts, 0, [bf16]), where, mine, other, dz_t, dzo_t)[0]

    def other_parts(mine, other, dz_t, dzo_t):
        return line(
            functools.partial(parts, 1, [bf16, bf16, f32]), where, mine, other, dz_t, dzo_t
        )

    swap_a = swap(weight_a)
    swap_b = swap(weight_b)
    a0 = line(mask_image, where, position_mask, group, image_a)
    a2 = send(across, a0)
    a1 = send(along, a0)
    b0 = line(mask_image, where, position_mask, group, image_b)
    full_b = lax.all_gather(b0, "mp", axis=1, tiled=True)
    mine_a = line(functools.partial(load, 0), where, weight_a)
    mine_b = line(load_whole, weight_b)
    wait(a1, a2)
    a3 = send(along, a2)
    other_a = line(functools.partial(load, 0), where, swap_a)
    keep_a, give_a = line(forward_open, a0, a1, a2, mine_a, other_a)
    other_b = line(functools.partial(load, 0), where, swap_b)
    wait(a3)
    own_a, sent_a = line(forward_close, where, a3, mine_a, other_a, keep_a, give_a)
    got_sum = send(swap, sent_a)
    got_a = send(exchange, line(pack_images, where, a0, a1, a2, a3))
    wait(got_sum)
    dz_a, dzt_a, sums_a, hidden_a = line(
        functools.partial(tower, first_kernel, "tower_a", array((rows, units), f32)),
        own_a,
        got_sum,
        tower_bias[0:1],
        stitch[0:1],
        stitch[2:3],
        cotan_a,
        cotan_b,
    )
    dzo_a = send(swap, dzt_a)
    wait(dzo_a)
    first_a = first_part(mine_a, other_a, dzt_a, dzo_a)
    in1_a = send(inward, first_a)
    second_a, third_a, kept_a = other_parts(mine_a, other_a, dzt_a, dzo_a)
    in2_a = send(inward, second_a)
    packed_dz = line(pack_dz, dz_a, sums_a)
    wait(in1_a)
    sum1_a = line(add, first_a, in1_a)
    mid1_a = send(between, sum1_a)
    wait(got_a)
    far_a = send(swap, got_a)
    dzs_a = send(exchange, packed_dz)
    wait(in2_a)
    sum2_a = line(add, second_a, in2_a)
    wait(full_b)
    own_b = line(forward_full, full_b, mine_b)
    dz_b, dzt_b, sums_b, local = line(
        functools.partial(tower, second_kernel, "tower_b", array((2 * rows, units), bf16)),
        own_b,
        tower_bias[1:2],
        stitch[1:2],
        stitch[3:4],
        cotan_a,
        cotan_b,
        hidden_a,
        stitch,
    )
    dzo_b = send(swap, dzt_b)
    stitched = lax.all_gather(local, "mp", axis=1, tiled=True)
    wait(dzs_a)
    got_b = send(exchange, line(pack_both, where, full_b, dz_b, sums_b))
    wait(dzo_b)
    first_b = first_part(mine_b, other_b, dzt_b, dzo_b)
    in1_b = send(inward, first_b)
    second_b, third_b, kept_b = other_parts(mine_b, other_b, dzt_b, dzo_b)
    in2_b = send(inward, second_b)
    mid2_a = send(between, sum2_a)
    wait(mid1_a)
    out_a = send(outward, line(add, third_a, mid1_a))
    wait(far_a)
    grad_weight_a = line(
        functools.partial(weight_grad, cols, units, 0), where, got_a, dzs_a, far_a
    )
    wait(in1_b)
    mid1_b = send(between, line(add, first_b, in1_b))
    in3_b = send(inward, third_b)
    wait(in2_b)
    mid2_b = send(between, line(add, second_b, in2_b))
    in3_a = send(inward, third_a)
    wait(mid1_b)
    out_b = send(outward, line(add, third_b, mid1_b))
    far_b = [send(swap, got_b[q]) for q in range(4)]
    wait(in3_a, mid2_a, out_a)
    grad_image_a = line(finish, where, position_mask, group, kept_a, in3_a, mid2_a, out_a)
    grad_weight_b = line(
        functools.partial(weight_grad, cols, units, cols), where, got_b, got_b, *far_b
    )
    grad_image_b = line(finish, where, position_mask, group, kept_b, in3_b, mid2_b, out_b)
    sums_a = total_sums(dzs_a, 0, units)
    sums_b = total_sums(got_b, cols, units)
    grad_bias = jnp.stack([sums_a[0], sums_b[0]])
    grad_stitch = jnp.stack([sums_a[1], sums_b[1], sums_a[2], sums_b[2]])
    return (
        stitched[:rows],
        stitched[rows:],
        grad_image_a,
        grad_image_b,
        grad_weight_a,
        grad_weight_b,
        grad_bias,
        grad_stitch,
    )


def solution(mesh):
    placed = (
        P("dp", "mp"),
        P("dp", "mp"),
        P("dp"),
        P(),
        P(None, "mp"),
        P(None, "mp"),
        P(None, "mp"),
        P(None, "mp"),
        P("dp", "mp"),
        P("dp", "mp"),
    )
    fits = mesh.shape["dp"] == 4 and mesh.shape["mp"] == 8
    return jax.shard_map(
        fast_shards if fits else general_shards,
        mesh=mesh,
        in_specs=placed,
        out_specs=(
            P("dp", None),
            P("dp", None),
            P("mp", "dp"),
            P("mp", "dp"),
            P("dp", "mp"),
            P("dp", "mp"),
            P(None, "mp"),
            P(None, "mp"),
        ),
        check_vma=False,
    )
```

```python
import functools

import jax
import jax.numpy as jnp
from jax import lax
from jax.experimental import pallas as pl
from jax.experimental.pallas import tpu as pltpu
from jax.sharding import PartitionSpec as P

CH = 256
POS = 36


def keep_block(image_group, position_mask, first_col, cols):
    positions = (first_col + lax.iota(jnp.int32, cols)) // CH
    onehot = (positions[:, None] == lax.iota(jnp.int32, POS)[None, :]).astype(jnp.float32)
    per_position = jnp.dot(onehot, position_mask.astype(jnp.float32).T)
    return jnp.where(
        image_group[:, None] == 1, per_position[:, 1][None, :], per_position[:, 0][None, :]
    )


def general_shards(
    image_a,
    image_b,
    image_group,
    position_mask,
    weight_a,
    weight_b,
    tower_bias,
    stitch,
    cotan_a,
    cotan_b,
):
    batch_rows = image_a.shape[0]
    shard_cols = image_a.shape[1]
    first_col = lax.axis_index("mp") * shard_cols
    keep_mask = keep_block(image_group, position_mask, first_col, shard_cols)
    keep_low = keep_mask.astype(jnp.bfloat16)
    contract_rows = (((0,), (0,)), ((), ()))
    contract_units = (((1,), (1,)), ((), ()))
    full_a = lax.all_gather(image_a * keep_low, "mp", axis=1, tiled=True)
    full_b = lax.all_gather(image_b * keep_low, "mp", axis=1, tiled=True)
    pre_a = jnp.dot(full_a, weight_a, preferred_element_type=jnp.float32) + tower_bias[0][None, :]
    pre_b = jnp.dot(full_b, weight_b, preferred_element_type=jnp.float32) + tower_bias[1][None, :]
    sigma_a = jax.nn.sigmoid(pre_a)
    sigma_b = jax.nn.sigmoid(pre_b)
    hidden_a = pre_a * sigma_a
    hidden_b = pre_b * sigma_b
    local_a = (stitch[0][None, :] * hidden_a + stitch[1][None, :] * hidden_b).astype(jnp.bfloat16)
    local_b = (stitch[2][None, :] * hidden_a + stitch[3][None, :] * hidden_b).astype(jnp.bfloat16)
    stitched_a = lax.all_gather(local_a, "mp", axis=1, tiled=True)
    stitched_b = lax.all_gather(local_b, "mp", axis=1, tiled=True)
    upper_a = cotan_a.astype(jnp.float32)
    upper_b = cotan_b.astype(jnp.float32)
    dhid_a = stitch[0][None, :] * upper_a + stitch[2][None, :] * upper_b
    dhid_b = stitch[1][None, :] * upper_a + stitch[3][None, :] * upper_b
    dpre_a = dhid_a * (sigma_a * (1.0 + pre_a * (1.0 - sigma_a)))
    dpre_b = dhid_b * (sigma_b * (1.0 + pre_b * (1.0 - sigma_b)))
    bias_terms = jnp.stack([jnp.sum(dpre_a, axis=0), jnp.sum(dpre_b, axis=0)])
    stitch_terms = jnp.stack(
        [
            jnp.sum(upper_a * hidden_a, axis=0),
            jnp.sum(upper_a * hidden_b, axis=0),
            jnp.sum(upper_b * hidden_a, axis=0),
            jnp.sum(upper_b * hidden_b, axis=0),
        ]
    )
    grad_bias, grad_stitch = lax.psum((bias_terms, stitch_terms), "dp")
    dlow_a = dpre_a.astype(jnp.bfloat16)
    dlow_b = dpre_b.astype(jnp.bfloat16)
    block_a = lax.dot_general(full_a, dlow_a, contract_rows, preferred_element_type=jnp.float32)
    block_b = lax.dot_general(full_b, dlow_b, contract_rows, preferred_element_type=jnp.float32)
    grad_weight_a = lax.psum_scatter(block_a, "dp", scatter_dimension=0, tiled=True)
    grad_weight_b = lax.psum_scatter(block_b, "dp", scatter_dimension=0, tiled=True)
    part_a = lax.dot_general(weight_a, dlow_a, contract_units, preferred_element_type=jnp.float32)
    part_b = lax.dot_general(weight_b, dlow_b, contract_units, preferred_element_type=jnp.float32)
    summed = lax.psum_scatter(
        jnp.concatenate([part_a, part_b], axis=1), "mp", scatter_dimension=0, tiled=True
    )
    keep_cols = keep_mask.T
    grad_image_a = (summed[:, :batch_rows] * keep_cols).astype(jnp.bfloat16)
    grad_image_b = (summed[:, batch_rows:] * keep_cols).astype(jnp.bfloat16)
    return (
        stitched_a,
        stitched_b,
        grad_image_a,
        grad_image_b,
        grad_weight_a,
        grad_weight_b,
        grad_bias,
        grad_stitch,
    )


SWAP_CORE = [(d, d ^ 1) for d in range(8)]
NEAR_Z = [(d, d ^ 2) for d in range(8)]
FAR_Z = [(d, d ^ 4) for d in range(8)]
ENDS_IN = [(0, 2), (1, 3), (6, 4), (7, 5)]
MIDS = [(2, 4), (3, 5), (4, 2), (5, 3)]
ENDS_OUT = [(2, 0), (3, 1), (4, 6), (5, 7)]
SLOTS = ((3, 2, 1, 0), (3, 2, 0, 1), (0, 1, 3, 2), (0, 1, 2, 3))
LANES = 128
EXTRA = 16
VMEM_LIMIT = 14 * 1024 * 1024
SMEM = pl.BlockSpec(memory_space=pltpu.SMEM)
VMEM = pl.BlockSpec(memory_space=pltpu.VMEM)
HBM = pl.BlockSpec(memory_space=pltpu.HBM)
ANY = pl.BlockSpec(memory_space=pl.ANY)
LITTLE = pl.CostEstimate(flops=1, bytes_accessed=1, transcendentals=0)


def low(x):
    return x.astype(jnp.bfloat16)


def wide(x):
    return x.astype(jnp.float32)


def array(shape, dtype):
    return jax.ShapeDtypeStruct(shape, dtype)


class Line:
    def __init__(self):
        self.token = None

    def tie(self, *xs):
        if self.token is None:
            return xs
        *xs, self.token = lax.optimization_barrier((*xs, self.token))
        return xs

    def wait(self, *arrived):
        arrived = self.tie(*arrived)
        return arrived if len(arrived) > 1 else arrived[0]

    def send(self, move, x):
        return move(*self.tie(x))


line = Line()


def call(kernel, out_shape, in_specs, out_specs, name, scratch=()):
    single = not isinstance(out_shape, list)
    outs = [out_shape] if single else out_shape
    places = [out_specs] if single else out_specs
    n_in, n_out = len(in_specs), len(outs)
    before = () if line.token is None else (line.token,)

    def body(*refs):
        start = n_in + len(before)
        refs[start + n_out][...] = jnp.zeros((8, LANES), jnp.float32)
        kernel(*refs[:n_in], *refs[start : start + n_out], *refs[start + n_out + 1 :])

    run = pl.pallas_call(
        body,
        out_shape=[*outs, array((8, LANES), jnp.float32)],
        in_specs=[*in_specs, *[HBM] * len(before)],
        out_specs=[*places, VMEM],
        scratch_shapes=scratch,
        compiler_params=pltpu.CompilerParams(vmem_limit_bytes=VMEM_LIMIT),
        cost_estimate=LITTLE,
        name=name,
    )

    def go(*operands):
        *results, line.token = run(*operands, *before)
        return results[0] if single else results

    return go


def marks_of(marks, where, cols, chunk):
    position = (where[8] * cols + chunk * LANES) // CH
    return marks[0, position], marks[1, position]


def mask_kernel(where, marks, group, image, out):
    rows, cols = image.shape
    second = jnp.broadcast_to(jnp.where(group[...] == 1, 1.0, 0.0), (8, rows)).T[:, 0:1] > 0.5
    for chunk in range(cols // LANES):
        zero, one = marks_of(marks, where, cols, chunk)
        keep = wide(jnp.where(second, one, zero))
        lanes = slice(chunk * LANES, (chunk + 1) * LANES)
        out[:, lanes] = low(wide(image[:, lanes]) * keep)


def mask_image(where, marks, group, image):
    return call(
        mask_kernel, array(image.shape, jnp.bfloat16), [SMEM, SMEM, VMEM, VMEM], VMEM, "mask_image"
    )(where, marks, group, image)


def load_kernel(where, weight, out, sems):
    cols = out.shape[0] // 4
    copies = []
    for k in range(4):
        block = 2 * (where[0] ^ k) + where[1]
        copies.append(
            pltpu.make_async_copy(
                weight.at[pl.ds(pl.multiple_of(block * cols, cols), cols), :],
                out.at[pl.ds(k * cols, cols), :],
                sems.at[k],
            )
        )
    for copy in copies:
        copy.start()
    for copy in copies:
        copy.wait()


def load(where, weight):
    rows, units = weight.shape
    weight = pltpu.with_memory_space_constraint(weight, pltpu.HBM)
    return call(
        load_kernel,
        pltpu.VMEM((rows // 2, units), weight.dtype),
        [SMEM, HBM],
        VMEM,
        "load_weight",
        [pltpu.SemaphoreType.DMA((4,))],
    )(where, weight)


def dot(x, y):
    return jnp.dot(x, y, preferred_element_type=jnp.float32)


def open_kernel(p0, p1, p2, mine, other, keep, send):
    cols = p0.shape[1]
    for weight, out in ((mine, keep), (other, send)):
        total = None
        for k, piece in enumerate((p0, p1, p2)):
            term = dot(piece[...], weight[k * cols : (k + 1) * cols, :])
            total = term if total is None else total + term
        out[...] = total


def forward_open(p0, p1, p2, mine, other):
    out = array((p0.shape[0], mine.shape[1]), jnp.float32)
    return call(open_kernel, [out] * 2, [VMEM] * 5, [VMEM] * 2, "forward_open")(
        p0, p1, p2, mine, other
    )


def close_kernel(p3, mine, other, keep, send, out, sent):
    cols = p3.shape[1]
    sent[...] = send[...] + dot(p3[...], other[3 * cols :, :])
    out[...] = keep[...] + dot(p3[...], mine[3 * cols :, :])


def forward_close(*operands):
    out = array(operands[-1].shape, jnp.float32)
    return call(close_kernel, [out] * 2, [VMEM] * 5, [VMEM] * 2, "forward_close")(*operands)


def tower_math(pre, bias, unit_a, unit_b, upper_a, upper_b, dz, dz_t, sums):
    pre = pre + bias[...]
    sigma = jax.nn.sigmoid(pre)
    hidden = pre * sigma
    cot_a = wide(upper_a[...])
    cot_b = wide(upper_b[...])
    dhid = unit_a[...] * cot_a + unit_b[...] * cot_b
    dpre = dhid * (sigma * (1.0 + pre * (1.0 - sigma)))
    dz[...] = low(dpre)
    dz_t[...] = low(dpre).T
    sums[0:1, :] = jnp.sum(dpre, axis=0, keepdims=True)
    sums[1:2, :] = jnp.sum(cot_a * hidden, axis=0, keepdims=True)
    sums[2:3, :] = jnp.sum(cot_b * hidden, axis=0, keepdims=True)
    sums[3:4, :] = jnp.zeros_like(sums[3:4, :])
    return hidden


def first_kernel(own, got, bias, stitch, upper_a, upper_b, dz, dz_t, sums, hidden):
    hidden[...] = tower_math(
        own[...] + got[...],
        bias[0:1, :],
        stitch[0:1, :],
        stitch[2:3, :],
        upper_a,
        upper_b,
        dz,
        dz_t,
        sums,
    )


def second_kernel(own, got, earlier, bias, stitch, upper_a, upper_b, dz, dz_t, sums, local):
    hidden = tower_math(
        own[...] + got[...],
        bias[1:2, :],
        stitch[1:2, :],
        stitch[3:4, :],
        upper_a,
        upper_b,
        dz,
        dz_t,
        sums,
    )
    rows = hidden.shape[0]
    before = earlier[...]
    local[0:rows, :] = low(stitch[0:1, :] * before + stitch[1:2, :] * hidden)
    local[rows : 2 * rows, :] = low(stitch[2:3, :] * before + stitch[3:4, :] * hidden)


def tower(kernel, name, last, *operands):
    rows, units = operands[0].shape
    return call(
        kernel,
        [
            array((rows, units), jnp.bfloat16),
            array((units, rows), jnp.bfloat16),
            array((4, units), jnp.float32),
            last,
        ],
        [VMEM] * len(operands),
        [VMEM] * 4,
        name,
    )(*operands)


def part_kernel(slots, where, mine, other, dz_t, dzo_t, *outs):
    cols = mine.shape[0] // 4
    for slot, at, block in slots:
        rows = pl.ds(pl.multiple_of(where[3 + slot] * cols, cols), cols)
        total = dot(mine[rows, :], dz_t[...]) + dot(other[rows, :], dzo_t[...])
        outs[at][block * cols : (block + 1) * cols, :] = total.astype(outs[at].dtype)


def parts(slots, outs, where, mine, other, dz_t, dzo_t):
    cols = mine.shape[0] // 4
    rows = dz_t.shape[1]
    return call(
        functools.partial(part_kernel, slots),
        [array((blocks * cols, rows), dtype) for blocks, dtype in outs],
        [SMEM] + [VMEM] * 4,
        [VMEM] * len(outs),
        "parts",
    )(where, mine, other, dz_t, dzo_t)


def choose_kernel(where, at_end, in_middle, out, sem):
    for flag, source in enumerate((at_end, in_middle)):
        pl.when(where[2] == flag)(pltpu.make_async_copy(source, out, sem).start)
    pltpu.make_async_copy(at_end, out, sem).wait()


def choose(where, at_end, in_middle):
    return call(
        choose_kernel,
        array(at_end.shape, at_end.dtype),
        [SMEM, ANY, ANY],
        VMEM,
        "choose",
        [pltpu.SemaphoreType.DMA],
    )(where, at_end, in_middle)


def join_kernel(one, two, out):
    rows = one.shape[0]
    out[0:rows, :] = one[...]
    out[rows : 2 * rows, :] = two[...]


def join(one, two):
    rows, cols = one.shape
    return call(join_kernel, array((2 * rows, cols), one.dtype), [VMEM, VMEM], VMEM, "join")(
        one, two
    )


def lay_kernel(where, *refs):
    own, far, (out_a, out_b, sems) = refs[0:4], refs[4:6], refs[6:]
    rows = out_a.shape[0]
    units = own[0].shape[1]
    copies = []
    for side in range(2):
        for k in range(4):
            block = 2 * (where[0] ^ k) + (where[1] ^ side)
            lanes = pl.ds(pl.multiple_of(block * units, units), units)
            source, start = (own[k], 0) if side == 0 else (far[k // 2], 2 * rows * (k % 2))
            for half, out in enumerate((out_a, out_b)):
                at = pl.ds(start + half * rows, rows)
                sem = sems.at[side * 8 + k * 2 + half]
                copies.append(pltpu.make_async_copy(source.at[at, :], out.at[:, lanes], sem))
    for copy in copies:
        copy.start()
    for copy in copies:
        copy.wait()


def lay_out(where, *sources):
    rows, units = sources[0].shape
    return call(
        lay_kernel,
        [array((rows // 2, 8 * units), jnp.bfloat16)] * 2,
        [SMEM] + [ANY] * 6,
        [VMEM] * 2,
        "lay_out",
        [pltpu.SemaphoreType.DMA((16,))],
    )(where, *sources)


def add_kernel(one, two, out):
    rows = out.shape[0]
    out[...] = low(wide(one[...]) + wide(two[0:rows, :]))


def add(one, two):
    return call(add_kernel, array(one.shape, jnp.bfloat16), [VMEM, VMEM], VMEM, "add")(one, two)


def finish_kernel(third_at, where, marks, group, kept, third, cross, last, out):
    second = group[...] == 1
    cols = out.shape[0]
    cross_at = cross.shape[0] - cols
    for chunk in range(cols // LANES):
        zero, one = marks_of(marks, where, cols, chunk)
        keep = wide(jnp.where(second, one, zero))
        at = chunk * LANES
        total = kept[at : at + LANES, :] + wide(last[at : at + LANES, :])
        total += wide(third[third_at + at : third_at + at + LANES, :])
        total += wide(cross[cross_at + at : cross_at + at + LANES, :])
        out[at : at + LANES, :] = low(total * keep)


def finish(third_at, where, marks, group, kept, third, cross, last):
    return call(
        functools.partial(finish_kernel, third_at * kept.shape[0]),
        array(kept.shape, jnp.bfloat16),
        [SMEM, SMEM] + [VMEM] * 5,
        VMEM,
        "finish",
    )(where, marks, group, kept, third, cross, last)


def pack_kernel(where, p0, p1, p2, p3, dz, sums, out, sems):
    rows, units = dz.shape
    cols = p0.shape[1]
    for q in range(4):
        block = out.at[q, pl.ds(0, rows), pl.ds(0, cols)]
        for index, piece in enumerate((p0, p1, p2, p3)):
            start = pltpu.make_async_copy(piece, block, sems.at[q]).start
            pl.when(where[0] ^ q == index)(start)
    extra = jnp.zeros((EXTRA, cols + units), jnp.bfloat16)
    for q in range(4):
        out[q, rows : rows + EXTRA, :] = extra
        out[q, 0:rows, cols : cols + units] = dz[...]
    for k in range(3):
        rest = sums[k : k + 1, :]
        for term in range(3):
            piece = low(rest)
            row = rows + 3 * k + term
            for q in range(4):
                out[q, row : row + 1, cols : cols + units] = piece
            rest = rest - wide(piece)
    for q in range(4):
        block = out.at[q, pl.ds(0, rows), pl.ds(0, cols)]
        pltpu.make_async_copy(p0, block, sems.at[q]).wait()


def pack(where, pieces, dz, sums):
    rows, units = dz.shape
    cols = pieces[0].shape[1]
    return call(
        pack_kernel,
        array((4, rows + EXTRA, cols + units), jnp.bfloat16),
        [SMEM] + [ANY] * 4 + [VMEM] * 2,
        VMEM,
        "pack",
        [pltpu.SemaphoreType.DMA((4,))],
    )(where, *pieces, dz, sums)


def weight_kernel(where, near, far, out, images, dzs, tiles, sems):
    rows, units = dzs.shape[1:]
    cols = images.shape[3]
    tile = tiles.shape[1]
    steps = cols // tile

    def fetch(q):
        source = near.at[q, pl.ds(0, rows), pl.ds(cols, units)]
        return pltpu.make_async_copy(source, dzs.at[q], sems.at[q])

    def block(source, p, q):
        image = source.at[q, pl.ds(0, rows), pl.ds(0, cols)]
        return pltpu.make_async_copy(image, images.at[p, q], sems.at[4 + 4 * p + q])

    def give(p, t):
        slot = p * steps + t
        return pltpu.make_async_copy(
            tiles.at[slot], out.at[pl.ds(slot * tile, tile), :], sems.at[12 + slot]
        )

    for q in range(4):
        fetch(q).start()
    for p in range(2):
        for q in range(4):
            pl.when(where[1] == p)(block(near, p, q).start)
            pl.when(where[1] != p)(block(far, p, q).start)
    for q in range(4):
        fetch(q).wait()
    for p in range(2):
        for q in range(4):
            block(near, p, q).wait()
        for t in range(steps):
            total = None
            for q in range(4):
                term = lax.dot_general(
                    images[p, q, :, t * tile : (t + 1) * tile],
                    dzs[q],
                    (((0,), (0,)), ((), ())),
                    preferred_element_type=jnp.float32,
                )
                total = term if total is None else total + term
            tiles[p * steps + t] = total
            give(p, t).start()
    for p in range(2):
        for t in range(steps):
            give(p, t).wait()


def weight_grad(rows, cols, where, near, far):
    units = near.shape[2] - cols
    tile = cols // 3
    return call(
        weight_kernel,
        array((2 * cols, units), jnp.float32),
        [SMEM, ANY, ANY],
        HBM,
        "weight_grad",
        [
            pltpu.VMEM((2, 4, rows, cols), jnp.bfloat16),
            pltpu.VMEM((4, rows, units), jnp.bfloat16),
            pltpu.VMEM((6, tile, units), jnp.float32),
            pltpu.SemaphoreType.DMA((18,)),
        ],
    )(where, near, far)


def sums_kernel(rows, cols, got_a, got_b, bias, stitch, terms, sems):
    units = bias.shape[1]
    copies = [
        pltpu.make_async_copy(
            got.at[:, pl.ds(rows, EXTRA), pl.ds(cols, units)], terms.at[side], sems.at[side]
        )
        for side, got in enumerate((got_a, got_b))
    ]
    for copy in copies:
        copy.start()
    for copy in copies:
        copy.wait()
    for side in range(2):
        totals = []
        for k in range(3):
            each = [
                (
                    wide(terms[side, q, 3 * k + 2 : 3 * k + 3, :])
                    + wide(terms[side, q, 3 * k + 1 : 3 * k + 2, :])
                )
                + wide(terms[side, q, 3 * k : 3 * k + 1, :])
                for q in range(4)
            ]
            totals.append((each[0] + each[1]) + (each[2] + each[3]))
        bias[side : side + 1, :] = totals[0]
        stitch[side : side + 1, :] = totals[1]
        stitch[2 + side : 3 + side, :] = totals[2]


def total_sums(rows, cols, got_a, got_b):
    units = got_a.shape[2] - cols
    return call(
        functools.partial(sums_kernel, rows, cols),
        [array((2, units), jnp.float32), array((4, units), jnp.float32)],
        [ANY, ANY],
        [VMEM, VMEM],
        "total_sums",
        [pltpu.VMEM((2, 4, EXTRA, units), jnp.bfloat16), pltpu.SemaphoreType.DMA((2,))],
    )(got_a, got_b)


def swap(x):
    return lax.ppermute(x, "mp", SWAP_CORE)


def along(x):
    return lax.ppermute(x, "mp", NEAR_Z)


def across(x):
    return lax.ppermute(x, "mp", FAR_Z)


def inward(x):
    return lax.ppermute(x, "mp", ENDS_IN)


def between(x):
    return lax.ppermute(x, "mp", MIDS)


def outward(x):
    return lax.ppermute(x, "mp", ENDS_OUT)


def exchange(x):
    return lax.all_to_all(x, "dp", 0, 0)


def fast_shards(
    image_a,
    image_b,
    image_group,
    position_mask,
    weight_a,
    weight_b,
    tower_bias,
    stitch,
    cotan_a,
    cotan_b,
):
    rows, cols = image_a.shape
    units = weight_a.shape[1]
    place = lax.axis_index("mp").astype(jnp.int32)
    z = place // 2
    core = place % 2
    quarter = lax.axis_index("dp").astype(jnp.int32)
    middle = ((z == 1) | (z == 2)).astype(jnp.int32)
    slots = jnp.take(jnp.asarray(SLOTS, jnp.int32), z, axis=0) ^ z
    where = jnp.concatenate(
        [jnp.stack([z, core, middle]), slots, jnp.stack([quarter, place])]
    ).astype(jnp.int32)
    group = image_group[None, :]
    line.token = None
    bf16, f32 = jnp.bfloat16, jnp.float32
    send, wait = line.send, line.wait

    whole_a = swap(weight_a)
    whole_b = swap(weight_b)
    a0 = mask_image(where, position_mask, group, image_a)
    a2 = send(across, a0)
    a1 = send(along, a0)
    b0 = mask_image(where, position_mask, group, image_b)
    mine_a = load(where, weight_a)
    mine_b = load(where, weight_b)
    a1, a2 = wait(a1, a2)
    a3 = send(along, a2)
    b_mid = send(between, b0)
    b1 = send(along, b0)
    whole_a, whole_b = wait(whole_a, whole_b)
    other_a = load(where, whole_a)
    other_b = load(where, whole_b)
    keep_a, give_a = forward_open(a0, a1, a2, mine_a, other_a)
    a3 = wait(a3)
    own_a, sent_a = forward_close(a3, mine_a, other_a, keep_a, give_a)
    got_sum = wait(send(swap, sent_a))
    dz_a, dzt_a, sums_a, hidden_a = tower(
        first_kernel,
        "tower_a",
        array((rows, units), f32),
        own_a,
        got_sum,
        tower_bias,
        stitch,
        cotan_a,
        cotan_b,
    )
    dzo_a = send(swap, dzt_a)
    b1, b_mid = wait(b1, b_mid)
    got_a = send(exchange, pack(where, (a0, a1, a2, a3), dz_a, sums_a))
    b_end = send(outward, b_mid)
    b_mid2 = send(between, b1)
    dzo_a = wait(dzo_a)
    first_a, second_a, third_a, kept_a = parts(
        ((0, 0, 0), (1, 1, 0), (2, 2, 0), (3, 3, 0)),
        [(1, bf16), (1, bf16), (1, bf16), (1, f32)],
        where,
        mine_a,
        other_a,
        dzt_a,
        dzo_a,
    )
    in1_a = send(inward, first_a)
    in2_a = send(inward, second_a)
    b_end, b_mid2 = wait(b_end, b_mid2)
    b_end2 = send(outward, b_mid2)
    b2 = choose(where, b_end, b_mid2)
    keep_b, give_b = forward_open(b0, b1, b2, mine_b, other_b)
    in1_a = wait(in1_a)
    cross1_a = send(between, add(first_a, in1_a))
    b_end2 = wait(b_end2)
    b3 = choose(where, b_end2, b_mid)
    own_b, sent_b = forward_close(b3, mine_b, other_b, keep_b, give_b)
    got_sum = send(swap, sent_b)
    in2_a = wait(in2_a)
    sum2_a = add(second_a, in2_a)
    got_sum = wait(got_sum)
    dz_b, dzt_b, sums_b, local = tower(
        second_kernel,
        "tower_b",
        array((2 * rows, units), bf16),
        own_b,
        got_sum,
        hidden_a,
        tower_bias,
        stitch,
        cotan_a,
        cotan_b,
    )
    dzo_b = send(swap, dzt_b)
    cross1_a = wait(cross1_a)
    sum3_a = add(third_a, cross1_a)
    got_a = wait(got_a)
    far_a = send(swap, got_a)
    got_b = send(exchange, pack(where, (b0, b1, b2, b3), dz_b, sums_b))
    dzo_b, far_a = wait(dzo_b, far_a)
    (first_b,) = parts(((0, 0, 0),), [(1, bf16)], where, mine_b, other_b, dzt_b, dzo_b)
    in1_b = send(inward, first_b)
    s1 = send(along, local)
    s_mid = send(between, local)
    cross2_a = send(between, sum2_a)
    out_a = send(outward, sum3_a)
    second_b, third_b, kept_b = parts(
        ((1, 0, 0), (2, 1, 0), (3, 2, 0)),
        [(1, bf16), (1, bf16), (1, f32)],
        where,
        mine_b,
        other_b,
        dzt_b,
        dzo_b,
    )
    in2_b = send(inward, second_b)
    grad_weight_a = weight_grad(rows, cols, where, got_a, far_a)
    in1_b = wait(in1_b)
    cross1_b = send(between, add(first_b, in1_b))
    s1, s_mid = wait(s1, s_mid)
    s_end = send(outward, s_mid)
    s_mid2 = send(between, s1)
    in2_b = wait(in2_b)
    cross2_b = send(between, add(second_b, in2_b))
    cross1_b = wait(cross1_b)
    out_b = send(outward, add(third_b, cross1_b))
    s_end, s_mid2 = wait(s_end, s_mid2)
    s_end2 = send(outward, s_mid2)
    in3_a = send(inward, third_a)
    s2 = choose(where, s_end, s_mid2)
    in3_b = send(inward, third_b)
    cross2_a, out_a = wait(cross2_a, out_a)
    cross2_b, out_b = wait(cross2_b, out_b)
    s_end2, in3_a = wait(s_end2, in3_a)
    s3 = choose(where, s_end2, s_mid)
    grad_image_a = finish(0, where, position_mask, group, kept_a, in3_a, cross2_a, out_a)
    got_b, in3_b = wait(got_b, in3_b)
    far_b = send(swap, got_b)
    far_high = send(swap, join(s2, s3))
    far_low = send(swap, join(local, s1))
    grad_bias, grad_stitch = total_sums(rows, cols, got_a, got_b)
    grad_image_b = finish(0, where, position_mask, group, kept_b, in3_b, cross2_b, out_b)
    stitched_a, stitched_b = lay_out(where, local, s1, s2, s3, far_low, far_high)
    grad_weight_b = weight_grad(rows, cols, where, got_b, far_b)
    return (
        stitched_a,
        stitched_b,
        grad_image_a,
        grad_image_b,
        grad_weight_a,
        grad_weight_b,
        grad_bias,
        grad_stitch,
    )


def solution(mesh):
    placed = (
        P("dp", "mp"),
        P("dp", "mp"),
        P("dp"),
        P(),
        P(None, "mp"),
        P(None, "mp"),
        P(None, "mp"),
        P(None, "mp"),
        P("dp", "mp"),
        P("dp", "mp"),
    )
    fits = mesh.shape["dp"] == 4 and mesh.shape["mp"] == 8
    return jax.shard_map(
        fast_shards if fits else general_shards,
        mesh=mesh,
        in_specs=placed,
        out_specs=(
            P("dp", None),
            P("dp", None),
            P("mp", "dp"),
            P("mp", "dp"),
            P("dp", "mp"),
            P("dp", "mp"),
            P(None, "mp"),
            P(None, "mp"),
        ),
        check_vma=False,
    )
```

```python
import functools

import jax
import jax.numpy as jnp
from jax import lax
from jax.experimental import pallas as pl
from jax.experimental.pallas import tpu as pltpu
from jax.sharding import PartitionSpec as P

CH = 256
POS = 36


def keep_block(image_group, position_mask, first_col, cols):
    positions = (first_col + lax.iota(jnp.int32, cols)) // CH
    onehot = (positions[:, None] == lax.iota(jnp.int32, POS)[None, :]).astype(jnp.float32)
    per_position = jnp.dot(onehot, position_mask.astype(jnp.float32).T)
    return jnp.where(
        image_group[:, None] == 1, per_position[:, 1][None, :], per_position[:, 0][None, :]
    )


def general_shards(
    image_a,
    image_b,
    image_group,
    position_mask,
    weight_a,
    weight_b,
    tower_bias,
    stitch,
    cotan_a,
    cotan_b,
):
    batch_rows = image_a.shape[0]
    shard_cols = image_a.shape[1]
    first_col = lax.axis_index("mp") * shard_cols
    keep_mask = keep_block(image_group, position_mask, first_col, shard_cols)
    keep_low = keep_mask.astype(jnp.bfloat16)
    contract_rows = (((0,), (0,)), ((), ()))
    contract_units = (((1,), (1,)), ((), ()))
    full_a = lax.all_gather(image_a * keep_low, "mp", axis=1, tiled=True)
    full_b = lax.all_gather(image_b * keep_low, "mp", axis=1, tiled=True)
    pre_a = jnp.dot(full_a, weight_a, preferred_element_type=jnp.float32) + tower_bias[0][None, :]
    pre_b = jnp.dot(full_b, weight_b, preferred_element_type=jnp.float32) + tower_bias[1][None, :]
    sigma_a = jax.nn.sigmoid(pre_a)
    sigma_b = jax.nn.sigmoid(pre_b)
    hidden_a = pre_a * sigma_a
    hidden_b = pre_b * sigma_b
    local_a = (stitch[0][None, :] * hidden_a + stitch[1][None, :] * hidden_b).astype(jnp.bfloat16)
    local_b = (stitch[2][None, :] * hidden_a + stitch[3][None, :] * hidden_b).astype(jnp.bfloat16)
    stitched_a = lax.all_gather(local_a, "mp", axis=1, tiled=True)
    stitched_b = lax.all_gather(local_b, "mp", axis=1, tiled=True)
    upper_a = cotan_a.astype(jnp.float32)
    upper_b = cotan_b.astype(jnp.float32)
    dhid_a = stitch[0][None, :] * upper_a + stitch[2][None, :] * upper_b
    dhid_b = stitch[1][None, :] * upper_a + stitch[3][None, :] * upper_b
    dpre_a = dhid_a * (sigma_a * (1.0 + pre_a * (1.0 - sigma_a)))
    dpre_b = dhid_b * (sigma_b * (1.0 + pre_b * (1.0 - sigma_b)))
    bias_terms = jnp.stack([jnp.sum(dpre_a, axis=0), jnp.sum(dpre_b, axis=0)])
    stitch_terms = jnp.stack(
        [
            jnp.sum(upper_a * hidden_a, axis=0),
            jnp.sum(upper_a * hidden_b, axis=0),
            jnp.sum(upper_b * hidden_a, axis=0),
            jnp.sum(upper_b * hidden_b, axis=0),
        ]
    )
    grad_bias, grad_stitch = lax.psum((bias_terms, stitch_terms), "dp")
    dlow_a = dpre_a.astype(jnp.bfloat16)
    dlow_b = dpre_b.astype(jnp.bfloat16)
    block_a = lax.dot_general(full_a, dlow_a, contract_rows, preferred_element_type=jnp.float32)
    block_b = lax.dot_general(full_b, dlow_b, contract_rows, preferred_element_type=jnp.float32)
    grad_weight_a = lax.psum_scatter(block_a, "dp", scatter_dimension=0, tiled=True)
    grad_weight_b = lax.psum_scatter(block_b, "dp", scatter_dimension=0, tiled=True)
    part_a = lax.dot_general(weight_a, dlow_a, contract_units, preferred_element_type=jnp.float32)
    part_b = lax.dot_general(weight_b, dlow_b, contract_units, preferred_element_type=jnp.float32)
    summed = lax.psum_scatter(
        jnp.concatenate([part_a, part_b], axis=1), "mp", scatter_dimension=0, tiled=True
    )
    keep_cols = keep_mask.T
    grad_image_a = (summed[:, :batch_rows] * keep_cols).astype(jnp.bfloat16)
    grad_image_b = (summed[:, batch_rows:] * keep_cols).astype(jnp.bfloat16)
    return (
        stitched_a,
        stitched_b,
        grad_image_a,
        grad_image_b,
        grad_weight_a,
        grad_weight_b,
        grad_bias,
        grad_stitch,
    )


SWAP_CORE = [(d, d ^ 1) for d in range(8)]
NEAR_Z = [(d, d ^ 2) for d in range(8)]
FAR_Z = [(d, d ^ 4) for d in range(8)]
ENDS_IN = [(0, 2), (1, 3), (6, 4), (7, 5)]
MIDS = [(2, 4), (3, 5), (4, 2), (5, 3)]
ENDS_OUT = [(2, 0), (3, 1), (4, 6), (5, 7)]
SLOTS = ((3, 2, 1, 0), (3, 2, 0, 1), (0, 1, 3, 2), (0, 1, 2, 3))
LANES = 128
EXTRA = 16
VMEM_LIMIT = 22 * 1024 * 1024
SMEM = pl.BlockSpec(memory_space=pltpu.SMEM)
VMEM = pl.BlockSpec(memory_space=pltpu.VMEM)
HBM = pl.BlockSpec(memory_space=pltpu.HBM)
ANY = pl.BlockSpec(memory_space=pl.ANY)
LITTLE = pl.CostEstimate(flops=1, bytes_accessed=1, transcendentals=0)


def low(x):
    return x.astype(jnp.bfloat16)


def wide(x):
    return x.astype(jnp.float32)


def array(shape, dtype):
    return jax.ShapeDtypeStruct(shape, dtype)


class Line:
    def __init__(self):
        self.token = None

    def tie(self, *xs):
        if self.token is None:
            return xs
        *xs, self.token = lax.optimization_barrier((*xs, self.token))
        return xs

    def wait(self, *arrived):
        arrived = self.tie(*arrived)
        return arrived if len(arrived) > 1 else arrived[0]

    def send(self, move, x):
        return move(*self.tie(x))


line = Line()


def call(kernel, out_shape, in_specs, out_specs, name, scratch=(), aliases={}):
    single = not isinstance(out_shape, list)
    outs = [out_shape] if single else out_shape
    places = [out_specs] if single else out_specs
    n_in, n_out = len(in_specs), len(outs)
    before = () if line.token is None else (line.token,)

    def body(*refs):
        start = n_in + len(before)
        refs[start + n_out][...] = jnp.zeros((8, LANES), jnp.float32)
        kernel(*refs[:n_in], *refs[start : start + n_out], *refs[start + n_out + 1 :])

    run = pl.pallas_call(
        body,
        out_shape=[*outs, array((8, LANES), jnp.float32)],
        in_specs=[*in_specs, *[HBM] * len(before)],
        out_specs=[*places, VMEM],
        scratch_shapes=scratch,
        input_output_aliases=aliases,
        compiler_params=pltpu.CompilerParams(vmem_limit_bytes=VMEM_LIMIT),
        cost_estimate=LITTLE,
        name=name,
    )

    def go(*operands):
        *results, line.token = run(*operands, *before)
        return results[0] if single else results

    return go


def marks_of(marks, where, cols, chunk):
    position = (where[8] * cols + chunk * LANES) // CH
    return marks[0, position], marks[1, position]


def mask_kernel(where, marks, group, image, out):
    rows, cols = image.shape
    second = jnp.broadcast_to(jnp.where(group[...] == 1, 1.0, 0.0), (8, rows)).T[:, 0:1] > 0.5
    for chunk in range(cols // LANES):
        zero, one = marks_of(marks, where, cols, chunk)
        keep = wide(jnp.where(second, one, zero))
        lanes = slice(chunk * LANES, (chunk + 1) * LANES)
        out[:, lanes] = low(wide(image[:, lanes]) * keep)


def mask_image(where, marks, group, image):
    return call(
        mask_kernel, array(image.shape, jnp.bfloat16), [SMEM, SMEM, VMEM, VMEM], VMEM, "mask_image"
    )(where, marks, group, image)


def in_hbm(x):
    return pltpu.with_memory_space_constraint(x, pltpu.HBM)


def dot(x, y):
    return jnp.dot(x, y, preferred_element_type=jnp.float32)


def products(where, ks, mine, other, held, sems, emit):
    cols = held.shape[2]

    def copies(i):
        block = 2 * (where[0] ^ ks[i]) + where[1]
        rows = pl.ds(pl.multiple_of(block * cols, cols), cols)
        return [
            pltpu.make_async_copy(weight.at[rows, :], held.at[i, side], sems.at[i, side])
            for side, weight in enumerate((mine, other))
        ]

    for i in range(len(ks)):
        for copy in copies(i):
            copy.start()
    for i in range(len(ks)):
        for copy in copies(i):
            copy.wait()
        emit(i, held[i, 0], held[i, 1])


def open_kernel(where, p0, p1, p2, mine, other, keep, send, last, slot, held, sems):
    pieces = (p0, p1, p2)
    cols = p0.shape[1]
    ahead = []
    for at, (k, out) in enumerate(((3, last), (where[3], slot))):
        block = 2 * (where[0] ^ k) + where[1]
        rows = pl.ds(pl.multiple_of(block * cols, cols), cols)
        for side, weight in enumerate((mine, other)):
            ahead.append(
                pltpu.make_async_copy(weight.at[rows, :], out.at[side], sems.at[3 + at, side])
            )

    def emit(i, own_block, other_block):
        if i == 0:
            for copy in ahead:
                copy.start()
            keep[...] = dot(p0[...], own_block)
            send[...] = dot(p0[...], other_block)
        else:
            keep[...] += dot(pieces[i][...], own_block)
            send[...] += dot(pieces[i][...], other_block)

    products(where, (0, 1, 2), mine, other, held, sems, emit)
    for copy in ahead:
        copy.wait()


def forward_open(where, p0, p1, p2, mine, other):
    rows, cols = p0.shape
    units = mine.shape[1]
    blocks = pltpu.VMEM((2, cols, units), jnp.bfloat16)
    return call(
        open_kernel,
        [array((rows, units), jnp.float32)] * 2 + [blocks] * 2,
        [SMEM] + [VMEM] * 3 + [HBM] * 2,
        [VMEM] * 4,
        "forward_open",
        [pltpu.VMEM((3, 2, cols, units), jnp.bfloat16), pltpu.SemaphoreType.DMA((5, 2))],
    )(where, p0, p1, p2, in_hbm(mine), in_hbm(other))


def close_kernel(p3, weights, keep, send, out, sent):
    sent[...] = send[...] + dot(p3[...], weights[1])
    out[...] = keep[...] + dot(p3[...], weights[0])


def forward_close(p3, weights, keep, send):
    return call(
        close_kernel,
        [array(keep.shape, jnp.float32)] * 2,
        [VMEM] * 4,
        [VMEM] * 2,
        "forward_close",
    )(p3, weights, keep, send)


def slot_kernel(weights, dz_t, dzo_t, out):
    out[...] = low(dot(weights[0], dz_t[...]) + dot(weights[1], dzo_t[...]))


def first_slot(weights, dz_t, dzo_t):
    return call(
        slot_kernel,
        array((weights.shape[1], dz_t.shape[1]), jnp.bfloat16),
        [VMEM] * 3,
        VMEM,
        "first_slot",
    )(weights, dz_t, dzo_t)


def tower_math(pre, bias, unit_a, unit_b, upper_a, upper_b, dz, dz_t, sums):
    pre = pre + bias[...]
    sigma = jax.nn.sigmoid(pre)
    hidden = pre * sigma
    cot_a = wide(upper_a[...])
    cot_b = wide(upper_b[...])
    dhid = unit_a[...] * cot_a + unit_b[...] * cot_b
    dpre = dhid * (sigma * (1.0 + pre * (1.0 - sigma)))
    dz[...] = low(dpre)
    dz_t[...] = low(dpre).T
    sums[0:1, :] = jnp.sum(dpre, axis=0, keepdims=True)
    sums[1:2, :] = jnp.sum(cot_a * hidden, axis=0, keepdims=True)
    sums[2:3, :] = jnp.sum(cot_b * hidden, axis=0, keepdims=True)
    sums[3:4, :] = jnp.zeros_like(sums[3:4, :])
    return hidden


def first_kernel(own, got, bias, stitch, upper_a, upper_b, dz, dz_t, sums, hidden):
    hidden[...] = tower_math(
        own[...] + got[...],
        bias[0:1, :],
        stitch[0:1, :],
        stitch[2:3, :],
        upper_a,
        upper_b,
        dz,
        dz_t,
        sums,
    )


def second_kernel(own, got, earlier, bias, stitch, upper_a, upper_b, dz, dz_t, sums, local):
    hidden = tower_math(
        own[...] + got[...],
        bias[1:2, :],
        stitch[1:2, :],
        stitch[3:4, :],
        upper_a,
        upper_b,
        dz,
        dz_t,
        sums,
    )
    rows = hidden.shape[0]
    before = earlier[...]
    local[0:rows, :] = low(stitch[0:1, :] * before + stitch[1:2, :] * hidden)
    local[rows : 2 * rows, :] = low(stitch[2:3, :] * before + stitch[3:4, :] * hidden)


def tower(kernel, name, last, *operands):
    rows, units = operands[0].shape
    return call(
        kernel,
        [
            array((rows, units), jnp.bfloat16),
            array((units, rows), jnp.bfloat16),
            array((4, units), jnp.float32),
            last,
        ],
        [VMEM] * len(operands),
        [VMEM] * 4,
        name,
    )(*operands)


def part_kernel(slots, where, mine, other, dz_t, dzo_t, *refs):
    *outs, held, sems = refs
    cols = held.shape[2]

    def emit(i, own_block, other_block):
        _, at, block = slots[i]
        total = dot(own_block, dz_t[...]) + dot(other_block, dzo_t[...])
        outs[at][block * cols : (block + 1) * cols, :] = total.astype(outs[at].dtype)

    products(where, [where[3 + slot] for slot, _, _ in slots], mine, other, held, sems, emit)


def parts(slots, outs, where, mine, other, dz_t, dzo_t):
    units, rows = dz_t.shape
    cols = mine.shape[0] // 8
    return call(
        functools.partial(part_kernel, slots),
        [array((blocks * cols, rows), dtype) for blocks, dtype in outs],
        [SMEM, HBM, HBM, VMEM, VMEM],
        [VMEM] * len(outs),
        "parts",
        [
            pltpu.VMEM((len(slots), 2, cols, units), jnp.bfloat16),
            pltpu.SemaphoreType.DMA((len(slots), 2)),
        ],
    )(where, in_hbm(mine), in_hbm(other), dz_t, dzo_t)


def choose_kernel(where, at_end, in_middle, out, sem):
    for flag, source in enumerate((at_end, in_middle)):
        pl.when(where[2] == flag)(pltpu.make_async_copy(source, out, sem).start)
    pltpu.make_async_copy(at_end, out, sem).wait()


def choose(where, at_end, in_middle):
    return call(
        choose_kernel,
        array(at_end.shape, at_end.dtype),
        [SMEM, ANY, ANY],
        VMEM,
        "choose",
        [pltpu.SemaphoreType.DMA],
    )(where, at_end, in_middle)


def join_kernel(one, two, out):
    rows = one.shape[0]
    out[0:rows, :] = one[...]
    out[rows : 2 * rows, :] = two[...]


def join(one, two):
    rows, cols = one.shape
    return call(join_kernel, array((2 * rows, cols), one.dtype), [VMEM, VMEM], VMEM, "join")(
        one, two
    )


def lay_kernel(where, *refs):
    own, far, (out_a, out_b, sems) = refs[0:4], refs[4:6], refs[6:]
    rows = out_a.shape[0]
    units = own[0].shape[1]
    copies = []
    for side in range(2):
        for k in range(4):
            block = 2 * (where[0] ^ k) + (where[1] ^ side)
            lanes = pl.ds(pl.multiple_of(block * units, units), units)
            source, start = (own[k], 0) if side == 0 else (far[k // 2], 2 * rows * (k % 2))
            for half, out in enumerate((out_a, out_b)):
                at = pl.ds(start + half * rows, rows)
                sem = sems.at[side * 8 + k * 2 + half]
                copies.append(pltpu.make_async_copy(source.at[at, :], out.at[:, lanes], sem))
    for copy in copies:
        copy.start()
    for copy in copies:
        copy.wait()


def lay_out(where, *sources):
    rows, units = sources[0].shape
    return call(
        lay_kernel,
        [array((rows // 2, 8 * units), jnp.bfloat16)] * 2,
        [SMEM] + [ANY] * 6,
        [VMEM] * 2,
        "lay_out",
        [pltpu.SemaphoreType.DMA((16,))],
    )(where, *sources)


def add_kernel(at, one, two, out):
    rows = out.shape[0]
    out[...] = low(wide(one[at : at + rows, :]) + wide(two[0:rows, :]))


def add(one, two, block=0, rows=None):
    rows = rows or min(one.shape[0], two.shape[0])
    return call(
        functools.partial(add_kernel, block * rows),
        array((rows, one.shape[1]), jnp.bfloat16),
        [VMEM, VMEM],
        VMEM,
        "add",
    )(one, two)


def finish_kernel(where, marks, group, kept, third, cross, last, out, held, own, sems):
    second = group[...] == 1
    cols = out.shape[0]
    copies = [pltpu.make_async_copy(kept, own, sems.at[3])]
    for n, source in enumerate((third, cross, last)):
        copies.append(pltpu.make_async_copy(source, held.at[n], sems.at[n]))
    for copy in copies:
        copy.start()
    for copy in copies:
        copy.wait()
    for chunk in range(cols // LANES):
        zero, one = marks_of(marks, where, cols, chunk)
        keep = wide(jnp.where(second, one, zero))
        rows = slice(chunk * LANES, (chunk + 1) * LANES)
        total = own[rows, :] + wide(held[0, rows, :])
        total += wide(held[1, rows, :]) + wide(held[2, rows, :])
        out[rows, :] = low(total * keep)


def finish(where, marks, group, kept, third, cross, last):
    return call(
        finish_kernel,
        array(kept.shape, jnp.bfloat16),
        [SMEM, SMEM, VMEM] + [HBM] * 4,
        VMEM,
        "finish",
        [
            pltpu.VMEM((3, *kept.shape), jnp.bfloat16),
            pltpu.VMEM(kept.shape, jnp.float32),
            pltpu.SemaphoreType.DMA((4,)),
        ],
    )(where, marks, group, *[in_hbm(x) for x in (kept, third, cross, last)])


def pack_kernel(where, p0, p1, p2, p3, dz, sums, given, out, sems):
    rows, units = dz.shape
    cols = p0.shape[1]
    for q in range(4):
        block = out.at[q, pl.ds(0, rows), pl.ds(0, cols)]
        for index, piece in enumerate((p0, p1, p2, p3)):
            start = pltpu.make_async_copy(piece, block, sems.at[q]).start
            pl.when(where[0] ^ q == index)(start)
    extra = jnp.zeros((EXTRA, cols + units), jnp.bfloat16)
    for q in range(4):
        out[q, rows : rows + EXTRA, :] = extra
        out[q, 0:rows, cols : cols + units] = dz[...]
    for k in range(3):
        rest = sums[k : k + 1, :]
        for term in range(3):
            piece = low(rest)
            row = rows + 3 * k + term
            for q in range(4):
                out[q, row : row + 1, cols : cols + units] = piece
            rest = rest - wide(piece)
    gives = [pltpu.make_async_copy(out.at[q], given.at[q], sems.at[4 + q]) for q in range(4)]
    for q in range(4):
        block = out.at[q, pl.ds(0, rows), pl.ds(0, cols)]
        pltpu.make_async_copy(p0, block, sems.at[q]).wait()
        gives[q].start()
    for give in gives:
        give.wait()


def pack(where, pieces, dz, sums):
    rows, units = dz.shape
    cols = pieces[0].shape[1]
    return call(
        pack_kernel,
        pltpu.HBM((4, rows + EXTRA, cols + units), jnp.bfloat16),
        [SMEM] + [ANY] * 4 + [VMEM] * 2,
        HBM,
        "pack",
        [
            pltpu.VMEM((4, rows + EXTRA, cols + units), jnp.bfloat16),
            pltpu.SemaphoreType.DMA((8,)),
        ],
    )(where, *pieces, dz, sums)


def weight_kernel(sides, where, *refs):
    n = len(sides)
    images_of, dz_of = refs[:n], refs[n]
    before, (out, images, dzs, tiles, sems) = refs[n + 1 : -5], refs[-5:]
    rows, units = dzs.shape[1:]
    cols = images.shape[3]
    tile = tiles.shape[1]
    steps = cols // tile

    def fetch(q):
        source = dz_of.at[q, pl.ds(0, rows), pl.ds(cols, units)]
        return pltpu.make_async_copy(source, dzs.at[q], sems.at[q])

    def block(i, q):
        image = images_of[i].at[q, pl.ds(0, rows), pl.ds(0, cols)]
        return pltpu.make_async_copy(image, images.at[i, q], sems.at[4 + 4 * i + q])

    def give(i, t):
        at = pl.multiple_of((where[1] ^ sides[i]) * cols + t * tile, tile)
        slot = i * steps + t
        return pltpu.make_async_copy(
            tiles.at[slot], out.at[pl.ds(at, tile), :], sems.at[12 + slot]
        )

    for q in range(4):
        fetch(q).start()
    for i in range(n):
        for q in range(4):
            block(i, q).start()
    for q in range(4):
        fetch(q).wait()
    for i in range(n):
        for q in range(4):
            block(i, q).wait()
        for t in range(steps):
            total = None
            for q in range(4):
                term = lax.dot_general(
                    images[i, q, :, t * tile : (t + 1) * tile],
                    dzs[q],
                    (((0,), (0,)), ((), ())),
                    preferred_element_type=jnp.float32,
                )
                total = term if total is None else total + term
            tiles[i * steps + t] = total
            give(i, t).start()
    for i in range(n):
        for t in range(steps):
            give(i, t).wait()


def weight_grad(sides, rows, cols, where, images, dz, *before):
    units = dz.shape[2] - cols
    tile = cols // 3
    n = len(sides)
    return call(
        functools.partial(weight_kernel, sides),
        pltpu.HBM((2 * cols, units), jnp.float32),
        [SMEM] + [ANY] * (n + 1) + [HBM] * len(before),
        HBM,
        "weight_grad",
        [
            pltpu.VMEM((n, 4, rows, cols), jnp.bfloat16),
            pltpu.VMEM((4, rows, units), jnp.bfloat16),
            pltpu.VMEM((3 * n, tile, units), jnp.float32),
            pltpu.SemaphoreType.DMA((18,)),
        ],
        {n + 2: 0} if before else {},
    )(where, *images, dz, *before)


def sums_kernel(rows, cols, got_a, got_b, bias, stitch, terms, sems):
    units = bias.shape[1]
    copies = [
        pltpu.make_async_copy(
            got.at[:, pl.ds(rows, EXTRA), pl.ds(cols, units)], terms.at[side], sems.at[side]
        )
        for side, got in enumerate((got_a, got_b))
    ]
    for copy in copies:
        copy.start()
    for copy in copies:
        copy.wait()
    for side in range(2):
        totals = []
        for k in range(3):
            each = [
                (
                    wide(terms[side, q, 3 * k + 2 : 3 * k + 3, :])
                    + wide(terms[side, q, 3 * k + 1 : 3 * k + 2, :])
                )
                + wide(terms[side, q, 3 * k : 3 * k + 1, :])
                for q in range(4)
            ]
            totals.append((each[0] + each[1]) + (each[2] + each[3]))
        bias[side : side + 1, :] = totals[0]
        stitch[side : side + 1, :] = totals[1]
        stitch[2 + side : 3 + side, :] = totals[2]


def total_sums(rows, cols, got_a, got_b):
    units = got_a.shape[2] - cols
    return call(
        functools.partial(sums_kernel, rows, cols),
        [array((2, units), jnp.float32), array((4, units), jnp.float32)],
        [ANY, ANY],
        [VMEM, VMEM],
        "total_sums",
        [pltpu.VMEM((2, 4, EXTRA, units), jnp.bfloat16), pltpu.SemaphoreType.DMA((2,))],
    )(got_a, got_b)


def swap(x):
    return lax.ppermute(x, "mp", SWAP_CORE)


def along(x):
    return lax.ppermute(x, "mp", NEAR_Z)


def across(x):
    return lax.ppermute(x, "mp", FAR_Z)


def inward(x):
    return lax.ppermute(x, "mp", ENDS_IN)


def between(x):
    return lax.ppermute(x, "mp", MIDS)


def outward(x):
    return lax.ppermute(x, "mp", ENDS_OUT)


def exchange(x):
    return lax.all_to_all(x, "dp", 0, 0)


def fast_shards(
    image_a,
    image_b,
    image_group,
    position_mask,
    weight_a,
    weight_b,
    tower_bias,
    stitch,
    cotan_a,
    cotan_b,
):
    rows, cols = image_a.shape
    units = weight_a.shape[1]
    place = lax.axis_index("mp").astype(jnp.int32)
    z = place // 2
    core = place % 2
    quarter = lax.axis_index("dp").astype(jnp.int32)
    middle = ((z == 1) | (z == 2)).astype(jnp.int32)
    slots = jnp.take(jnp.asarray(SLOTS, jnp.int32), z, axis=0) ^ z
    where = jnp.concatenate(
        [jnp.stack([z, core, middle]), slots, jnp.stack([quarter, place])]
    ).astype(jnp.int32)
    group = image_group[None, :]
    line.token = None
    bf16, f32 = jnp.bfloat16, jnp.float32
    send, wait = line.send, line.wait

    whole_a = swap(weight_a)
    whole_b = swap(weight_b)
    a0 = mask_image(where, position_mask, group, image_a)
    a2 = send(across, a0)
    a1 = send(along, a0)
    b0 = mask_image(where, position_mask, group, image_b)
    a1, a2 = wait(a1, a2)
    a3 = send(along, a2)
    b_mid = send(between, b0)
    b1 = send(along, b0)
    whole_a, whole_b = wait(whole_a, whole_b)
    keep_a, give_a, last_a, slot_a = forward_open(where, a0, a1, a2, weight_a, whole_a)
    a3 = wait(a3)
    own_a, sent_a = forward_close(a3, last_a, keep_a, give_a)
    got_sum = wait(send(swap, sent_a))
    dz_a, dzt_a, sums_a, hidden_a = tower(
        first_kernel,
        "tower_a",
        array((rows, units), f32),
        own_a,
        got_sum,
        tower_bias,
        stitch,
        cotan_a,
        cotan_b,
    )
    dzo_a = send(swap, dzt_a)
    packed_a = pack(where, (a0, a1, a2, a3), dz_a, sums_a)
    b1, b_mid = wait(b1, b_mid)
    got_a = send(exchange, packed_a)
    b_end = send(outward, b_mid)
    b_mid2 = send(between, b1)
    dzo_a = wait(dzo_a)
    first_a = first_slot(slot_a, dzt_a, dzo_a)
    in1_a = send(inward, first_a)
    second_a, third_a, kept_a = parts(
        ((1, 0, 0), (2, 1, 0), (3, 2, 0)),
        [(1, bf16), (1, bf16), (1, f32)],
        where,
        weight_a,
        whole_a,
        dzt_a,
        dzo_a,
    )
    in2_a = send(inward, second_a)
    b_end, b_mid2 = wait(b_end, b_mid2)
    b_end2 = send(outward, b_mid2)
    b2 = choose(where, b_end, b_mid2)
    keep_b, give_b, last_b, slot_b = forward_open(where, b0, b1, b2, weight_b, whole_b)
    in1_a = wait(in1_a)
    cross1_a = send(between, add(first_a, in1_a))
    b_end2 = wait(b_end2)
    b3 = choose(where, b_end2, b_mid)
    own_b, sent_b = forward_close(b3, last_b, keep_b, give_b)
    got_sum = send(swap, sent_b)
    in2_a = wait(in2_a)
    sum2_a = add(second_a, in2_a)
    got_sum = wait(got_sum)
    dz_b, dzt_b, sums_b, local = tower(
        second_kernel,
        "tower_b",
        array((2 * rows, units), bf16),
        own_b,
        got_sum,
        hidden_a,
        tower_bias,
        stitch,
        cotan_a,
        cotan_b,
    )
    dzo_b = send(swap, dzt_b)
    packed_b = pack(where, (b0, b1, b2, b3), dz_b, sums_b)
    cross1_a = wait(cross1_a)
    sum3_a = add(third_a, cross1_a)
    got_a = wait(got_a)
    far_a = send(swap, got_a)
    got_b = send(exchange, packed_b)
    cross2_a = send(between, sum2_a)
    dzo_b, far_a = wait(dzo_b, far_a)
    first_b = first_slot(slot_b, dzt_b, dzo_b)
    in1_b = send(inward, first_b)
    s1 = send(along, local)
    s_mid = send(between, local)
    second_b, third_b, kept_b = parts(
        ((1, 0, 0), (2, 1, 0), (3, 2, 0)),
        [(1, bf16), (1, bf16), (1, f32)],
        where,
        weight_b,
        whole_b,
        dzt_b,
        dzo_b,
    )
    grad_weight_a = weight_grad((0, 1), rows, cols, where, (got_a, far_a), got_a)
    cross2_a = wait(cross2_a)
    in1_b = wait(in1_b)
    cross1_b = send(between, add(first_b, in1_b))
    in2_b = send(inward, second_b)
    out_a = send(outward, sum3_a)
    s1, s_mid = wait(s1, s_mid)
    s_end = send(outward, s_mid)
    s_mid2 = send(between, s1)
    cross1_b = wait(cross1_b)
    out_b = send(outward, add(third_b, cross1_b))
    in2_b = wait(in2_b)
    cross2_b = send(between, add(second_b, in2_b))
    out_a = wait(out_a)
    in3_b = send(inward, third_b)
    s_end, s_mid2 = wait(s_end, s_mid2)
    s_end2 = send(outward, s_mid2)
    in3_a = send(inward, third_a)
    s2 = choose(where, s_end, s_mid2)
    got_b = wait(got_b)
    grad_bias, grad_stitch = total_sums(rows, cols, got_a, got_b)
    half_b = weight_grad((0,), rows, cols, where, (got_b,), got_b)
    in3_b, out_b, cross2_b = wait(in3_b, out_b, cross2_b)
    grad_image_b = finish(where, position_mask, group, kept_b, in3_b, cross2_b, out_b)
    s_end2, in3_a = wait(s_end2, in3_a)
    s3 = choose(where, s_end2, s_mid)
    far_b = send(swap, got_b)
    far_high = send(swap, join(s2, s3))
    far_low = send(swap, join(local, s1))
    grad_image_a = finish(where, position_mask, group, kept_a, in3_a, cross2_a, out_a)
    stitched_a, stitched_b = lay_out(where, local, s1, s2, s3, far_low, far_high)
    grad_weight_b = weight_grad((1,), rows, cols, where, (far_b,), got_b, half_b)
    return (
        stitched_a,
        stitched_b,
        grad_image_a,
        grad_image_b,
        grad_weight_a,
        grad_weight_b,
        grad_bias,
        grad_stitch,
    )


def solution(mesh):
    placed = (
        P("dp", "mp"),
        P("dp", "mp"),
        P("dp"),
        P(),
        P(None, "mp"),
        P(None, "mp"),
        P(None, "mp"),
        P(None, "mp"),
        P("dp", "mp"),
        P("dp", "mp"),
    )
    fits = mesh.shape["dp"] == 4 and mesh.shape["mp"] == 8
    return jax.shard_map(
        fast_shards if fits else general_shards,
        mesh=mesh,
        in_specs=placed,
        out_specs=(
            P("dp", None),
            P("dp", None),
            P("mp", "dp"),
            P("mp", "dp"),
            P("dp", "mp"),
            P("dp", "mp"),
            P(None, "mp"),
            P(None, "mp"),
        ),
        check_vma=False,
    )
```

```python
import functools

import jax
import jax.numpy as jnp
from jax import lax
from jax.experimental import pallas as pl
from jax.experimental.pallas import tpu as pltpu
from jax.sharding import PartitionSpec as P

CH = 256
POS = 36


def keep_block(image_group, position_mask, first_col, cols):
    positions = (first_col + lax.iota(jnp.int32, cols)) // CH
    onehot = (positions[:, None] == lax.iota(jnp.int32, POS)[None, :]).astype(jnp.float32)
    per_position = jnp.dot(onehot, position_mask.astype(jnp.float32).T)
    return jnp.where(
        image_group[:, None] == 1, per_position[:, 1][None, :], per_position[:, 0][None, :]
    )


def general_shards(
    image_a,
    image_b,
    image_group,
    position_mask,
    weight_a,
    weight_b,
    tower_bias,
    stitch,
    cotan_a,
    cotan_b,
):
    batch_rows = image_a.shape[0]
    shard_cols = image_a.shape[1]
    first_col = lax.axis_index("mp") * shard_cols
    keep_mask = keep_block(image_group, position_mask, first_col, shard_cols)
    keep_low = keep_mask.astype(jnp.bfloat16)
    contract_rows = (((0,), (0,)), ((), ()))
    contract_units = (((1,), (1,)), ((), ()))
    full_a = lax.all_gather(image_a * keep_low, "mp", axis=1, tiled=True)
    full_b = lax.all_gather(image_b * keep_low, "mp", axis=1, tiled=True)
    pre_a = jnp.dot(full_a, weight_a, preferred_element_type=jnp.float32) + tower_bias[0][None, :]
    pre_b = jnp.dot(full_b, weight_b, preferred_element_type=jnp.float32) + tower_bias[1][None, :]
    sigma_a = jax.nn.sigmoid(pre_a)
    sigma_b = jax.nn.sigmoid(pre_b)
    hidden_a = pre_a * sigma_a
    hidden_b = pre_b * sigma_b
    local_a = (stitch[0][None, :] * hidden_a + stitch[1][None, :] * hidden_b).astype(jnp.bfloat16)
    local_b = (stitch[2][None, :] * hidden_a + stitch[3][None, :] * hidden_b).astype(jnp.bfloat16)
    stitched_a = lax.all_gather(local_a, "mp", axis=1, tiled=True)
    stitched_b = lax.all_gather(local_b, "mp", axis=1, tiled=True)
    upper_a = cotan_a.astype(jnp.float32)
    upper_b = cotan_b.astype(jnp.float32)
    dhid_a = stitch[0][None, :] * upper_a + stitch[2][None, :] * upper_b
    dhid_b = stitch[1][None, :] * upper_a + stitch[3][None, :] * upper_b
    dpre_a = dhid_a * (sigma_a * (1.0 + pre_a * (1.0 - sigma_a)))
    dpre_b = dhid_b * (sigma_b * (1.0 + pre_b * (1.0 - sigma_b)))
    bias_terms = jnp.stack([jnp.sum(dpre_a, axis=0), jnp.sum(dpre_b, axis=0)])
    stitch_terms = jnp.stack(
        [
            jnp.sum(upper_a * hidden_a, axis=0),
            jnp.sum(upper_a * hidden_b, axis=0),
            jnp.sum(upper_b * hidden_a, axis=0),
            jnp.sum(upper_b * hidden_b, axis=0),
        ]
    )
    grad_bias, grad_stitch = lax.psum((bias_terms, stitch_terms), "dp")
    dlow_a = dpre_a.astype(jnp.bfloat16)
    dlow_b = dpre_b.astype(jnp.bfloat16)
    block_a = lax.dot_general(full_a, dlow_a, contract_rows, preferred_element_type=jnp.float32)
    block_b = lax.dot_general(full_b, dlow_b, contract_rows, preferred_element_type=jnp.float32)
    grad_weight_a = lax.psum_scatter(block_a, "dp", scatter_dimension=0, tiled=True)
    grad_weight_b = lax.psum_scatter(block_b, "dp", scatter_dimension=0, tiled=True)
    part_a = lax.dot_general(weight_a, dlow_a, contract_units, preferred_element_type=jnp.float32)
    part_b = lax.dot_general(weight_b, dlow_b, contract_units, preferred_element_type=jnp.float32)
    summed = lax.psum_scatter(
        jnp.concatenate([part_a, part_b], axis=1), "mp", scatter_dimension=0, tiled=True
    )
    keep_cols = keep_mask.T
    grad_image_a = (summed[:, :batch_rows] * keep_cols).astype(jnp.bfloat16)
    grad_image_b = (summed[:, batch_rows:] * keep_cols).astype(jnp.bfloat16)
    return (
        stitched_a,
        stitched_b,
        grad_image_a,
        grad_image_b,
        grad_weight_a,
        grad_weight_b,
        grad_bias,
        grad_stitch,
    )


SWAP_CORE = [(d, d ^ 1) for d in range(8)]
NEAR_Z = [(d, d ^ 2) for d in range(8)]
FAR_Z = [(d, d ^ 4) for d in range(8)]
ENDS_IN = [(0, 2), (1, 3), (6, 4), (7, 5)]
MIDS = [(2, 4), (3, 5), (4, 2), (5, 3)]
ENDS_OUT = [(2, 0), (3, 1), (4, 6), (5, 7)]
SLOTS = ((3, 2, 1, 0), (3, 2, 0, 1), (0, 1, 3, 2), (0, 1, 2, 3))
LANES = 128
EXTRA = 16
VMEM_LIMIT = 22 * 1024 * 1024
SMEM = pl.BlockSpec(memory_space=pltpu.SMEM)
VMEM = pl.BlockSpec(memory_space=pltpu.VMEM)
HBM = pl.BlockSpec(memory_space=pltpu.HBM)
ANY = pl.BlockSpec(memory_space=pl.ANY)
LITTLE = pl.CostEstimate(flops=1, bytes_accessed=1, transcendentals=0)


def low(x):
    return x.astype(jnp.bfloat16)


def wide(x):
    return x.astype(jnp.float32)


def array(shape, dtype):
    return jax.ShapeDtypeStruct(shape, dtype)


class Line:
    def __init__(self):
        self.token = None

    def tie(self, *xs):
        if self.token is None:
            return xs
        *xs, self.token = lax.optimization_barrier((*xs, self.token))
        return xs

    def wait(self, *arrived):
        arrived = self.tie(*arrived)
        return arrived if len(arrived) > 1 else arrived[0]

    def send(self, move, x):
        return move(*self.tie(x))


line = Line()


def call(kernel, out_shape, in_specs, out_specs, name, scratch=(), aliases={}):
    single = not isinstance(out_shape, list)
    outs = [out_shape] if single else out_shape
    places = [out_specs] if single else out_specs
    n_in, n_out = len(in_specs), len(outs)
    before = () if line.token is None else (line.token,)

    def body(*refs):
        start = n_in + len(before)
        refs[start + n_out][...] = jnp.zeros((8, LANES), jnp.float32)
        kernel(*refs[:n_in], *refs[start : start + n_out], *refs[start + n_out + 1 :])

    run = pl.pallas_call(
        body,
        out_shape=[*outs, array((8, LANES), jnp.float32)],
        in_specs=[*in_specs, *[HBM] * len(before)],
        out_specs=[*places, VMEM],
        scratch_shapes=scratch,
        input_output_aliases=aliases,
        compiler_params=pltpu.CompilerParams(vmem_limit_bytes=VMEM_LIMIT),
        cost_estimate=LITTLE,
        name=name,
    )

    def go(*operands):
        *results, line.token = run(*operands, *before)
        return results[0] if single else results

    return go


def marks_of(marks, place, cols, chunk):
    position = (place * cols + chunk * LANES) // CH
    return marks[0, position], marks[1, position]


def mask_kernel(place, marks, group, image, out, held, sem):
    rows, cols = image.shape
    copy = pltpu.make_async_copy(image, held, sem)
    copy.start()
    second = jnp.broadcast_to(jnp.where(group[...] == 1, 1.0, 0.0), (8, rows)).T[:, 0:1] > 0.5
    copy.wait()
    for chunk in range(cols // LANES):
        zero, one = marks_of(marks, place[0], cols, chunk)
        keep = wide(jnp.where(second, one, zero))
        lanes = slice(chunk * LANES, (chunk + 1) * LANES)
        out[:, lanes] = low(wide(held[:, lanes]) * keep)


def mask_image(place, marks, group, image):
    return call(
        mask_kernel,
        array(image.shape, jnp.bfloat16),
        [SMEM, SMEM, VMEM, HBM],
        VMEM,
        "mask_image",
        [pltpu.VMEM(image.shape, jnp.bfloat16), pltpu.SemaphoreType.DMA],
    )(place, marks, group, in_hbm(image))


def in_hbm(x):
    return pltpu.with_memory_space_constraint(x, pltpu.HBM)


def dot(x, y):
    return jnp.dot(x, y, preferred_element_type=jnp.float32)


def products(where, ks, mine, other, held, sems, emit):
    cols = held.shape[2]

    def copies(i):
        block = 2 * (where[0] ^ ks[i]) + where[1]
        rows = pl.ds(pl.multiple_of(block * cols, cols), cols)
        return [
            pltpu.make_async_copy(weight.at[rows, :], held.at[i, side], sems.at[i, side])
            for side, weight in enumerate((mine, other))
        ]

    for i in range(len(ks)):
        for copy in copies(i):
            copy.start()
    for i in range(len(ks)):
        for copy in copies(i):
            copy.wait()
        emit(i, held[i, 0], held[i, 1])


def open_kernel(where, p0, p1, p2, mine, other, keep, send, last, slot, held, sems):
    pieces = (p0, p1, p2)
    cols = p0.shape[1]
    ahead = []
    for at, (k, out) in enumerate(((3, last), (where[3], slot))):
        block = 2 * (where[0] ^ k) + where[1]
        rows = pl.ds(pl.multiple_of(block * cols, cols), cols)
        for side, weight in enumerate((mine, other)):
            ahead.append(
                pltpu.make_async_copy(weight.at[rows, :], out.at[side], sems.at[3 + at, side])
            )

    def emit(i, own_block, other_block):
        if i == 0:
            for copy in ahead:
                copy.start()
            keep[...] = dot(p0[...], own_block)
            send[...] = dot(p0[...], other_block)
        else:
            keep[...] += dot(pieces[i][...], own_block)
            send[...] += dot(pieces[i][...], other_block)

    products(where, (0, 1, 2), mine, other, held, sems, emit)
    for copy in ahead:
        copy.wait()


def forward_open(where, p0, p1, p2, mine, other):
    rows, cols = p0.shape
    units = mine.shape[1]
    blocks = pltpu.VMEM((2, cols, units), jnp.bfloat16)
    return call(
        open_kernel,
        [array((rows, units), jnp.float32)] * 2 + [blocks] * 2,
        [SMEM] + [VMEM] * 3 + [HBM] * 2,
        [VMEM] * 4,
        "forward_open",
        [pltpu.VMEM((3, 2, cols, units), jnp.bfloat16), pltpu.SemaphoreType.DMA((5, 2))],
    )(where, p0, p1, p2, in_hbm(mine), in_hbm(other))


def close_kernel(p3, weights, keep, send, out, sent):
    sent[...] = send[...] + dot(p3[...], weights[1])
    out[...] = keep[...] + dot(p3[...], weights[0])


def forward_close(p3, weights, keep, send):
    return call(
        close_kernel,
        [array(keep.shape, jnp.float32)] * 2,
        [VMEM] * 4,
        [VMEM] * 2,
        "forward_close",
    )(p3, weights, keep, send)


def slot_kernel(weights, dz_t, dzo_t, out):
    out[...] = low(dot(weights[0], dz_t[...]) + dot(weights[1], dzo_t[...]))


def first_slot(weights, dz_t, dzo_t):
    return call(
        slot_kernel,
        array((weights.shape[1], dz_t.shape[1]), jnp.bfloat16),
        [VMEM] * 3,
        VMEM,
        "first_slot",
    )(weights, dz_t, dzo_t)


def tower_math(pre, bias, unit_a, unit_b, upper_a, upper_b, dz, dz_t, sums):
    pre = pre + bias[...]
    sigma = jax.nn.sigmoid(pre)
    hidden = pre * sigma
    cot_a = wide(upper_a[...])
    cot_b = wide(upper_b[...])
    dhid = unit_a[...] * cot_a + unit_b[...] * cot_b
    dpre = dhid * (sigma * (1.0 + pre * (1.0 - sigma)))
    dz[...] = low(dpre)
    dz_t[...] = low(dpre).T
    sums[0:1, :] = jnp.sum(dpre, axis=0, keepdims=True)
    sums[1:2, :] = jnp.sum(cot_a * hidden, axis=0, keepdims=True)
    sums[2:3, :] = jnp.sum(cot_b * hidden, axis=0, keepdims=True)
    sums[3:4, :] = jnp.zeros_like(sums[3:4, :])
    return hidden


def first_kernel(own, got, bias, stitch, upper_a, upper_b, dz, dz_t, sums, hidden):
    hidden[...] = tower_math(
        own[...] + got[...],
        bias[0:1, :],
        stitch[0:1, :],
        stitch[2:3, :],
        upper_a,
        upper_b,
        dz,
        dz_t,
        sums,
    )


def second_kernel(own, got, earlier, bias, stitch, upper_a, upper_b, dz, dz_t, sums, local):
    hidden = tower_math(
        own[...] + got[...],
        bias[1:2, :],
        stitch[1:2, :],
        stitch[3:4, :],
        upper_a,
        upper_b,
        dz,
        dz_t,
        sums,
    )
    rows = hidden.shape[0]
    before = earlier[...]
    local[0:rows, :] = low(stitch[0:1, :] * before + stitch[1:2, :] * hidden)
    local[rows : 2 * rows, :] = low(stitch[2:3, :] * before + stitch[3:4, :] * hidden)


def tower(kernel, name, last, *operands):
    rows, units = operands[0].shape
    return call(
        kernel,
        [
            array((rows, units), jnp.bfloat16),
            array((units, rows), jnp.bfloat16),
            array((4, units), jnp.float32),
            last,
        ],
        [VMEM] * len(operands),
        [VMEM] * 4,
        name,
    )(*operands)


def part_kernel(slots, where, mine, other, dz_t, dzo_t, *refs):
    *outs, held, sems = refs
    cols = held.shape[2]

    def emit(i, own_block, other_block):
        _, at, block = slots[i]
        total = dot(own_block, dz_t[...]) + dot(other_block, dzo_t[...])
        outs[at][block * cols : (block + 1) * cols, :] = total.astype(outs[at].dtype)

    products(where, [where[3 + slot] for slot, _, _ in slots], mine, other, held, sems, emit)


def parts(slots, outs, where, mine, other, dz_t, dzo_t):
    units, rows = dz_t.shape
    cols = mine.shape[0] // 8
    return call(
        functools.partial(part_kernel, slots),
        [array((blocks * cols, rows), dtype) for blocks, dtype in outs],
        [SMEM, HBM, HBM, VMEM, VMEM],
        [VMEM] * len(outs),
        "parts",
        [
            pltpu.VMEM((len(slots), 2, cols, units), jnp.bfloat16),
            pltpu.SemaphoreType.DMA((len(slots), 2)),
        ],
    )(where, in_hbm(mine), in_hbm(other), dz_t, dzo_t)


def choose_kernel(where, at_end, in_middle, out, sem):
    for flag, source in enumerate((at_end, in_middle)):
        pl.when(where[2] == flag)(pltpu.make_async_copy(source, out, sem).start)
    pltpu.make_async_copy(at_end, out, sem).wait()


def choose(where, at_end, in_middle):
    return call(
        choose_kernel,
        array(at_end.shape, at_end.dtype),
        [SMEM, ANY, ANY],
        VMEM,
        "choose",
        [pltpu.SemaphoreType.DMA],
    )(where, at_end, in_middle)


def join_kernel(one, two, out):
    rows = one.shape[0]
    out[0:rows, :] = one[...]
    out[rows : 2 * rows, :] = two[...]


def join(one, two):
    rows, cols = one.shape
    return call(join_kernel, array((2 * rows, cols), one.dtype), [VMEM, VMEM], VMEM, "join")(
        one, two
    )


def lay_kernel(where, *refs):
    own, far, (out_a, out_b, sems) = refs[0:4], refs[4:6], refs[6:]
    rows = out_a.shape[0]
    units = own[0].shape[1]
    copies = []
    for side in range(2):
        for k in range(4):
            block = 2 * (where[0] ^ k) + (where[1] ^ side)
            lanes = pl.ds(pl.multiple_of(block * units, units), units)
            source, start = (own[k], 0) if side == 0 else (far[k // 2], 2 * rows * (k % 2))
            for half, out in enumerate((out_a, out_b)):
                at = pl.ds(start + half * rows, rows)
                sem = sems.at[side * 8 + k * 2 + half]
                copies.append(pltpu.make_async_copy(source.at[at, :], out.at[:, lanes], sem))
    for copy in copies:
        copy.start()
    for copy in copies:
        copy.wait()


def lay_out(where, *sources):
    rows, units = sources[0].shape
    return call(
        lay_kernel,
        [array((rows // 2, 8 * units), jnp.bfloat16)] * 2,
        [SMEM] + [ANY] * 6,
        [VMEM] * 2,
        "lay_out",
        [pltpu.SemaphoreType.DMA((16,))],
    )(where, *sources)


def add_kernel(at, one, two, out):
    rows = out.shape[0]
    out[...] = low(wide(one[at : at + rows, :]) + wide(two[0:rows, :]))


def add(one, two, block=0, rows=None):
    rows = rows or min(one.shape[0], two.shape[0])
    return call(
        functools.partial(add_kernel, block * rows),
        array((rows, one.shape[1]), jnp.bfloat16),
        [VMEM, VMEM],
        VMEM,
        "add",
    )(one, two)


def finish_kernel(where, marks, group, kept, third, cross, last, out, held, own, sems):
    second = group[...] == 1
    cols = out.shape[0]
    copies = [pltpu.make_async_copy(kept, own, sems.at[3])]
    for n, source in enumerate((third, cross, last)):
        copies.append(pltpu.make_async_copy(source, held.at[n], sems.at[n]))
    for copy in copies:
        copy.start()
    for copy in copies:
        copy.wait()
    for chunk in range(cols // LANES):
        zero, one = marks_of(marks, where[8], cols, chunk)
        keep = wide(jnp.where(second, one, zero))
        rows = slice(chunk * LANES, (chunk + 1) * LANES)
        total = own[rows, :] + wide(held[0, rows, :])
        total += wide(held[1, rows, :]) + wide(held[2, rows, :])
        out[rows, :] = low(total * keep)


def finish(where, marks, group, kept, third, cross, last):
    return call(
        finish_kernel,
        array(kept.shape, jnp.bfloat16),
        [SMEM, SMEM, VMEM] + [HBM] * 4,
        VMEM,
        "finish",
        [
            pltpu.VMEM((3, *kept.shape), jnp.bfloat16),
            pltpu.VMEM(kept.shape, jnp.float32),
            pltpu.SemaphoreType.DMA((4,)),
        ],
    )(where, marks, group, *[in_hbm(x) for x in (kept, third, cross, last)])


def pack_kernel(where, p0, p1, p2, p3, dz, sums, given, out, sems):
    rows, units = dz.shape
    cols = p0.shape[1]
    for q in range(4):
        block = out.at[q, pl.ds(0, rows), pl.ds(0, cols)]
        for index, piece in enumerate((p0, p1, p2, p3)):
            start = pltpu.make_async_copy(piece, block, sems.at[q]).start
            pl.when(where[0] ^ q == index)(start)
    extra = jnp.zeros((EXTRA, cols + units), jnp.bfloat16)
    for q in range(4):
        out[q, rows : rows + EXTRA, :] = extra
        out[q, 0:rows, cols : cols + units] = dz[...]
    for k in range(3):
        rest = sums[k : k + 1, :]
        for term in range(3):
            piece = low(rest)
            row = rows + 3 * k + term
            for q in range(4):
                out[q, row : row + 1, cols : cols + units] = piece
            rest = rest - wide(piece)
    gives = [pltpu.make_async_copy(out.at[q], given.at[q], sems.at[4 + q]) for q in range(4)]
    for q in range(4):
        block = out.at[q, pl.ds(0, rows), pl.ds(0, cols)]
        pltpu.make_async_copy(p0, block, sems.at[q]).wait()
        gives[q].start()
    for give in gives:
        give.wait()


def pack(where, pieces, dz, sums):
    rows, units = dz.shape
    cols = pieces[0].shape[1]
    return call(
        pack_kernel,
        pltpu.HBM((4, rows + EXTRA, cols + units), jnp.bfloat16),
        [SMEM] + [ANY] * 4 + [VMEM] * 2,
        HBM,
        "pack",
        [
            pltpu.VMEM((4, rows + EXTRA, cols + units), jnp.bfloat16),
            pltpu.SemaphoreType.DMA((8,)),
        ],
    )(where, *pieces, dz, sums)


def weight_kernel(sides, where, *refs):
    n = len(sides)
    images_of, dz_of = refs[:n], refs[n]
    *outs, images, dzs, tiles, sems = refs[n + 1 + (sides == (1,)) :]
    out = outs[0]
    rows, units = dzs.shape[1:]
    cols = images.shape[3]
    tile = tiles.shape[1]
    steps = cols // tile

    def fetch(q):
        source = dz_of.at[q, pl.ds(0, rows), pl.ds(cols, units)]
        return pltpu.make_async_copy(source, dzs.at[q], sems.at[q])

    def block(i, q):
        image = images_of[i].at[q, pl.ds(0, rows), pl.ds(0, cols)]
        return pltpu.make_async_copy(image, images.at[i, q], sems.at[4 + 4 * i + q])

    def give(i, t):
        at = pl.multiple_of((where[1] ^ sides[i]) * cols + t * tile, tile)
        slot = i * steps + t
        return pltpu.make_async_copy(
            tiles.at[slot], out.at[pl.ds(at, tile), :], sems.at[12 + slot]
        )

    for q in range(4):
        fetch(q).start()
    for i in range(n):
        for q in range(4):
            block(i, q).start()
    for q in range(4):
        fetch(q).wait()
    for i in range(n):
        for q in range(4):
            block(i, q).wait()
        if len(outs) > 1:
            for q in range(4):
                pltpu.make_async_copy(images.at[i, q], outs[1].at[q], sems.at[4 + q]).start()
        for t in range(steps):
            total = None
            for q in range(4):
                term = lax.dot_general(
                    images[i, q, :, t * tile : (t + 1) * tile],
                    dzs[q],
                    (((0,), (0,)), ((), ())),
                    preferred_element_type=jnp.float32,
                )
                total = term if total is None else total + term
            tiles[i * steps + t] = total
            give(i, t).start()
    for i in range(n):
        for t in range(steps):
            give(i, t).wait()
    if len(outs) > 1:
        for q in range(4):
            pltpu.make_async_copy(images.at[0, q], outs[1].at[q], sems.at[4 + q]).wait()


def weight_grad(sides, rows, cols, where, images, dz, *before):
    units = dz.shape[2] - cols
    tile = cols // 3
    n = len(sides)
    outs = [pltpu.HBM((2 * cols, units), jnp.float32)]
    if sides == (0,):
        outs.append(pltpu.HBM((4, rows, cols), jnp.bfloat16))
    return call(
        functools.partial(weight_kernel, sides),
        outs if len(outs) > 1 else outs[0],
        [SMEM] + [ANY] * (n + 1) + [HBM] * len(before),
        [HBM] * len(outs) if len(outs) > 1 else HBM,
        "weight_grad",
        [
            pltpu.VMEM((n, 4, rows, cols), jnp.bfloat16),
            pltpu.VMEM((4, rows, units), jnp.bfloat16),
            pltpu.VMEM((3 * n, tile, units), jnp.float32),
            pltpu.SemaphoreType.DMA((18,)),
        ],
        {n + 2: 0} if before else {},
    )(where, *images, dz, *before)


def sums_kernel(rows, cols, got_a, got_b, bias, stitch, terms, sems):
    units = bias.shape[1]
    copies = [
        pltpu.make_async_copy(
            got.at[:, pl.ds(rows, EXTRA), pl.ds(cols, units)], terms.at[side], sems.at[side]
        )
        for side, got in enumerate((got_a, got_b))
    ]
    for copy in copies:
        copy.start()
    for copy in copies:
        copy.wait()
    for side in range(2):
        totals = []
        for k in range(3):
            each = [
                (
                    wide(terms[side, q, 3 * k + 2 : 3 * k + 3, :])
                    + wide(terms[side, q, 3 * k + 1 : 3 * k + 2, :])
                )
                + wide(terms[side, q, 3 * k : 3 * k + 1, :])
                for q in range(4)
            ]
            totals.append((each[0] + each[1]) + (each[2] + each[3]))
        bias[side : side + 1, :] = totals[0]
        stitch[side : side + 1, :] = totals[1]
        stitch[2 + side : 3 + side, :] = totals[2]


def total_sums(rows, cols, got_a, got_b):
    units = got_a.shape[2] - cols
    return call(
        functools.partial(sums_kernel, rows, cols),
        [array((2, units), jnp.float32), array((4, units), jnp.float32)],
        [ANY, ANY],
        [VMEM, VMEM],
        "total_sums",
        [pltpu.VMEM((2, 4, EXTRA, units), jnp.bfloat16), pltpu.SemaphoreType.DMA((2,))],
    )(got_a, got_b)


def swap(x):
    return lax.ppermute(x, "mp", SWAP_CORE)


def along(x):
    return lax.ppermute(x, "mp", NEAR_Z)


def across(x):
    return lax.ppermute(x, "mp", FAR_Z)


def inward(x):
    return lax.ppermute(x, "mp", ENDS_IN)


def between(x):
    return lax.ppermute(x, "mp", MIDS)


def outward(x):
    return lax.ppermute(x, "mp", ENDS_OUT)


def exchange(x):
    return lax.all_to_all(x, "dp", 0, 0)


def fast_shards(
    image_a,
    image_b,
    image_group,
    position_mask,
    weight_a,
    weight_b,
    tower_bias,
    stitch,
    cotan_a,
    cotan_b,
):
    rows, cols = image_a.shape
    units = weight_a.shape[1]
    place = lax.axis_index("mp").astype(jnp.int32)
    z = place // 2
    core = place % 2
    quarter = lax.axis_index("dp").astype(jnp.int32)
    middle = ((z == 1) | (z == 2)).astype(jnp.int32)
    slots = jnp.take(jnp.asarray(SLOTS, jnp.int32), z, axis=0) ^ z
    where = jnp.concatenate(
        [jnp.stack([z, core, middle]), slots, jnp.stack([quarter, place])]
    ).astype(jnp.int32)
    group = image_group[None, :]
    line.token = None
    bf16, f32 = jnp.bfloat16, jnp.float32
    send, wait = line.send, line.wait

    whole_a = swap(weight_a)
    whole_b = swap(weight_b)
    a0 = mask_image(place[None], position_mask, group, image_a)
    a2 = send(across, a0)
    a1 = send(along, a0)
    b0 = mask_image(place[None], position_mask, group, image_b)
    a1, a2 = wait(a1, a2)
    a3 = send(along, a2)
    b_mid = send(between, b0)
    b1 = send(along, b0)
    whole_a, whole_b = wait(whole_a, whole_b)
    keep_a, give_a, last_a, slot_a = forward_open(where, a0, a1, a2, weight_a, whole_a)
    a3 = wait(a3)
    own_a, sent_a = forward_close(a3, last_a, keep_a, give_a)
    got_sum = wait(send(swap, sent_a))
    dz_a, dzt_a, sums_a, hidden_a = tower(
        first_kernel,
        "tower_a",
        array((rows, units), f32),
        own_a,
        got_sum,
        tower_bias,
        stitch,
        cotan_a,
        cotan_b,
    )
    dzo_a = send(swap, dzt_a)
    packed_a = pack(where, (a0, a1, a2, a3), dz_a, sums_a)
    b1, b_mid = wait(b1, b_mid)
    got_a = send(exchange, packed_a)
    b_end = send(outward, b_mid)
    b_mid2 = send(between, b1)
    dzo_a = wait(dzo_a)
    first_a = first_slot(slot_a, dzt_a, dzo_a)
    in1_a = send(inward, first_a)
    second_a, third_a, kept_a = parts(
        ((1, 0, 0), (2, 1, 0), (3, 2, 0)),
        [(1, bf16), (1, bf16), (1, f32)],
        where,
        weight_a,
        whole_a,
        dzt_a,
        dzo_a,
    )
    in2_a = send(inward, second_a)
    b_end, b_mid2 = wait(b_end, b_mid2)
    b_end2 = send(outward, b_mid2)
    b2 = choose(where, b_end, b_mid2)
    keep_b, give_b, last_b, slot_b = forward_open(where, b0, b1, b2, weight_b, whole_b)
    in1_a = wait(in1_a)
    cross1_a = send(between, add(first_a, in1_a))
    b_end2 = wait(b_end2)
    b3 = choose(where, b_end2, b_mid)
    own_b, sent_b = forward_close(b3, last_b, keep_b, give_b)
    got_sum = send(swap, sent_b)
    in2_a = wait(in2_a)
    sum2_a = add(second_a, in2_a)
    got_sum = wait(got_sum)
    dz_b, dzt_b, sums_b, local = tower(
        second_kernel,
        "tower_b",
        array((2 * rows, units), bf16),
        own_b,
        got_sum,
        hidden_a,
        tower_bias,
        stitch,
        cotan_a,
        cotan_b,
    )
    dzo_b = send(swap, dzt_b)
    packed_b = pack(where, (b0, b1, b2, b3), dz_b, sums_b)
    cross1_a = wait(cross1_a)
    sum3_a = add(third_a, cross1_a)
    got_a = wait(got_a)
    far_a = send(swap, got_a)
    got_b = send(exchange, packed_b)
    cross2_a = send(between, sum2_a)
    dzo_b, far_a = wait(dzo_b, far_a)
    first_b = first_slot(slot_b, dzt_b, dzo_b)
    in1_b = send(inward, first_b)
    s1 = send(along, local)
    s_mid = send(between, local)
    second_b, third_b, kept_b = parts(
        ((1, 0, 0), (2, 1, 0), (3, 2, 0)),
        [(1, bf16), (1, bf16), (1, f32)],
        where,
        weight_b,
        whole_b,
        dzt_b,
        dzo_b,
    )
    grad_weight_a = weight_grad((0, 1), rows, cols, where, (got_a, far_a), got_a)
    cross2_a = wait(cross2_a)
    in1_b = wait(in1_b)
    cross1_b = send(between, add(first_b, in1_b))
    in2_b = send(inward, second_b)
    out_a = send(outward, sum3_a)
    s1, s_mid = wait(s1, s_mid)
    s_end = send(outward, s_mid)
    s_mid2 = send(between, s1)
    cross1_b = wait(cross1_b)
    out_b = send(outward, add(third_b, cross1_b))
    in2_b = wait(in2_b)
    cross2_b = send(between, add(second_b, in2_b))
    out_a = wait(out_a)
    in3_b = send(inward, third_b)
    s_end, s_mid2 = wait(s_end, s_mid2)
    s_end2 = send(outward, s_mid2)
    in3_a = send(inward, third_a)
    s2 = choose(where, s_end, s_mid2)
    got_b = wait(got_b)
    grad_bias, grad_stitch = total_sums(rows, cols, got_a, got_b)
    half_b, block_b = weight_grad((0,), rows, cols, where, (got_b,), got_b)
    in3_b, out_b, cross2_b = wait(in3_b, out_b, cross2_b)
    grad_image_b = finish(where, position_mask, group, kept_b, in3_b, cross2_b, out_b)
    s_end2, in3_a = wait(s_end2, in3_a)
    s3 = choose(where, s_end2, s_mid)
    high = join(s2, s3)
    low_half = join(local, s1)
    far_high = send(swap, high)
    far_low = send(swap, low_half)
    far_b = send(swap, block_b)
    grad_image_a = finish(where, position_mask, group, kept_a, in3_a, cross2_a, out_a)
    stitched_a, stitched_b = lay_out(where, local, s1, s2, s3, far_low, far_high)
    grad_weight_b = weight_grad((1,), rows, cols, where, (far_b,), got_b, half_b)
    return (
        stitched_a,
        stitched_b,
        grad_image_a,
        grad_image_b,
        grad_weight_a,
        grad_weight_b,
        grad_bias,
        grad_stitch,
    )


def solution(mesh):
    placed = (
        P("dp", "mp"),
        P("dp", "mp"),
        P("dp"),
        P(),
        P(None, "mp"),
        P(None, "mp"),
        P(None, "mp"),
        P(None, "mp"),
        P("dp", "mp"),
        P("dp", "mp"),
    )
    fits = mesh.shape["dp"] == 4 and mesh.shape["mp"] == 8
    return jax.shard_map(
        fast_shards if fits else general_shards,
        mesh=mesh,
        in_specs=placed,
        out_specs=(
            P("dp", None),
            P("dp", None),
            P("mp", "dp"),
            P("mp", "dp"),
            P("dp", "mp"),
            P("dp", "mp"),
            P(None, "mp"),
            P(None, "mp"),
        ),
        check_vma=False,
    )
```

```python
import functools

import jax
import jax.numpy as jnp
from jax import lax
from jax.experimental import pallas as pl
from jax.experimental.pallas import tpu as pltpu
from jax.sharding import PartitionSpec as P

CH = 256
POS = 36


def keep_block(image_group, position_mask, first_col, cols):
    positions = (first_col + lax.iota(jnp.int32, cols)) // CH
    onehot = (positions[:, None] == lax.iota(jnp.int32, POS)[None, :]).astype(jnp.float32)
    per_position = jnp.dot(onehot, position_mask.astype(jnp.float32).T)
    return jnp.where(
        image_group[:, None] == 1, per_position[:, 1][None, :], per_position[:, 0][None, :]
    )


def general_shards(
    image_a,
    image_b,
    image_group,
    position_mask,
    weight_a,
    weight_b,
    tower_bias,
    stitch,
    cotan_a,
    cotan_b,
):
    batch_rows = image_a.shape[0]
    shard_cols = image_a.shape[1]
    first_col = lax.axis_index("mp") * shard_cols
    keep_mask = keep_block(image_group, position_mask, first_col, shard_cols)
    keep_low = keep_mask.astype(jnp.bfloat16)
    contract_rows = (((0,), (0,)), ((), ()))
    contract_units = (((1,), (1,)), ((), ()))
    full_a = lax.all_gather(image_a * keep_low, "mp", axis=1, tiled=True)
    full_b = lax.all_gather(image_b * keep_low, "mp", axis=1, tiled=True)
    pre_a = jnp.dot(full_a, weight_a, preferred_element_type=jnp.float32) + tower_bias[0][None, :]
    pre_b = jnp.dot(full_b, weight_b, preferred_element_type=jnp.float32) + tower_bias[1][None, :]
    sigma_a = jax.nn.sigmoid(pre_a)
    sigma_b = jax.nn.sigmoid(pre_b)
    hidden_a = pre_a * sigma_a
    hidden_b = pre_b * sigma_b
    local_a = (stitch[0][None, :] * hidden_a + stitch[1][None, :] * hidden_b).astype(jnp.bfloat16)
    local_b = (stitch[2][None, :] * hidden_a + stitch[3][None, :] * hidden_b).astype(jnp.bfloat16)
    stitched_a = lax.all_gather(local_a, "mp", axis=1, tiled=True)
    stitched_b = lax.all_gather(local_b, "mp", axis=1, tiled=True)
    upper_a = cotan_a.astype(jnp.float32)
    upper_b = cotan_b.astype(jnp.float32)
    dhid_a = stitch[0][None, :] * upper_a + stitch[2][None, :] * upper_b
    dhid_b = stitch[1][None, :] * upper_a + stitch[3][None, :] * upper_b
    dpre_a = dhid_a * (sigma_a * (1.0 + pre_a * (1.0 - sigma_a)))
    dpre_b = dhid_b * (sigma_b * (1.0 + pre_b * (1.0 - sigma_b)))
    bias_terms = jnp.stack([jnp.sum(dpre_a, axis=0), jnp.sum(dpre_b, axis=0)])
    stitch_terms = jnp.stack(
        [
            jnp.sum(upper_a * hidden_a, axis=0),
            jnp.sum(upper_a * hidden_b, axis=0),
            jnp.sum(upper_b * hidden_a, axis=0),
            jnp.sum(upper_b * hidden_b, axis=0),
        ]
    )
    grad_bias, grad_stitch = lax.psum((bias_terms, stitch_terms), "dp")
    dlow_a = dpre_a.astype(jnp.bfloat16)
    dlow_b = dpre_b.astype(jnp.bfloat16)
    block_a = lax.dot_general(full_a, dlow_a, contract_rows, preferred_element_type=jnp.float32)
    block_b = lax.dot_general(full_b, dlow_b, contract_rows, preferred_element_type=jnp.float32)
    grad_weight_a = lax.psum_scatter(block_a, "dp", scatter_dimension=0, tiled=True)
    grad_weight_b = lax.psum_scatter(block_b, "dp", scatter_dimension=0, tiled=True)
    part_a = lax.dot_general(weight_a, dlow_a, contract_units, preferred_element_type=jnp.float32)
    part_b = lax.dot_general(weight_b, dlow_b, contract_units, preferred_element_type=jnp.float32)
    summed = lax.psum_scatter(
        jnp.concatenate([part_a, part_b], axis=1), "mp", scatter_dimension=0, tiled=True
    )
    keep_cols = keep_mask.T
    grad_image_a = (summed[:, :batch_rows] * keep_cols).astype(jnp.bfloat16)
    grad_image_b = (summed[:, batch_rows:] * keep_cols).astype(jnp.bfloat16)
    return (
        stitched_a,
        stitched_b,
        grad_image_a,
        grad_image_b,
        grad_weight_a,
        grad_weight_b,
        grad_bias,
        grad_stitch,
    )


SWAP_CORE = [(d, d ^ 1) for d in range(8)]
NEAR_Z = [(d, d ^ 2) for d in range(8)]
FAR_Z = [(d, d ^ 4) for d in range(8)]
ENDS_IN = [(0, 2), (1, 3), (6, 4), (7, 5)]
MIDS = [(2, 4), (3, 5), (4, 2), (5, 3)]
ENDS_OUT = [(2, 0), (3, 1), (4, 6), (5, 7)]
SLOTS = ((3, 2, 1, 0), (3, 2, 0, 1), (0, 1, 3, 2), (0, 1, 2, 3))
LANES = 128
EXTRA = 16
VMEM_LIMIT = 22 * 1024 * 1024
SMEM = pl.BlockSpec(memory_space=pltpu.SMEM)
VMEM = pl.BlockSpec(memory_space=pltpu.VMEM)
HBM = pl.BlockSpec(memory_space=pltpu.HBM)
ANY = pl.BlockSpec(memory_space=pl.ANY)
LITTLE = pl.CostEstimate(flops=1, bytes_accessed=1, transcendentals=0)


def low(x):
    return x.astype(jnp.bfloat16)


def wide(x):
    return x.astype(jnp.float32)


def array(shape, dtype):
    return jax.ShapeDtypeStruct(shape, dtype)


class Line:
    def __init__(self):
        self.token = None

    def tie(self, *xs):
        if self.token is None:
            return xs
        *xs, self.token = lax.optimization_barrier((*xs, self.token))
        return xs

    def wait(self, *arrived):
        arrived = self.tie(*arrived)
        return arrived if len(arrived) > 1 else arrived[0]

    def send(self, move, x):
        return move(*self.tie(x))


line = Line()


def call(kernel, out_shape, in_specs, out_specs, name, scratch=(), aliases={}):
    single = not isinstance(out_shape, list)
    outs = [out_shape] if single else out_shape
    places = [out_specs] if single else out_specs
    n_in, n_out = len(in_specs), len(outs)
    before = () if line.token is None else (line.token,)

    def body(*refs):
        start = n_in + len(before)
        refs[start + n_out][...] = jnp.zeros((8, LANES), jnp.float32)
        kernel(*refs[:n_in], *refs[start : start + n_out], *refs[start + n_out + 1 :])

    run = pl.pallas_call(
        body,
        out_shape=[*outs, array((8, LANES), jnp.float32)],
        in_specs=[*in_specs, *[HBM] * len(before)],
        out_specs=[*places, VMEM],
        scratch_shapes=scratch,
        input_output_aliases=aliases,
        compiler_params=pltpu.CompilerParams(vmem_limit_bytes=VMEM_LIMIT),
        cost_estimate=LITTLE,
        name=name,
    )

    def go(*operands):
        *results, line.token = run(*operands, *before)
        return results[0] if single else results

    return go


def marks_of(marks, place, cols, chunk):
    position = (place * cols + chunk * LANES) // CH
    return marks[0, position], marks[1, position]


def mask_kernel(place, marks, group, image, out, held, sem):
    rows, cols = image.shape
    copy = pltpu.make_async_copy(image, held, sem)
    copy.start()
    second = jnp.broadcast_to(jnp.where(group[...] == 1, 1.0, 0.0), (8, rows)).T[:, 0:1] > 0.5
    copy.wait()
    for chunk in range(cols // LANES):
        zero, one = marks_of(marks, place[0], cols, chunk)
        keep = wide(jnp.where(second, one, zero))
        lanes = slice(chunk * LANES, (chunk + 1) * LANES)
        out[:, lanes] = low(wide(held[:, lanes]) * keep)


def mask_image(place, marks, group, image):
    return call(
        mask_kernel,
        array(image.shape, jnp.bfloat16),
        [SMEM, SMEM, VMEM, ANY],
        VMEM,
        "mask_image",
        [pltpu.VMEM(image.shape, jnp.bfloat16), pltpu.SemaphoreType.DMA],
    )(place, marks, group, image)


def in_hbm(x):
    return pltpu.with_memory_space_constraint(x, pltpu.HBM)


def dot(x, y):
    return jnp.dot(x, y, preferred_element_type=jnp.float32)


def products(where, ks, mine, other, held, sems, emit):
    cols = held.shape[2]

    def copies(i):
        block = 2 * (where[0] ^ ks[i]) + where[1]
        rows = pl.ds(pl.multiple_of(block * cols, cols), cols)
        return [
            pltpu.make_async_copy(weight.at[rows, :], held.at[i, side], sems.at[i, side])
            for side, weight in enumerate((mine, other))
        ]

    for i in range(len(ks)):
        for copy in copies(i):
            copy.start()
    for i in range(len(ks)):
        for copy in copies(i):
            copy.wait()
        emit(i, held[i, 0], held[i, 1])


def open_kernel(where, p0, p1, p2, mine, other, keep, send, last, slot, held, sems):
    pieces = (p0, p1, p2)
    cols = p0.shape[1]
    ahead = []
    for at, (k, out) in enumerate(((3, last), (where[3], slot))):
        block = 2 * (where[0] ^ k) + where[1]
        rows = pl.ds(pl.multiple_of(block * cols, cols), cols)
        for side, weight in enumerate((mine, other)):
            ahead.append(
                pltpu.make_async_copy(weight.at[rows, :], out.at[side], sems.at[3 + at, side])
            )

    def emit(i, own_block, other_block):
        if i == 0:
            for copy in ahead:
                copy.start()
            keep[...] = dot(p0[...], own_block)
            send[...] = dot(p0[...], other_block)
        else:
            keep[...] += dot(pieces[i][...], own_block)
            send[...] += dot(pieces[i][...], other_block)

    products(where, (0, 1, 2), mine, other, held, sems, emit)
    for copy in ahead:
        copy.wait()


def forward_open(where, p0, p1, p2, mine, other):
    rows, cols = p0.shape
    units = mine.shape[1]
    blocks = pltpu.VMEM((2, cols, units), jnp.bfloat16)
    return call(
        open_kernel,
        [array((rows, units), jnp.float32)] * 2 + [blocks] * 2,
        [SMEM] + [VMEM] * 3 + [HBM] * 2,
        [VMEM] * 4,
        "forward_open",
        [pltpu.VMEM((3, 2, cols, units), jnp.bfloat16), pltpu.SemaphoreType.DMA((5, 2))],
    )(where, p0, p1, p2, in_hbm(mine), in_hbm(other))


def close_kernel(p3, weights, keep, send, out, sent):
    sent[...] = send[...] + dot(p3[...], weights[1])
    out[...] = keep[...] + dot(p3[...], weights[0])


def forward_close(p3, weights, keep, send):
    return call(
        close_kernel,
        [array(keep.shape, jnp.float32)] * 2,
        [VMEM] * 4,
        [VMEM] * 2,
        "forward_close",
    )(p3, weights, keep, send)


def slot_kernel(weights, dz_t, dzo_t, out):
    out[...] = low(dot(weights[0], dz_t[...]) + dot(weights[1], dzo_t[...]))


def first_slot(weights, dz_t, dzo_t):
    return call(
        slot_kernel,
        array((weights.shape[1], dz_t.shape[1]), jnp.bfloat16),
        [VMEM] * 3,
        VMEM,
        "first_slot",
    )(weights, dz_t, dzo_t)


def tower_math(pre, bias, unit_a, unit_b, upper_a, upper_b, dz, dz_t, sums):
    pre = pre + bias[...]
    sigma = jax.nn.sigmoid(pre)
    hidden = pre * sigma
    cot_a = wide(upper_a[...])
    cot_b = wide(upper_b[...])
    dhid = unit_a[...] * cot_a + unit_b[...] * cot_b
    dpre = dhid * (sigma * (1.0 + pre * (1.0 - sigma)))
    dz[...] = low(dpre)
    dz_t[...] = low(dpre).T
    sums[0:1, :] = jnp.sum(dpre, axis=0, keepdims=True)
    sums[1:2, :] = jnp.sum(cot_a * hidden, axis=0, keepdims=True)
    sums[2:3, :] = jnp.sum(cot_b * hidden, axis=0, keepdims=True)
    sums[3:4, :] = jnp.zeros_like(sums[3:4, :])
    return hidden


def first_kernel(own, got, bias, stitch, upper_a, upper_b, dz, dz_t, sums, hidden):
    hidden[...] = tower_math(
        own[...] + got[...],
        bias[0:1, :],
        stitch[0:1, :],
        stitch[2:3, :],
        upper_a,
        upper_b,
        dz,
        dz_t,
        sums,
    )


def second_kernel(own, got, earlier, bias, stitch, upper_a, upper_b, dz, dz_t, sums, local):
    hidden = tower_math(
        own[...] + got[...],
        bias[1:2, :],
        stitch[1:2, :],
        stitch[3:4, :],
        upper_a,
        upper_b,
        dz,
        dz_t,
        sums,
    )
    rows = hidden.shape[0]
    before = earlier[...]
    local[0:rows, :] = low(stitch[0:1, :] * before + stitch[1:2, :] * hidden)
    local[rows : 2 * rows, :] = low(stitch[2:3, :] * before + stitch[3:4, :] * hidden)


def tower(kernel, name, last, *operands):
    rows, units = operands[0].shape
    return call(
        kernel,
        [
            array((rows, units), jnp.bfloat16),
            array((units, rows), jnp.bfloat16),
            array((4, units), jnp.float32),
            last,
        ],
        [VMEM] * len(operands),
        [VMEM] * 4,
        name,
    )(*operands)


def part_kernel(slots, where, mine, other, dz_t, dzo_t, *refs):
    *outs, held, sems = refs
    cols = held.shape[2]

    def emit(i, own_block, other_block):
        _, at, block = slots[i]
        total = dot(own_block, dz_t[...]) + dot(other_block, dzo_t[...])
        outs[at][block * cols : (block + 1) * cols, :] = total.astype(outs[at].dtype)

    products(where, [where[3 + slot] for slot, _, _ in slots], mine, other, held, sems, emit)


def parts(slots, outs, where, mine, other, dz_t, dzo_t):
    units, rows = dz_t.shape
    cols = mine.shape[0] // 8
    return call(
        functools.partial(part_kernel, slots),
        [array((blocks * cols, rows), dtype) for blocks, dtype in outs],
        [SMEM, HBM, HBM, VMEM, VMEM],
        [VMEM] * len(outs),
        "parts",
        [
            pltpu.VMEM((len(slots), 2, cols, units), jnp.bfloat16),
            pltpu.SemaphoreType.DMA((len(slots), 2)),
        ],
    )(where, in_hbm(mine), in_hbm(other), dz_t, dzo_t)


def choose_kernel(where, at_end, in_middle, out, sem):
    for flag, source in enumerate((at_end, in_middle)):
        pl.when(where[2] == flag)(pltpu.make_async_copy(source, out, sem).start)
    pltpu.make_async_copy(at_end, out, sem).wait()


def choose(where, at_end, in_middle):
    return call(
        choose_kernel,
        array(at_end.shape, at_end.dtype),
        [SMEM, ANY, ANY],
        VMEM,
        "choose",
        [pltpu.SemaphoreType.DMA],
    )(where, at_end, in_middle)


def join_kernel(where, one, at_end, in_middle, out, sems):
    rows = one.shape[0]
    copies = [pltpu.make_async_copy(one, out.at[pl.ds(0, rows), :], sems.at[0])]
    copies[0].start()
    rest = out.at[pl.ds(rows, rows), :]
    for flag, source in enumerate((at_end, in_middle)):
        pl.when(where[2] == flag)(pltpu.make_async_copy(source, rest, sems.at[1]).start)
    copies[0].wait()
    pltpu.make_async_copy(at_end, rest, sems.at[1]).wait()


def join(where, one, at_end, in_middle):
    rows, cols = one.shape
    return call(
        join_kernel,
        array((2 * rows, cols), one.dtype),
        [SMEM] + [ANY] * 3,
        VMEM,
        "join",
        [pltpu.SemaphoreType.DMA((2,))],
    )(where, one, at_end, in_middle)


def lay_kernel(where, low, high, far_low, far_high, out_a, out_b, stage, sems):
    rows = out_a.shape[0]
    units = low.shape[1]
    pieces = []
    for side, (first, second) in enumerate(((low, high), (far_low, far_high))):
        for k in range(4):
            block = 2 * (where[0] ^ k) + (where[1] ^ side)
            lanes = pl.ds(pl.multiple_of(block * units, units), units)
            source = (first, second)[k // 2]
            for half in range(2):
                at = pl.ds((2 * (k % 2) + half) * rows, rows)
                sem = sems.at[half, 4 * side + k]
                pieces.append(
                    pltpu.make_async_copy(source.at[at, :], stage.at[half, :, lanes], sem)
                )
    gives = [
        pltpu.make_async_copy(stage.at[half], out, sems.at[half, 8])
        for half, out in enumerate((out_a, out_b))
    ]
    for copy in pieces:
        copy.start()
    for half in range(2):
        for copy in pieces[half::2]:
            copy.wait()
        gives[half].start()
    for give in gives:
        give.wait()


def lay_out(where, low, high, far_low, far_high):
    rows, units = low.shape[0] // 4, low.shape[1]
    stitched = pltpu.HBM((rows, 8 * units), jnp.bfloat16)
    return call(
        lay_kernel,
        [stitched, stitched],
        [SMEM] + [ANY] * 4,
        [HBM] * 2,
        "lay_out",
        [
            pltpu.VMEM((2, rows, 8 * units), jnp.bfloat16),
            pltpu.SemaphoreType.DMA((2, 9)),
        ],
    )(where, low, high, far_low, far_high)


def add_kernel(at, one, two, out):
    rows = out.shape[0]
    out[...] = low(wide(one[at : at + rows, :]) + wide(two[0:rows, :]))


def add(one, two, block=0, rows=None):
    rows = rows or min(one.shape[0], two.shape[0])
    return call(
        functools.partial(add_kernel, block * rows),
        array((rows, one.shape[1]), jnp.bfloat16),
        [VMEM, VMEM],
        VMEM,
        "add",
    )(one, two)


def finish_kernel(where, marks, group, kept, third, cross, last, out, held, own, sems):
    second = group[...] == 1
    cols = out.shape[0]
    copies = [pltpu.make_async_copy(kept, own, sems.at[3])]
    for n, source in enumerate((third, cross, last)):
        copies.append(pltpu.make_async_copy(source, held.at[n], sems.at[n]))
    for copy in copies:
        copy.start()
    for copy in copies:
        copy.wait()
    for chunk in range(cols // LANES):
        zero, one = marks_of(marks, where[8], cols, chunk)
        keep = wide(jnp.where(second, one, zero))
        rows = slice(chunk * LANES, (chunk + 1) * LANES)
        total = own[rows, :] + wide(held[0, rows, :])
        total += wide(held[1, rows, :]) + wide(held[2, rows, :])
        out[rows, :] = low(total * keep)


def finish(where, marks, group, kept, third, cross, last):
    return call(
        finish_kernel,
        array(kept.shape, jnp.bfloat16),
        [SMEM, SMEM, VMEM] + [HBM] * 4,
        VMEM,
        "finish",
        [
            pltpu.VMEM((3, *kept.shape), jnp.bfloat16),
            pltpu.VMEM(kept.shape, jnp.float32),
            pltpu.SemaphoreType.DMA((4,)),
        ],
    )(where, marks, group, *[in_hbm(x) for x in (kept, third, cross, last)])


def pack_kernel(where, p0, p1, p2, p3, dz, sums, given, out, sems):
    rows, units = dz.shape
    cols = p0.shape[1]
    for q in range(4):
        block = out.at[q, pl.ds(0, rows), pl.ds(0, cols)]
        for index, piece in enumerate((p0, p1, p2, p3)):
            start = pltpu.make_async_copy(piece, block, sems.at[q]).start
            pl.when(where[0] ^ q == index)(start)
    extra = jnp.zeros((EXTRA, cols + units), jnp.bfloat16)
    for q in range(4):
        out[q, rows : rows + EXTRA, :] = extra
        out[q, 0:rows, cols : cols + units] = dz[...]
    for k in range(3):
        rest = sums[k : k + 1, :]
        for term in range(3):
            piece = low(rest)
            row = rows + 3 * k + term
            for q in range(4):
                out[q, row : row + 1, cols : cols + units] = piece
            rest = rest - wide(piece)
    gives = [pltpu.make_async_copy(out.at[q], given.at[q], sems.at[4 + q]) for q in range(4)]
    for q in range(4):
        block = out.at[q, pl.ds(0, rows), pl.ds(0, cols)]
        pltpu.make_async_copy(p0, block, sems.at[q]).wait()
        gives[q].start()
    for give in gives:
        give.wait()


def pack(where, pieces, dz, sums):
    rows, units = dz.shape
    cols = pieces[0].shape[1]
    return call(
        pack_kernel,
        pltpu.HBM((4, rows + EXTRA, cols + units), jnp.bfloat16),
        [SMEM] + [ANY] * 4 + [VMEM] * 2,
        HBM,
        "pack",
        [
            pltpu.VMEM((4, rows + EXTRA, cols + units), jnp.bfloat16),
            pltpu.SemaphoreType.DMA((8,)),
        ],
    )(where, *pieces, dz, sums)


def weight_kernel(sides, where, *refs):
    n = len(sides)
    images_of, dz_of = refs[:n], refs[n]
    *outs, images, dzs, tiles, sems = refs[n + 1 + (sides == (1,)) :]
    out = outs[0]
    rows, units = dzs.shape[1:]
    cols = images.shape[3]
    tile = tiles.shape[1]
    steps = cols // tile

    def fetch(q):
        source = dz_of.at[q, pl.ds(0, rows), pl.ds(cols, units)]
        return pltpu.make_async_copy(source, dzs.at[q], sems.at[q])

    def block(i, q):
        image = images_of[i].at[q, pl.ds(0, rows), pl.ds(0, cols)]
        return pltpu.make_async_copy(image, images.at[i, q], sems.at[4 + 4 * i + q])

    def give(i, t):
        at = pl.multiple_of((where[1] ^ sides[i]) * cols + t * tile, tile)
        slot = i * steps + t
        return pltpu.make_async_copy(
            tiles.at[slot], out.at[pl.ds(at, tile), :], sems.at[12 + slot]
        )

    for q in range(4):
        fetch(q).start()
    for i in range(n):
        for q in range(4):
            block(i, q).start()
    for q in range(4):
        fetch(q).wait()
    for i in range(n):
        for q in range(4):
            block(i, q).wait()
        if len(outs) > 1:
            for q in range(4):
                pltpu.make_async_copy(images.at[i, q], outs[1].at[q], sems.at[4 + q]).start()
        for t in range(steps):
            total = None
            for q in range(4):
                term = lax.dot_general(
                    images[i, q, :, t * tile : (t + 1) * tile],
                    dzs[q],
                    (((0,), (0,)), ((), ())),
                    preferred_element_type=jnp.float32,
                )
                total = term if total is None else total + term
            tiles[i * steps + t] = total
            give(i, t).start()
    for i in range(n):
        for t in range(steps):
            give(i, t).wait()
    if len(outs) > 1:
        for q in range(4):
            pltpu.make_async_copy(images.at[0, q], outs[1].at[q], sems.at[4 + q]).wait()


def weight_grad(sides, rows, cols, where, images, dz, *before):
    units = dz.shape[2] - cols
    tile = cols // 3
    n = len(sides)
    outs = [pltpu.HBM((2 * cols, units), jnp.float32)]
    if sides == (0,):
        outs.append(pltpu.HBM((4, rows, cols), jnp.bfloat16))
    return call(
        functools.partial(weight_kernel, sides),
        outs if len(outs) > 1 else outs[0],
        [SMEM] + [ANY] * (n + 1) + [HBM] * len(before),
        [HBM] * len(outs) if len(outs) > 1 else HBM,
        "weight_grad",
        [
            pltpu.VMEM((n, 4, rows, cols), jnp.bfloat16),
            pltpu.VMEM((4, rows, units), jnp.bfloat16),
            pltpu.VMEM((3 * n, tile, units), jnp.float32),
            pltpu.SemaphoreType.DMA((18,)),
        ],
        {n + 2: 0} if before else {},
    )(where, *images, dz, *before)


def sums_kernel(rows, cols, got_a, got_b, bias, stitch, terms, sems):
    units = bias.shape[1]
    copies = [
        pltpu.make_async_copy(
            got.at[:, pl.ds(rows, EXTRA), pl.ds(cols, units)], terms.at[side], sems.at[side]
        )
        for side, got in enumerate((got_a, got_b))
    ]
    for copy in copies:
        copy.start()
    for copy in copies:
        copy.wait()
    for side in range(2):
        totals = []
        for k in range(3):
            each = [
                (
                    wide(terms[side, q, 3 * k + 2 : 3 * k + 3, :])
                    + wide(terms[side, q, 3 * k + 1 : 3 * k + 2, :])
                )
                + wide(terms[side, q, 3 * k : 3 * k + 1, :])
                for q in range(4)
            ]
            totals.append((each[0] + each[1]) + (each[2] + each[3]))
        bias[side : side + 1, :] = totals[0]
        stitch[side : side + 1, :] = totals[1]
        stitch[2 + side : 3 + side, :] = totals[2]


def total_sums(rows, cols, got_a, got_b):
    units = got_a.shape[2] - cols
    return call(
        functools.partial(sums_kernel, rows, cols),
        [array((2, units), jnp.float32), array((4, units), jnp.float32)],
        [ANY, ANY],
        [VMEM, VMEM],
        "total_sums",
        [pltpu.VMEM((2, 4, EXTRA, units), jnp.bfloat16), pltpu.SemaphoreType.DMA((2,))],
    )(got_a, got_b)


def swap(x):
    return lax.ppermute(x, "mp", SWAP_CORE)


def along(x):
    return lax.ppermute(x, "mp", NEAR_Z)


def across(x):
    return lax.ppermute(x, "mp", FAR_Z)


def inward(x):
    return lax.ppermute(x, "mp", ENDS_IN)


def between(x):
    return lax.ppermute(x, "mp", MIDS)


def outward(x):
    return lax.ppermute(x, "mp", ENDS_OUT)


def exchange(x):
    return lax.all_to_all(x, "dp", 0, 0)


def fast_shards(
    image_a,
    image_b,
    image_group,
    position_mask,
    weight_a,
    weight_b,
    tower_bias,
    stitch,
    cotan_a,
    cotan_b,
):
    rows, cols = image_a.shape
    units = weight_a.shape[1]
    place = lax.axis_index("mp").astype(jnp.int32)
    z = place // 2
    core = place % 2
    quarter = lax.axis_index("dp").astype(jnp.int32)
    middle = ((z == 1) | (z == 2)).astype(jnp.int32)
    slots = jnp.take(jnp.asarray(SLOTS, jnp.int32), z, axis=0) ^ z
    where = jnp.concatenate(
        [jnp.stack([z, core, middle]), slots, jnp.stack([quarter, place])]
    ).astype(jnp.int32)
    group = image_group[None, :]
    line.token = None
    bf16, f32 = jnp.bfloat16, jnp.float32
    send, wait = line.send, line.wait

    whole_a = swap(weight_a)
    whole_b = swap(weight_b)
    def masked(k, image):
        spot = (2 * (z ^ k) + core)[None]
        return mask_image(spot, position_mask, group, image)

    raw2 = across(image_a)
    raw1 = along(image_a)
    b0 = masked(0, in_hbm(image_b))
    a0 = masked(0, in_hbm(image_a))
    raw1, raw2 = wait(raw1, raw2)
    raw3 = send(along, raw2)
    b_mid = send(between, b0)
    b1 = send(along, b0)
    a1 = masked(1, raw1)
    a2 = masked(2, raw2)
    whole_a, whole_b = wait(whole_a, whole_b)
    keep_a, give_a, last_a, slot_a = forward_open(where, a0, a1, a2, weight_a, whole_a)
    a3 = masked(3, wait(raw3))
    own_a, sent_a = forward_close(a3, last_a, keep_a, give_a)
    got_sum = wait(send(swap, sent_a))
    dz_a, dzt_a, sums_a, hidden_a = tower(
        first_kernel,
        "tower_a",
        array((rows, units), f32),
        own_a,
        got_sum,
        tower_bias,
        stitch,
        cotan_a,
        cotan_b,
    )
    dzo_a = send(swap, dzt_a)
    packed_a = pack(where, (a0, a1, a2, a3), dz_a, sums_a)
    b1, b_mid = wait(b1, b_mid)
    got_a = send(exchange, packed_a)
    b_end = send(outward, b_mid)
    b_mid2 = send(between, b1)
    dzo_a = wait(dzo_a)
    first_a = first_slot(slot_a, dzt_a, dzo_a)
    in1_a = send(inward, first_a)
    second_a, third_a, kept_a = parts(
        ((1, 0, 0), (2, 1, 0), (3, 2, 0)),
        [(1, bf16), (1, bf16), (1, f32)],
        where,
        weight_a,
        whole_a,
        dzt_a,
        dzo_a,
    )
    in2_a = send(inward, second_a)
    b_end, b_mid2 = wait(b_end, b_mid2)
    b_end2 = send(outward, b_mid2)
    b2 = choose(where, b_end, b_mid2)
    keep_b, give_b, last_b, slot_b = forward_open(where, b0, b1, b2, weight_b, whole_b)
    in1_a = wait(in1_a)
    cross1_a = send(between, add(first_a, in1_a))
    b_end2 = wait(b_end2)
    b3 = choose(where, b_end2, b_mid)
    own_b, sent_b = forward_close(b3, last_b, keep_b, give_b)
    got_sum = send(swap, sent_b)
    in2_a = wait(in2_a)
    sum2_a = add(second_a, in2_a)
    got_sum = wait(got_sum)
    dz_b, dzt_b, sums_b, local = tower(
        second_kernel,
        "tower_b",
        array((2 * rows, units), bf16),
        own_b,
        got_sum,
        hidden_a,
        tower_bias,
        stitch,
        cotan_a,
        cotan_b,
    )
    dzo_b = send(swap, dzt_b)
    packed_b = pack(where, (b0, b1, b2, b3), dz_b, sums_b)
    cross1_a = wait(cross1_a)
    sum3_a = add(third_a, cross1_a)
    got_a = wait(got_a)
    far_a = send(swap, got_a)
    got_b = send(exchange, packed_b)
    cross2_a = send(between, sum2_a)
    dzo_b, far_a = wait(dzo_b, far_a)
    first_b = first_slot(slot_b, dzt_b, dzo_b)
    in1_b = send(inward, first_b)
    out_a = send(outward, sum3_a)
    s1 = send(along, local)
    s_mid = send(between, local)
    second_b, third_b, kept_b = parts(
        ((1, 0, 0), (2, 1, 0), (3, 2, 0)),
        [(1, bf16), (1, bf16), (1, f32)],
        where,
        weight_b,
        whole_b,
        dzt_b,
        dzo_b,
    )
    grad_weight_a = weight_grad((0, 1), rows, cols, where, (got_a, far_a), got_a)
    cross2_a, out_a = wait(cross2_a, out_a)
    in1_b = wait(in1_b)
    cross1_b = send(between, add(first_b, in1_b))
    in2_b = send(inward, second_b)
    in3_b = send(inward, third_b)
    s1, s_mid = wait(s1, s_mid)
    s_end = send(outward, s_mid)
    s_mid2 = send(between, s1)
    low_half = join(where, local, s1, s1)
    cross1_b = wait(cross1_b)
    out_b = send(outward, add(third_b, cross1_b))
    in2_b = wait(in2_b)
    cross2_b = send(between, add(second_b, in2_b))
    s_end, s_mid2 = wait(s_end, s_mid2)
    s_end2 = send(outward, s_mid2)
    in3_a = send(inward, third_a)
    s2 = choose(where, s_end, s_mid2)
    got_b = wait(got_b)
    grad_bias, grad_stitch = total_sums(rows, cols, got_a, got_b)
    half_b, block_b = weight_grad((0,), rows, cols, where, (got_b,), got_b)
    in3_b, out_b, cross2_b = wait(in3_b, out_b, cross2_b)
    grad_image_b = finish(where, position_mask, group, kept_b, in3_b, cross2_b, out_b)
    s_end2, in3_a = wait(s_end2, in3_a)
    high = join(where, s2, s_end2, s_mid)
    far_high = send(swap, high)
    far_low = send(swap, low_half)
    far_b = send(swap, block_b)
    grad_image_a = finish(where, position_mask, group, kept_a, in3_a, cross2_a, out_a)
    grad_weight_b = weight_grad((1,), rows, cols, where, (far_b,), got_b, half_b)
    stitched_a, stitched_b = lay_out(where, low_half, high, far_low, far_high)
    return (
        stitched_a,
        stitched_b,
        grad_image_a,
        grad_image_b,
        grad_weight_a,
        grad_weight_b,
        grad_bias,
        grad_stitch,
    )


def solution(mesh):
    placed = (
        P("dp", "mp"),
        P("dp", "mp"),
        P("dp"),
        P(),
        P(None, "mp"),
        P(None, "mp"),
        P(None, "mp"),
        P(None, "mp"),
        P("dp", "mp"),
        P("dp", "mp"),
    )
    fits = mesh.shape["dp"] == 4 and mesh.shape["mp"] == 8
    return jax.shard_map(
        fast_shards if fits else general_shards,
        mesh=mesh,
        in_specs=placed,
        out_specs=(
            P("dp", None),
            P("dp", None),
            P("mp", "dp"),
            P("mp", "dp"),
            P("dp", "mp"),
            P("dp", "mp"),
            P(None, "mp"),
            P(None, "mp"),
        ),
        check_vma=False,
    )
```

```python
import functools

import jax
import jax.numpy as jnp
from jax import lax
from jax.experimental import pallas as pl
from jax.experimental.pallas import tpu as pltpu
from jax.sharding import PartitionSpec as P

CH = 256
POS = 36


def keep_block(image_group, position_mask, first_col, cols):
    positions = (first_col + lax.iota(jnp.int32, cols)) // CH
    onehot = (positions[:, None] == lax.iota(jnp.int32, POS)[None, :]).astype(jnp.float32)
    per_position = jnp.dot(onehot, position_mask.astype(jnp.float32).T)
    return jnp.where(
        image_group[:, None] == 1, per_position[:, 1][None, :], per_position[:, 0][None, :]
    )


def general_shards(
    image_a,
    image_b,
    image_group,
    position_mask,
    weight_a,
    weight_b,
    tower_bias,
    stitch,
    cotan_a,
    cotan_b,
):
    batch_rows = image_a.shape[0]
    shard_cols = image_a.shape[1]
    first_col = lax.axis_index("mp") * shard_cols
    keep_mask = keep_block(image_group, position_mask, first_col, shard_cols)
    keep_low = keep_mask.astype(jnp.bfloat16)
    contract_rows = (((0,), (0,)), ((), ()))
    contract_units = (((1,), (1,)), ((), ()))
    full_a = lax.all_gather(image_a * keep_low, "mp", axis=1, tiled=True)
    full_b = lax.all_gather(image_b * keep_low, "mp", axis=1, tiled=True)
    pre_a = jnp.dot(full_a, weight_a, preferred_element_type=jnp.float32) + tower_bias[0][None, :]
    pre_b = jnp.dot(full_b, weight_b, preferred_element_type=jnp.float32) + tower_bias[1][None, :]
    sigma_a = jax.nn.sigmoid(pre_a)
    sigma_b = jax.nn.sigmoid(pre_b)
    hidden_a = pre_a * sigma_a
    hidden_b = pre_b * sigma_b
    local_a = (stitch[0][None, :] * hidden_a + stitch[1][None, :] * hidden_b).astype(jnp.bfloat16)
    local_b = (stitch[2][None, :] * hidden_a + stitch[3][None, :] * hidden_b).astype(jnp.bfloat16)
    stitched_a = lax.all_gather(local_a, "mp", axis=1, tiled=True)
    stitched_b = lax.all_gather(local_b, "mp", axis=1, tiled=True)
    upper_a = cotan_a.astype(jnp.float32)
    upper_b = cotan_b.astype(jnp.float32)
    dhid_a = stitch[0][None, :] * upper_a + stitch[2][None, :] * upper_b
    dhid_b = stitch[1][None, :] * upper_a + stitch[3][None, :] * upper_b
    dpre_a = dhid_a * (sigma_a * (1.0 + pre_a * (1.0 - sigma_a)))
    dpre_b = dhid_b * (sigma_b * (1.0 + pre_b * (1.0 - sigma_b)))
    bias_terms = jnp.stack([jnp.sum(dpre_a, axis=0), jnp.sum(dpre_b, axis=0)])
    stitch_terms = jnp.stack(
        [
            jnp.sum(upper_a * hidden_a, axis=0),
            jnp.sum(upper_a * hidden_b, axis=0),
            jnp.sum(upper_b * hidden_a, axis=0),
            jnp.sum(upper_b * hidden_b, axis=0),
        ]
    )
    grad_bias, grad_stitch = lax.psum((bias_terms, stitch_terms), "dp")
    dlow_a = dpre_a.astype(jnp.bfloat16)
    dlow_b = dpre_b.astype(jnp.bfloat16)
    block_a = lax.dot_general(full_a, dlow_a, contract_rows, preferred_element_type=jnp.float32)
    block_b = lax.dot_general(full_b, dlow_b, contract_rows, preferred_element_type=jnp.float32)
    grad_weight_a = lax.psum_scatter(block_a, "dp", scatter_dimension=0, tiled=True)
    grad_weight_b = lax.psum_scatter(block_b, "dp", scatter_dimension=0, tiled=True)
    part_a = lax.dot_general(weight_a, dlow_a, contract_units, preferred_element_type=jnp.float32)
    part_b = lax.dot_general(weight_b, dlow_b, contract_units, preferred_element_type=jnp.float32)
    summed = lax.psum_scatter(
        jnp.concatenate([part_a, part_b], axis=1), "mp", scatter_dimension=0, tiled=True
    )
    keep_cols = keep_mask.T
    grad_image_a = (summed[:, :batch_rows] * keep_cols).astype(jnp.bfloat16)
    grad_image_b = (summed[:, batch_rows:] * keep_cols).astype(jnp.bfloat16)
    return (
        stitched_a,
        stitched_b,
        grad_image_a,
        grad_image_b,
        grad_weight_a,
        grad_weight_b,
        grad_bias,
        grad_stitch,
    )


SWAP_CORE = [(d, d ^ 1) for d in range(8)]
NEAR_Z = [(d, d ^ 2) for d in range(8)]
FAR_Z = [(d, d ^ 4) for d in range(8)]
ENDS_IN = [(0, 2), (1, 3), (6, 4), (7, 5)]
MIDS = [(2, 4), (3, 5), (4, 2), (5, 3)]
ENDS_OUT = [(2, 0), (3, 1), (4, 6), (5, 7)]
SLOTS = ((3, 2, 1, 0), (3, 2, 0, 1), (0, 1, 3, 2), (0, 1, 2, 3))
LANES = 128
EXTRA = 16
VMEM_LIMIT = 22 * 1024 * 1024
SMEM = pl.BlockSpec(memory_space=pltpu.SMEM)
VMEM = pl.BlockSpec(memory_space=pltpu.VMEM)
HBM = pl.BlockSpec(memory_space=pltpu.HBM)
ANY = pl.BlockSpec(memory_space=pl.ANY)
LITTLE = pl.CostEstimate(flops=1, bytes_accessed=1, transcendentals=0)


def low(x):
    return x.astype(jnp.bfloat16)


def wide(x):
    return x.astype(jnp.float32)


def array(shape, dtype):
    return jax.ShapeDtypeStruct(shape, dtype)


def far_array(shape, dtype):
    return pltpu.HBM(shape, dtype)


class Line:
    def __init__(self):
        self.token = None

    def tie(self, *xs):
        if self.token is None:
            return xs
        *xs, self.token = lax.optimization_barrier((*xs, self.token))
        return xs

    def wait(self, *arrived):
        arrived = self.tie(*arrived)
        return arrived if len(arrived) > 1 else arrived[0]

    def send(self, move, x):
        return move(*self.tie(x))


line = Line()


def call(kernel, out_shape, in_specs, out_specs, name, scratch=(), aliases={}):
    single = not isinstance(out_shape, list)
    outs = [out_shape] if single else out_shape
    places = [out_specs] if single else out_specs
    n_in, n_out = len(in_specs), len(outs)
    before = () if line.token is None else (line.token,)

    def body(*refs):
        start = n_in + len(before)
        refs[start + n_out][...] = jnp.zeros((8, LANES), jnp.float32)
        kernel(*refs[:n_in], *refs[start : start + n_out], *refs[start + n_out + 1 :])

    run = pl.pallas_call(
        body,
        out_shape=[*outs, array((8, LANES), jnp.float32)],
        in_specs=[*in_specs, *[HBM] * len(before)],
        out_specs=[*places, VMEM],
        scratch_shapes=scratch,
        input_output_aliases=aliases,
        compiler_params=pltpu.CompilerParams(vmem_limit_bytes=VMEM_LIMIT),
        cost_estimate=LITTLE,
        name=name,
    )

    def go(*operands):
        *results, line.token = run(*operands, *before)
        return results[0] if single else results

    return go


def marks_of(marks, place, cols, chunk):
    position = (place * cols + chunk * LANES) // CH
    return marks[0, position], marks[1, position]


def mask_kernel(place, marks, group, image, out, held, sem):
    rows, cols = image.shape
    copy = pltpu.make_async_copy(image, held, sem)
    copy.start()
    second = jnp.broadcast_to(jnp.where(group[...] == 1, 1.0, 0.0), (8, rows)).T[:, 0:1] > 0.5
    copy.wait()
    for chunk in range(cols // LANES):
        zero, one = marks_of(marks, place[0], cols, chunk)
        keep = wide(jnp.where(second, one, zero))
        lanes = slice(chunk * LANES, (chunk + 1) * LANES)
        out[:, lanes] = low(wide(held[:, lanes]) * keep)


def mask_image(place, marks, group, image):
    return call(
        mask_kernel,
        array(image.shape, jnp.bfloat16),
        [SMEM, SMEM, VMEM, ANY],
        VMEM,
        "mask_image",
        [pltpu.VMEM(image.shape, jnp.bfloat16), pltpu.SemaphoreType.DMA],
    )(place, marks, group, image)


def in_hbm(x):
    return pltpu.with_memory_space_constraint(x, pltpu.HBM)


def dot(x, y):
    return jnp.dot(x, y, preferred_element_type=jnp.float32)


def products(where, ks, mine, other, held, sems, emit):
    cols = held.shape[2]

    def copies(i):
        block = 2 * (where[0] ^ ks[i]) + where[1]
        rows = pl.ds(pl.multiple_of(block * cols, cols), cols)
        return [
            pltpu.make_async_copy(weight.at[rows, :], held.at[i, side], sems.at[i, side])
            for side, weight in enumerate((mine, other))
        ]

    for i in range(len(ks)):
        for copy in copies(i):
            copy.start()
    for i in range(len(ks)):
        for copy in copies(i):
            copy.wait()
        emit(i, held[i, 0], held[i, 1])


def open_kernel(where, p0, p1, p2, mine, other, keep, send, last, slot, held, sems):
    pieces = (p0, p1, p2)
    cols = p0.shape[1]
    ahead = []
    for at, (k, out) in enumerate(((3, last), (where[3], slot))):
        block = 2 * (where[0] ^ k) + where[1]
        rows = pl.ds(pl.multiple_of(block * cols, cols), cols)
        for side, weight in enumerate((mine, other)):
            ahead.append(
                pltpu.make_async_copy(weight.at[rows, :], out.at[side], sems.at[3 + at, side])
            )

    def emit(i, own_block, other_block):
        if i == 0:
            for copy in ahead:
                copy.start()
            keep[...] = dot(p0[...], own_block)
            send[...] = dot(p0[...], other_block)
        else:
            keep[...] += dot(pieces[i][...], own_block)
            send[...] += dot(pieces[i][...], other_block)

    products(where, (0, 1, 2), mine, other, held, sems, emit)
    for copy in ahead:
        copy.wait()


def forward_open(where, p0, p1, p2, mine, other):
    rows, cols = p0.shape
    units = mine.shape[1]
    blocks = pltpu.VMEM((2, cols, units), jnp.bfloat16)
    return call(
        open_kernel,
        [array((rows, units), jnp.float32)] * 2 + [blocks] * 2,
        [SMEM] + [VMEM] * 3 + [HBM] * 2,
        [VMEM] * 4,
        "forward_open",
        [pltpu.VMEM((3, 2, cols, units), jnp.bfloat16), pltpu.SemaphoreType.DMA((5, 2))],
    )(where, p0, p1, p2, in_hbm(mine), in_hbm(other))


def close_kernel(p3, weights, keep, send, out, sent):
    sent[...] = send[...] + dot(p3[...], weights[1])
    out[...] = keep[...] + dot(p3[...], weights[0])


def forward_close(p3, weights, keep, send):
    return call(
        close_kernel,
        [array(keep.shape, jnp.float32)] * 2,
        [VMEM] * 4,
        [VMEM] * 2,
        "forward_close",
    )(p3, weights, keep, send)


def slot_kernel(weights, dz_t, dzo_t, out):
    out[...] = low(dot(weights[0], dz_t[...]) + dot(weights[1], dzo_t[...]))


def first_slot(weights, dz_t, dzo_t):
    return call(
        slot_kernel,
        array((weights.shape[1], dz_t.shape[1]), jnp.bfloat16),
        [VMEM] * 3,
        VMEM,
        "first_slot",
    )(weights, dz_t, dzo_t)


def tower_math(pre, bias, unit_a, unit_b, upper_a, upper_b, dz, dz_t, sums):
    pre = pre + bias[...]
    sigma = jax.nn.sigmoid(pre)
    hidden = pre * sigma
    cot_a = wide(upper_a[...])
    cot_b = wide(upper_b[...])
    dhid = unit_a[...] * cot_a + unit_b[...] * cot_b
    dpre = dhid * (sigma * (1.0 + pre * (1.0 - sigma)))
    dz[...] = low(dpre)
    dz_t[...] = low(dpre).T
    sums[0:1, :] = jnp.sum(dpre, axis=0, keepdims=True)
    sums[1:2, :] = jnp.sum(cot_a * hidden, axis=0, keepdims=True)
    sums[2:3, :] = jnp.sum(cot_b * hidden, axis=0, keepdims=True)
    sums[3:4, :] = jnp.zeros_like(sums[3:4, :])
    return hidden


def first_kernel(own, got, bias, stitch, upper_a, upper_b, dz, dz_t, sums, hidden):
    hidden[...] = tower_math(
        own[...] + got[...],
        bias[0:1, :],
        stitch[0:1, :],
        stitch[2:3, :],
        upper_a,
        upper_b,
        dz,
        dz_t,
        sums,
    )


def second_kernel(own, got, earlier, bias, stitch, upper_a, upper_b, dz, dz_t, sums, local):
    hidden = tower_math(
        own[...] + got[...],
        bias[1:2, :],
        stitch[1:2, :],
        stitch[3:4, :],
        upper_a,
        upper_b,
        dz,
        dz_t,
        sums,
    )
    rows = hidden.shape[0]
    before = earlier[...]
    local[0:rows, :] = low(stitch[0:1, :] * before + stitch[1:2, :] * hidden)
    local[rows : 2 * rows, :] = low(stitch[2:3, :] * before + stitch[3:4, :] * hidden)


def tower(kernel, name, last, *operands):
    rows, units = operands[0].shape
    return call(
        kernel,
        [
            array((rows, units), jnp.bfloat16),
            far_array((units, rows), jnp.bfloat16),
            array((4, units), jnp.float32),
            last,
        ],
        [VMEM] * len(operands),
        [VMEM] * 4,
        name,
    )(*operands)


def part_kernel(slots, where, mine, other, dz_t, dzo_t, *refs):
    *outs, held, sems = refs
    cols = held.shape[2]

    def emit(i, own_block, other_block):
        _, at, block = slots[i]
        total = dot(own_block, dz_t[...]) + dot(other_block, dzo_t[...])
        outs[at][block * cols : (block + 1) * cols, :] = total.astype(outs[at].dtype)

    products(where, [where[3 + slot] for slot, _, _ in slots], mine, other, held, sems, emit)


def parts(slots, outs, where, mine, other, dz_t, dzo_t):
    units, rows = dz_t.shape
    cols = mine.shape[0] // 8
    return call(
        functools.partial(part_kernel, slots),
        [far_array((blocks * cols, rows), dtype) for blocks, dtype in outs],
        [SMEM, HBM, HBM, VMEM, VMEM],
        [VMEM] * len(outs),
        "parts",
        [
            pltpu.VMEM((len(slots), 2, cols, units), jnp.bfloat16),
            pltpu.SemaphoreType.DMA((len(slots), 2)),
        ],
    )(where, in_hbm(mine), in_hbm(other), dz_t, dzo_t)


def choose_kernel(where, at_end, in_middle, out, sem):
    for flag, source in enumerate((at_end, in_middle)):
        pl.when(where[2] == flag)(pltpu.make_async_copy(source, out, sem).start)
    pltpu.make_async_copy(at_end, out, sem).wait()


def choose(where, at_end, in_middle):
    return call(
        choose_kernel,
        array(at_end.shape, at_end.dtype),
        [SMEM, ANY, ANY],
        VMEM,
        "choose",
        [pltpu.SemaphoreType.DMA],
    )(where, at_end, in_middle)


def join_kernel(where, one, at_end, in_middle, out, sems):
    rows = one.shape[0]
    copies = [pltpu.make_async_copy(one, out.at[pl.ds(0, rows), :], sems.at[0])]
    copies[0].start()
    rest = out.at[pl.ds(rows, rows), :]
    for flag, source in enumerate((at_end, in_middle)):
        pl.when(where[2] == flag)(pltpu.make_async_copy(source, rest, sems.at[1]).start)
    copies[0].wait()
    pltpu.make_async_copy(at_end, rest, sems.at[1]).wait()


def join(where, one, at_end, in_middle):
    rows, cols = one.shape
    return call(
        join_kernel,
        array((2 * rows, cols), one.dtype),
        [SMEM] + [ANY] * 3,
        VMEM,
        "join",
        [pltpu.SemaphoreType.DMA((2,))],
    )(where, one, at_end, in_middle)


def lay_kernel(where, low, high, far_low, far_high, out_a, out_b, stage, sems):
    rows = out_a.shape[0]
    units = low.shape[1]
    pieces = []
    for side, (first, second) in enumerate(((low, high), (far_low, far_high))):
        for k in range(4):
            block = 2 * (where[0] ^ k) + (where[1] ^ side)
            lanes = pl.ds(pl.multiple_of(block * units, units), units)
            source = (first, second)[k // 2]
            for half in range(2):
                at = pl.ds((2 * (k % 2) + half) * rows, rows)
                sem = sems.at[half, 4 * side + k]
                pieces.append(
                    pltpu.make_async_copy(source.at[at, :], stage.at[half, :, lanes], sem)
                )
    gives = [
        pltpu.make_async_copy(stage.at[half], out, sems.at[half, 8])
        for half, out in enumerate((out_a, out_b))
    ]
    for copy in pieces:
        copy.start()
    for half in range(2):
        for copy in pieces[half::2]:
            copy.wait()
        gives[half].start()
    for give in gives:
        give.wait()


def lay_out(where, low, high, far_low, far_high):
    rows, units = low.shape[0] // 4, low.shape[1]
    stitched = pltpu.HBM((rows, 8 * units), jnp.bfloat16)
    return call(
        lay_kernel,
        [stitched, stitched],
        [SMEM] + [ANY] * 4,
        [HBM] * 2,
        "lay_out",
        [
            pltpu.VMEM((2, rows, 8 * units), jnp.bfloat16),
            pltpu.SemaphoreType.DMA((2, 9)),
        ],
    )(where, low, high, far_low, far_high)


def add_kernel(at, one, two, out):
    rows = out.shape[0]
    out[...] = low(wide(one[at : at + rows, :]) + wide(two[0:rows, :]))


def add(one, two, block=0, rows=None):
    rows = rows or min(one.shape[0], two.shape[0])
    return call(
        functools.partial(add_kernel, block * rows),
        far_array((rows, one.shape[1]), jnp.bfloat16),
        [VMEM, VMEM],
        VMEM,
        "add",
    )(one, two)


def finish_kernel(where, marks, group, kept, third, cross, last, out, held, own, done, sems):
    second = group[...] == 1
    cols = own.shape[0]
    tile = cols // 3

    def fetch(t):
        rows = pl.ds(t * tile, tile)
        copies = [pltpu.make_async_copy(kept.at[rows, :], own.at[rows, :], sems.at[t, 3])]
        for n, source in enumerate((third, cross, last)):
            copies.append(
                pltpu.make_async_copy(source.at[rows, :], held.at[n, rows, :], sems.at[t, n])
            )
        return copies

    def give(t):
        rows = pl.ds(t * tile, tile)
        return pltpu.make_async_copy(done.at[rows, :], out.at[rows, :], sems.at[t, 4])

    for t in range(3):
        for copy in fetch(t):
            copy.start()
    for t in range(3):
        for copy in fetch(t):
            copy.wait()
        for chunk in range(t * tile // LANES, (t + 1) * tile // LANES):
            zero, one = marks_of(marks, where[8], cols, chunk)
            keep = wide(jnp.where(second, one, zero))
            rows = slice(chunk * LANES, (chunk + 1) * LANES)
            total = own[rows, :] + wide(held[0, rows, :])
            total += wide(held[1, rows, :]) + wide(held[2, rows, :])
            done[rows, :] = low(total * keep)
        give(t).start()
    for t in range(3):
        give(t).wait()


def finish(where, marks, group, kept, third, cross, last):
    return call(
        finish_kernel,
        pltpu.HBM(kept.shape, jnp.bfloat16),
        [SMEM, SMEM, VMEM] + [HBM] * 4,
        HBM,
        "finish",
        [
            pltpu.VMEM((3, *kept.shape), jnp.bfloat16),
            pltpu.VMEM(kept.shape, jnp.float32),
            pltpu.VMEM(kept.shape, jnp.bfloat16),
            pltpu.SemaphoreType.DMA((3, 5)),
        ],
    )(where, marks, group, *[in_hbm(x) for x in (kept, third, cross, last)])


def pack_kernel(where, p0, p1, p2, p3, dz, sums, given, out, sems):
    rows, units = dz.shape
    cols = p0.shape[1]
    for q in range(4):
        block = out.at[q, pl.ds(0, rows), pl.ds(0, cols)]
        for index, piece in enumerate((p0, p1, p2, p3)):
            start = pltpu.make_async_copy(piece, block, sems.at[q]).start
            pl.when(where[0] ^ q == index)(start)
    extra = jnp.zeros((EXTRA, cols + units), jnp.bfloat16)
    for q in range(4):
        out[q, rows : rows + EXTRA, :] = extra
        out[q, 0:rows, cols : cols + units] = dz[...]
    for k in range(3):
        rest = sums[k : k + 1, :]
        for term in range(3):
            piece = low(rest)
            row = rows + 3 * k + term
            for q in range(4):
                out[q, row : row + 1, cols : cols + units] = piece
            rest = rest - wide(piece)
    gives = [pltpu.make_async_copy(out.at[q], given.at[q], sems.at[4 + q]) for q in range(4)]
    for q in range(4):
        block = out.at[q, pl.ds(0, rows), pl.ds(0, cols)]
        pltpu.make_async_copy(p0, block, sems.at[q]).wait()
        gives[q].start()
    for give in gives:
        give.wait()


def pack(where, pieces, dz, sums):
    rows, units = dz.shape
    cols = pieces[0].shape[1]
    return call(
        pack_kernel,
        pltpu.HBM((4, rows + EXTRA, cols + units), jnp.bfloat16),
        [SMEM] + [ANY] * 4 + [VMEM] * 2,
        HBM,
        "pack",
        [
            pltpu.VMEM((4, rows + EXTRA, cols + units), jnp.bfloat16),
            pltpu.SemaphoreType.DMA((8,)),
        ],
    )(where, *pieces, dz, sums)


def weight_kernel(sides, where, *refs):
    n = len(sides)
    images_of, dz_of = refs[:n], refs[n]
    *outs, images, dzs, tiles, sems = refs[n + 1 + (sides == (1,)) :]
    out = outs[0]
    rows, units = dzs.shape[1:]
    cols = images.shape[3]
    tile = tiles.shape[1]
    steps = cols // tile

    def fetch(q):
        source = dz_of.at[q, pl.ds(0, rows), pl.ds(cols, units)]
        return pltpu.make_async_copy(source, dzs.at[q], sems.at[q])

    def block(i, q):
        image = images_of[i].at[q, pl.ds(0, rows), pl.ds(0, cols)]
        return pltpu.make_async_copy(image, images.at[i, q], sems.at[4 + 4 * i + q])

    def give(i, t):
        at = pl.multiple_of((where[1] ^ sides[i]) * cols + t * tile, tile)
        slot = i * steps + t
        return pltpu.make_async_copy(
            tiles.at[slot], out.at[pl.ds(at, tile), :], sems.at[12 + slot]
        )

    for q in range(4):
        fetch(q).start()
    for i in range(n):
        for q in range(4):
            block(i, q).start()
    for q in range(4):
        fetch(q).wait()
    for i in range(n):
        for q in range(4):
            block(i, q).wait()
        if len(outs) > 1:
            for q in range(4):
                pltpu.make_async_copy(images.at[i, q], outs[1].at[q], sems.at[4 + q]).start()
        for t in range(steps):
            total = None
            for q in range(4):
                term = lax.dot_general(
                    images[i, q, :, t * tile : (t + 1) * tile],
                    dzs[q],
                    (((0,), (0,)), ((), ())),
                    preferred_element_type=jnp.float32,
                )
                total = term if total is None else total + term
            tiles[i * steps + t] = total
            give(i, t).start()
    for i in range(n):
        for t in range(steps):
            give(i, t).wait()
    if len(outs) > 1:
        for q in range(4):
            pltpu.make_async_copy(images.at[0, q], outs[1].at[q], sems.at[4 + q]).wait()


def weight_grad(sides, rows, cols, where, images, dz, *before):
    units = dz.shape[2] - cols
    tile = cols // 3
    n = len(sides)
    outs = [pltpu.HBM((2 * cols, units), jnp.float32)]
    if sides == (0,):
        outs.append(pltpu.HBM((4, rows, cols), jnp.bfloat16))
    return call(
        functools.partial(weight_kernel, sides),
        outs if len(outs) > 1 else outs[0],
        [SMEM] + [ANY] * (n + 1) + [HBM] * len(before),
        [HBM] * len(outs) if len(outs) > 1 else HBM,
        "weight_grad",
        [
            pltpu.VMEM((n, 4, rows, cols), jnp.bfloat16),
            pltpu.VMEM((4, rows, units), jnp.bfloat16),
            pltpu.VMEM((3 * n, tile, units), jnp.float32),
            pltpu.SemaphoreType.DMA((18,)),
        ],
        {n + 2: 0} if before else {},
    )(where, *images, dz, *before)


def sums_kernel(rows, cols, got_a, got_b, bias, stitch, terms, sems):
    units = bias.shape[1]
    copies = [
        pltpu.make_async_copy(
            got.at[:, pl.ds(rows, EXTRA), pl.ds(cols, units)], terms.at[side], sems.at[side]
        )
        for side, got in enumerate((got_a, got_b))
    ]
    for copy in copies:
        copy.start()
    for copy in copies:
        copy.wait()
    for side in range(2):
        totals = []
        for k in range(3):
            each = [
                (
                    wide(terms[side, q, 3 * k + 2 : 3 * k + 3, :])
                    + wide(terms[side, q, 3 * k + 1 : 3 * k + 2, :])
                )
                + wide(terms[side, q, 3 * k : 3 * k + 1, :])
                for q in range(4)
            ]
            totals.append((each[0] + each[1]) + (each[2] + each[3]))
        bias[side : side + 1, :] = totals[0]
        stitch[side : side + 1, :] = totals[1]
        stitch[2 + side : 3 + side, :] = totals[2]


def total_sums(rows, cols, got_a, got_b):
    units = got_a.shape[2] - cols
    return call(
        functools.partial(sums_kernel, rows, cols),
        [array((2, units), jnp.float32), array((4, units), jnp.float32)],
        [ANY, ANY],
        [VMEM, VMEM],
        "total_sums",
        [pltpu.VMEM((2, 4, EXTRA, units), jnp.bfloat16), pltpu.SemaphoreType.DMA((2,))],
    )(got_a, got_b)


def swap(x):
    return lax.ppermute(x, "mp", SWAP_CORE)


def along(x):
    return lax.ppermute(x, "mp", NEAR_Z)


def across(x):
    return lax.ppermute(x, "mp", FAR_Z)


def inward(x):
    return lax.ppermute(x, "mp", ENDS_IN)


def between(x):
    return lax.ppermute(x, "mp", MIDS)


def outward(x):
    return lax.ppermute(x, "mp", ENDS_OUT)


def exchange(x):
    return lax.all_to_all(x, "dp", 0, 0)


def fast_shards(
    image_a,
    image_b,
    image_group,
    position_mask,
    weight_a,
    weight_b,
    tower_bias,
    stitch,
    cotan_a,
    cotan_b,
):
    rows, cols = image_a.shape
    units = weight_a.shape[1]
    place = lax.axis_index("mp").astype(jnp.int32)
    z = place // 2
    core = place % 2
    quarter = lax.axis_index("dp").astype(jnp.int32)
    middle = ((z == 1) | (z == 2)).astype(jnp.int32)
    slots = jnp.take(jnp.asarray(SLOTS, jnp.int32), z, axis=0) ^ z
    where = jnp.concatenate(
        [jnp.stack([z, core, middle]), slots, jnp.stack([quarter, place])]
    ).astype(jnp.int32)
    group = image_group[None, :]
    line.token = None
    bf16, f32 = jnp.bfloat16, jnp.float32
    send, wait = line.send, line.wait

    whole_a = swap(weight_a)
    whole_b = swap(weight_b)
    def masked(k, image):
        spot = (2 * (z ^ k) + core)[None]
        return mask_image(spot, position_mask, group, image)

    raw2 = across(image_a)
    raw1 = along(image_a)
    b0 = masked(0, in_hbm(image_b))
    a0 = masked(0, in_hbm(image_a))
    raw1, raw2 = wait(raw1, raw2)
    raw3 = send(along, raw2)
    b_mid = send(between, b0)
    b1 = send(along, b0)
    a1 = masked(1, raw1)
    a2 = masked(2, raw2)
    whole_a, whole_b = wait(whole_a, whole_b)
    keep_a, give_a, last_a, slot_a = forward_open(where, a0, a1, a2, weight_a, whole_a)
    a3 = masked(3, wait(raw3))
    own_a, sent_a = forward_close(a3, last_a, keep_a, give_a)
    got_sum = wait(send(swap, sent_a))
    dz_a, dzt_a, sums_a, hidden_a = tower(
        first_kernel,
        "tower_a",
        far_array((rows, units), f32),
        own_a,
        got_sum,
        tower_bias,
        stitch,
        cotan_a,
        cotan_b,
    )
    dzo_a = send(swap, dzt_a)
    packed_a = pack(where, (a0, a1, a2, a3), dz_a, sums_a)
    b1, b_mid = wait(b1, b_mid)
    got_a = send(exchange, packed_a)
    b_end = send(outward, b_mid)
    b_mid2 = send(between, b1)
    dzo_a = wait(dzo_a)
    first_a = first_slot(slot_a, dzt_a, dzo_a)
    in1_a = send(inward, first_a)
    second_a, third_a, kept_a = parts(
        ((1, 0, 0), (2, 1, 0), (3, 2, 0)),
        [(1, bf16), (1, bf16), (1, f32)],
        where,
        weight_a,
        whole_a,
        dzt_a,
        dzo_a,
    )
    in2_a = send(inward, second_a)
    b_mid2 = wait(b_mid2)
    b_end2 = send(outward, b_mid2)
    b_end = wait(b_end)
    b2 = choose(where, b_end, b_mid2)
    keep_b, give_b, last_b, slot_b = forward_open(where, b0, b1, b2, weight_b, whole_b)
    in1_a = wait(in1_a)
    cross1_a = send(between, add(first_a, in1_a))
    b_end2 = wait(b_end2)
    b3 = choose(where, b_end2, b_mid)
    own_b, sent_b = forward_close(b3, last_b, keep_b, give_b)
    got_sum = send(swap, sent_b)
    in2_a = wait(in2_a)
    sum2_a = add(second_a, in2_a)
    got_sum = wait(got_sum)
    dz_b, dzt_b, sums_b, local = tower(
        second_kernel,
        "tower_b",
        far_array((2 * rows, units), bf16),
        own_b,
        got_sum,
        hidden_a,
        tower_bias,
        stitch,
        cotan_a,
        cotan_b,
    )
    dzo_b = send(swap, dzt_b)
    packed_b = pack(where, (b0, b1, b2, b3), dz_b, sums_b)
    cross1_a = wait(cross1_a)
    sum3_a = add(third_a, cross1_a)
    got_a = wait(got_a)
    far_a = send(swap, got_a)
    got_b = send(exchange, packed_b)
    cross2_a = send(between, sum2_a)
    dzo_b, far_a = wait(dzo_b, far_a)
    first_b = first_slot(slot_b, dzt_b, dzo_b)
    in1_b = send(inward, first_b)
    out_a = send(outward, sum3_a)
    s1 = send(along, local)
    s_mid = send(between, local)
    second_b, third_b, kept_b = parts(
        ((1, 0, 0), (2, 1, 0), (3, 2, 0)),
        [(1, bf16), (1, bf16), (1, f32)],
        where,
        weight_b,
        whole_b,
        dzt_b,
        dzo_b,
    )
    grad_weight_a = weight_grad((0, 1), rows, cols, where, (got_a, far_a), got_a)
    cross2_a, out_a = wait(cross2_a, out_a)
    in1_b = wait(in1_b)
    cross1_b = send(between, add(first_b, in1_b))
    in2_b = send(inward, second_b)
    in3_b = send(inward, third_b)
    s1, s_mid = wait(s1, s_mid)
    s_end = send(outward, s_mid)
    s_mid2 = send(between, s1)
    low_half = join(where, local, s1, s1)
    cross1_b = wait(cross1_b)
    out_b = send(outward, add(third_b, cross1_b))
    in2_b = wait(in2_b)
    cross2_b = send(between, add(second_b, in2_b))
    s_end, s_mid2 = wait(s_end, s_mid2)
    s_end2 = send(outward, s_mid2)
    in3_a = send(inward, third_a)
    s2 = choose(where, s_end, s_mid2)
    got_b = wait(got_b)
    grad_bias, grad_stitch = total_sums(rows, cols, got_a, got_b)
    half_b, block_b = weight_grad((0,), rows, cols, where, (got_b,), got_b)
    in3_b, out_b, cross2_b = wait(in3_b, out_b, cross2_b)
    grad_image_b = finish(where, position_mask, group, kept_b, in3_b, cross2_b, out_b)
    s_end2, in3_a = wait(s_end2, in3_a)
    high = join(where, s2, s_end2, s_mid)
    far_high = send(swap, high)
    far_low = send(swap, low_half)
    far_b = send(swap, block_b)
    grad_image_a = finish(where, position_mask, group, kept_a, in3_a, cross2_a, out_a)
    grad_weight_b = weight_grad((1,), rows, cols, where, (far_b,), got_b, half_b)
    stitched_a, stitched_b = lay_out(where, low_half, high, far_low, far_high)
    return (
        stitched_a,
        stitched_b,
        grad_image_a,
        grad_image_b,
        grad_weight_a,
        grad_weight_b,
        grad_bias,
        grad_stitch,
    )


def solution(mesh):
    placed = (
        P("dp", "mp"),
        P("dp", "mp"),
        P("dp"),
        P(),
        P(None, "mp"),
        P(None, "mp"),
        P(None, "mp"),
        P(None, "mp"),
        P("dp", "mp"),
        P("dp", "mp"),
    )
    fits = mesh.shape["dp"] == 4 and mesh.shape["mp"] == 8
    return jax.shard_map(
        fast_shards if fits else general_shards,
        mesh=mesh,
        in_specs=placed,
        out_specs=(
            P("dp", None),
            P("dp", None),
            P("mp", "dp"),
            P("mp", "dp"),
            P("dp", "mp"),
            P("dp", "mp"),
            P(None, "mp"),
            P(None, "mp"),
        ),
        check_vma=False,
    )
```

```python
import functools

import jax
import jax.numpy as jnp
from jax import lax
from jax.experimental import pallas as pl
from jax.experimental.pallas import tpu as pltpu
from jax.sharding import PartitionSpec as P

CH = 256
POS = 36


def keep_block(image_group, position_mask, first_col, cols):
    positions = (first_col + lax.iota(jnp.int32, cols)) // CH
    onehot = (positions[:, None] == lax.iota(jnp.int32, POS)[None, :]).astype(jnp.float32)
    per_position = jnp.dot(onehot, position_mask.astype(jnp.float32).T)
    return jnp.where(
        image_group[:, None] == 1, per_position[:, 1][None, :], per_position[:, 0][None, :]
    )


def general_shards(
    image_a,
    image_b,
    image_group,
    position_mask,
    weight_a,
    weight_b,
    tower_bias,
    stitch,
    cotan_a,
    cotan_b,
):
    batch_rows = image_a.shape[0]
    shard_cols = image_a.shape[1]
    first_col = lax.axis_index("mp") * shard_cols
    keep_mask = keep_block(image_group, position_mask, first_col, shard_cols)
    keep_low = keep_mask.astype(jnp.bfloat16)
    contract_rows = (((0,), (0,)), ((), ()))
    contract_units = (((1,), (1,)), ((), ()))
    full_a = lax.all_gather(image_a * keep_low, "mp", axis=1, tiled=True)
    full_b = lax.all_gather(image_b * keep_low, "mp", axis=1, tiled=True)
    pre_a = jnp.dot(full_a, weight_a, preferred_element_type=jnp.float32) + tower_bias[0][None, :]
    pre_b = jnp.dot(full_b, weight_b, preferred_element_type=jnp.float32) + tower_bias[1][None, :]
    sigma_a = jax.nn.sigmoid(pre_a)
    sigma_b = jax.nn.sigmoid(pre_b)
    hidden_a = pre_a * sigma_a
    hidden_b = pre_b * sigma_b
    local_a = (stitch[0][None, :] * hidden_a + stitch[1][None, :] * hidden_b).astype(jnp.bfloat16)
    local_b = (stitch[2][None, :] * hidden_a + stitch[3][None, :] * hidden_b).astype(jnp.bfloat16)
    stitched_a = lax.all_gather(local_a, "mp", axis=1, tiled=True)
    stitched_b = lax.all_gather(local_b, "mp", axis=1, tiled=True)
    upper_a = cotan_a.astype(jnp.float32)
    upper_b = cotan_b.astype(jnp.float32)
    dhid_a = stitch[0][None, :] * upper_a + stitch[2][None, :] * upper_b
    dhid_b = stitch[1][None, :] * upper_a + stitch[3][None, :] * upper_b
    dpre_a = dhid_a * (sigma_a * (1.0 + pre_a * (1.0 - sigma_a)))
    dpre_b = dhid_b * (sigma_b * (1.0 + pre_b * (1.0 - sigma_b)))
    bias_terms = jnp.stack([jnp.sum(dpre_a, axis=0), jnp.sum(dpre_b, axis=0)])
    stitch_terms = jnp.stack(
        [
            jnp.sum(upper_a * hidden_a, axis=0),
            jnp.sum(upper_a * hidden_b, axis=0),
            jnp.sum(upper_b * hidden_a, axis=0),
            jnp.sum(upper_b * hidden_b, axis=0),
        ]
    )
    grad_bias, grad_stitch = lax.psum((bias_terms, stitch_terms), "dp")
    dlow_a = dpre_a.astype(jnp.bfloat16)
    dlow_b = dpre_b.astype(jnp.bfloat16)
    block_a = lax.dot_general(full_a, dlow_a, contract_rows, preferred_element_type=jnp.float32)
    block_b = lax.dot_general(full_b, dlow_b, contract_rows, preferred_element_type=jnp.float32)
    grad_weight_a = lax.psum_scatter(block_a, "dp", scatter_dimension=0, tiled=True)
    grad_weight_b = lax.psum_scatter(block_b, "dp", scatter_dimension=0, tiled=True)
    part_a = lax.dot_general(weight_a, dlow_a, contract_units, preferred_element_type=jnp.float32)
    part_b = lax.dot_general(weight_b, dlow_b, contract_units, preferred_element_type=jnp.float32)
    summed = lax.psum_scatter(
        jnp.concatenate([part_a, part_b], axis=1), "mp", scatter_dimension=0, tiled=True
    )
    keep_cols = keep_mask.T
    grad_image_a = (summed[:, :batch_rows] * keep_cols).astype(jnp.bfloat16)
    grad_image_b = (summed[:, batch_rows:] * keep_cols).astype(jnp.bfloat16)
    return (
        stitched_a,
        stitched_b,
        grad_image_a,
        grad_image_b,
        grad_weight_a,
        grad_weight_b,
        grad_bias,
        grad_stitch,
    )


SWAP_CORE = [(d, d ^ 1) for d in range(8)]
NEAR_Z = [(d, d ^ 2) for d in range(8)]
FAR_Z = [(d, d ^ 4) for d in range(8)]
ENDS_IN = [(0, 2), (1, 3), (6, 4), (7, 5)]
MIDS = [(2, 4), (3, 5), (4, 2), (5, 3)]
ENDS_OUT = [(2, 0), (3, 1), (4, 6), (5, 7)]
SLOTS = ((3, 2, 1, 0), (3, 2, 0, 1), (0, 1, 3, 2), (0, 1, 2, 3))
LANES = 128
EXTRA = 16
VMEM_LIMIT = 22 * 1024 * 1024
SMEM = pl.BlockSpec(memory_space=pltpu.SMEM)
VMEM = pl.BlockSpec(memory_space=pltpu.VMEM)
HBM = pl.BlockSpec(memory_space=pltpu.HBM)
ANY = pl.BlockSpec(memory_space=pl.ANY)
LITTLE = pl.CostEstimate(flops=1, bytes_accessed=1, transcendentals=0)


def low(x):
    return x.astype(jnp.bfloat16)


def wide(x):
    return x.astype(jnp.float32)


def array(shape, dtype):
    return jax.ShapeDtypeStruct(shape, dtype)


def far_array(shape, dtype):
    return pltpu.HBM(shape, dtype)


class Line:
    def __init__(self):
        self.token = None

    def tie(self, *xs):
        if self.token is None:
            return xs
        *xs, self.token = lax.optimization_barrier((*xs, self.token))
        return xs

    def wait(self, *arrived):
        arrived = self.tie(*arrived)
        return arrived if len(arrived) > 1 else arrived[0]

    def send(self, move, x):
        return move(*self.tie(x))


line = Line()


def call(kernel, out_shape, in_specs, out_specs, name, scratch=(), aliases={}):
    single = not isinstance(out_shape, list)
    outs = [out_shape] if single else out_shape
    places = [out_specs] if single else out_specs
    n_in, n_out = len(in_specs), len(outs)
    before = () if line.token is None else (line.token,)

    def body(*refs):
        start = n_in + len(before)
        refs[start + n_out][...] = jnp.zeros((8, LANES), jnp.float32)
        kernel(*refs[:n_in], *refs[start : start + n_out], *refs[start + n_out + 1 :])

    run = pl.pallas_call(
        body,
        out_shape=[*outs, array((8, LANES), jnp.float32)],
        in_specs=[*in_specs, *[HBM] * len(before)],
        out_specs=[*places, VMEM],
        scratch_shapes=scratch,
        input_output_aliases=aliases,
        compiler_params=pltpu.CompilerParams(vmem_limit_bytes=VMEM_LIMIT),
        cost_estimate=LITTLE,
        name=name,
    )

    def go(*operands):
        *results, line.token = run(*operands, *before)
        return results[0] if single else results

    return go


def marks_of(marks, place, cols, chunk):
    position = (place * cols + chunk * LANES) // CH
    return marks[0, position], marks[1, position]


def mask_kernel(place, marks, group, image, out, held, sem):
    rows, cols = image.shape
    copy = pltpu.make_async_copy(image, held, sem)
    copy.start()
    second = jnp.broadcast_to(jnp.where(group[...] == 1, 1.0, 0.0), (8, rows)).T[:, 0:1] > 0.5
    copy.wait()
    for chunk in range(cols // LANES):
        zero, one = marks_of(marks, place[0], cols, chunk)
        keep = wide(jnp.where(second, one, zero))
        lanes = slice(chunk * LANES, (chunk + 1) * LANES)
        out[:, lanes] = low(wide(held[:, lanes]) * keep)


def mask_image(place, marks, group, image):
    return call(
        mask_kernel,
        array(image.shape, jnp.bfloat16),
        [SMEM, SMEM, VMEM, ANY],
        VMEM,
        "mask_image",
        [pltpu.VMEM(image.shape, jnp.bfloat16), pltpu.SemaphoreType.DMA],
    )(place, marks, group, image)


def in_hbm(x):
    return pltpu.with_memory_space_constraint(x, pltpu.HBM)


def dot(x, y):
    return jnp.dot(x, y, preferred_element_type=jnp.float32)


def products(where, ks, mine, other, held, sems, emit):
    cols = held.shape[2]

    def copies(i):
        block = 2 * (where[0] ^ ks[i]) + where[1]
        rows = pl.ds(pl.multiple_of(block * cols, cols), cols)
        return [
            pltpu.make_async_copy(weight.at[rows, :], held.at[i, side], sems.at[i, side])
            for side, weight in enumerate((mine, other))
        ]

    for i in range(len(ks)):
        for copy in copies(i):
            copy.start()
    for i in range(len(ks)):
        for copy in copies(i):
            copy.wait()
        emit(i, held[i, 0], held[i, 1])


def open_kernel(where, p0, p1, p2, mine, other, keep, send, last, slot, held, sems):
    pieces = (p0, p1, p2)
    cols = p0.shape[1]
    ahead = []
    for at, (k, out) in enumerate(((3, last), (where[3], slot))):
        block = 2 * (where[0] ^ k) + where[1]
        rows = pl.ds(pl.multiple_of(block * cols, cols), cols)
        for side, weight in enumerate((mine, other)):
            ahead.append(
                pltpu.make_async_copy(weight.at[rows, :], out.at[side], sems.at[3 + at, side])
            )

    def emit(i, own_block, other_block):
        if i == 0:
            for copy in ahead:
                copy.start()
            keep[...] = dot(p0[...], own_block)
            send[...] = dot(p0[...], other_block)
        else:
            keep[...] += dot(pieces[i][...], own_block)
            send[...] += dot(pieces[i][...], other_block)

    products(where, (0, 1, 2), mine, other, held, sems, emit)
    for copy in ahead:
        copy.wait()


def forward_open(where, p0, p1, p2, mine, other):
    rows, cols = p0.shape
    units = mine.shape[1]
    blocks = pltpu.VMEM((2, cols, units), jnp.bfloat16)
    return call(
        open_kernel,
        [array((rows, units), jnp.float32)] * 2 + [blocks] * 2,
        [SMEM] + [VMEM] * 3 + [HBM] * 2,
        [VMEM] * 4,
        "forward_open",
        [pltpu.VMEM((3, 2, cols, units), jnp.bfloat16), pltpu.SemaphoreType.DMA((5, 2))],
    )(where, p0, p1, p2, in_hbm(mine), in_hbm(other))


def close_kernel(p3, weights, keep, send, out, sent):
    sent[...] = send[...] + dot(p3[...], weights[1])
    out[...] = keep[...] + dot(p3[...], weights[0])


def forward_close(p3, weights, keep, send):
    return call(
        close_kernel,
        [array(keep.shape, jnp.float32)] * 2,
        [VMEM] * 4,
        [VMEM] * 2,
        "forward_close",
    )(p3, weights, keep, send)


def slot_kernel(weights, dz_t, dzo_t, out):
    out[...] = low(dot(weights[0], dz_t[...]) + dot(weights[1], dzo_t[...]))


def first_slot(weights, dz_t, dzo_t):
    return call(
        slot_kernel,
        array((weights.shape[1], dz_t.shape[1]), jnp.bfloat16),
        [VMEM] * 3,
        VMEM,
        "first_slot",
    )(weights, dz_t, dzo_t)


def tower_math(pre, bias, unit_a, unit_b, upper_a, upper_b, dz, dz_t, sums):
    pre = pre + bias[...]
    sigma = jax.nn.sigmoid(pre)
    hidden = pre * sigma
    cot_a = wide(upper_a[...])
    cot_b = wide(upper_b[...])
    dhid = unit_a[...] * cot_a + unit_b[...] * cot_b
    dpre = dhid * (sigma * (1.0 + pre * (1.0 - sigma)))
    dz[...] = low(dpre)
    dz_t[...] = low(dpre).T
    sums[0:1, :] = jnp.sum(dpre, axis=0, keepdims=True)
    sums[1:2, :] = jnp.sum(cot_a * hidden, axis=0, keepdims=True)
    sums[2:3, :] = jnp.sum(cot_b * hidden, axis=0, keepdims=True)
    sums[3:4, :] = jnp.zeros_like(sums[3:4, :])
    return hidden


def first_kernel(own, got, bias, stitch, upper_a, upper_b, dz, dz_t, sums, hidden):
    hidden[...] = tower_math(
        own[...] + got[...],
        bias[0:1, :],
        stitch[0:1, :],
        stitch[2:3, :],
        upper_a,
        upper_b,
        dz,
        dz_t,
        sums,
    )


def second_kernel(own, got, earlier, bias, stitch, upper_a, upper_b, dz, dz_t, sums, local):
    hidden = tower_math(
        own[...] + got[...],
        bias[1:2, :],
        stitch[1:2, :],
        stitch[3:4, :],
        upper_a,
        upper_b,
        dz,
        dz_t,
        sums,
    )
    rows = hidden.shape[0]
    before = earlier[...]
    local[0:rows, :] = low(stitch[0:1, :] * before + stitch[1:2, :] * hidden)
    local[rows : 2 * rows, :] = low(stitch[2:3, :] * before + stitch[3:4, :] * hidden)


def tower(kernel, name, last, *operands):
    rows, units = operands[0].shape
    return call(
        kernel,
        [
            array((rows, units), jnp.bfloat16),
            far_array((units, rows), jnp.bfloat16),
            array((4, units), jnp.float32),
            last,
        ],
        [VMEM] * len(operands),
        [VMEM] * 4,
        name,
    )(*operands)


def part_kernel(slots, where, mine, other, dz_t, dzo_t, *refs):
    *outs, held, sems = refs
    cols = held.shape[2]

    def emit(i, own_block, other_block):
        _, at, block = slots[i]
        total = dot(own_block, dz_t[...]) + dot(other_block, dzo_t[...])
        outs[at][block * cols : (block + 1) * cols, :] = total.astype(outs[at].dtype)

    products(where, [where[3 + slot] for slot, _, _ in slots], mine, other, held, sems, emit)


def parts(slots, outs, where, mine, other, dz_t, dzo_t):
    units, rows = dz_t.shape
    cols = mine.shape[0] // 8
    return call(
        functools.partial(part_kernel, slots),
        [far_array((blocks * cols, rows), dtype) for blocks, dtype in outs],
        [SMEM, HBM, HBM, VMEM, VMEM],
        [VMEM] * len(outs),
        "parts",
        [
            pltpu.VMEM((len(slots), 2, cols, units), jnp.bfloat16),
            pltpu.SemaphoreType.DMA((len(slots), 2)),
        ],
    )(where, in_hbm(mine), in_hbm(other), dz_t, dzo_t)


def choose_kernel(where, at_end, in_middle, out, sem):
    for flag, source in enumerate((at_end, in_middle)):
        pl.when(where[2] == flag)(pltpu.make_async_copy(source, out, sem).start)
    pltpu.make_async_copy(at_end, out, sem).wait()


def choose(where, at_end, in_middle):
    return call(
        choose_kernel,
        array(at_end.shape, at_end.dtype),
        [SMEM, ANY, ANY],
        VMEM,
        "choose",
        [pltpu.SemaphoreType.DMA],
    )(where, at_end, in_middle)


def join_kernel(where, one, at_end, in_middle, out, sems):
    rows = one.shape[0]
    copies = [pltpu.make_async_copy(one, out.at[pl.ds(0, rows), :], sems.at[0])]
    copies[0].start()
    rest = out.at[pl.ds(rows, rows), :]
    for flag, source in enumerate((at_end, in_middle)):
        pl.when(where[2] == flag)(pltpu.make_async_copy(source, rest, sems.at[1]).start)
    copies[0].wait()
    pltpu.make_async_copy(at_end, rest, sems.at[1]).wait()


def join(where, one, at_end, in_middle):
    rows, cols = one.shape
    return call(
        join_kernel,
        array((2 * rows, cols), one.dtype),
        [SMEM] + [ANY] * 3,
        VMEM,
        "join",
        [pltpu.SemaphoreType.DMA((2,))],
    )(where, one, at_end, in_middle)


def lay_kernel(where, low, high, far_low, far_high, out_a, out_b, stage, sems):
    rows = out_a.shape[0]
    units = low.shape[1]
    pieces = []
    for side, (first, second) in enumerate(((low, high), (far_low, far_high))):
        for k in range(4):
            block = 2 * (where[0] ^ k) + (where[1] ^ side)
            lanes = pl.ds(pl.multiple_of(block * units, units), units)
            source = (first, second)[k // 2]
            for half in range(2):
                at = pl.ds((2 * (k % 2) + half) * rows, rows)
                sem = sems.at[half, 4 * side + k]
                pieces.append(
                    pltpu.make_async_copy(source.at[at, :], stage.at[half, :, lanes], sem)
                )
    gives = [
        pltpu.make_async_copy(stage.at[half], out, sems.at[half, 8])
        for half, out in enumerate((out_a, out_b))
    ]
    for copy in pieces:
        copy.start()
    for half in range(2):
        for copy in pieces[half::2]:
            copy.wait()
        gives[half].start()
    for give in gives:
        give.wait()


def lay_out(where, low, high, far_low, far_high):
    rows, units = low.shape[0] // 4, low.shape[1]
    stitched = pltpu.HBM((rows, 8 * units), jnp.bfloat16)
    return call(
        lay_kernel,
        [stitched, stitched],
        [SMEM] + [ANY] * 4,
        [HBM] * 2,
        "lay_out",
        [
            pltpu.VMEM((2, rows, 8 * units), jnp.bfloat16),
            pltpu.SemaphoreType.DMA((2, 9)),
        ],
    )(where, low, high, far_low, far_high)


def add_kernel(at, one, two, out):
    rows = out.shape[0]
    out[...] = low(wide(one[at : at + rows, :]) + wide(two[0:rows, :]))


def add(one, two, block=0, rows=None):
    rows = rows or min(one.shape[0], two.shape[0])
    return call(
        functools.partial(add_kernel, block * rows),
        far_array((rows, one.shape[1]), jnp.bfloat16),
        [VMEM, VMEM],
        VMEM,
        "add",
    )(one, two)


def finish_kernel(
    block, where, marks, group, kept, third, cross, last, out, held, own, done, sems
):
    second = group[...] == 1
    cols = own.shape[0]
    tile = cols // 3

    def fetch(t):
        rows = pl.ds(t * tile, tile)
        copies = [pltpu.make_async_copy(kept.at[rows, :], own.at[rows, :], sems.at[t, 3])]
        for n, source in enumerate((third, cross, last)):
            start = block * cols + t * tile if n == 0 else t * tile
            part = source.at[pl.ds(start, tile), :]
            copies.append(pltpu.make_async_copy(part, held.at[n, rows, :], sems.at[t, n]))
        return copies

    def give(t):
        rows = pl.ds(t * tile, tile)
        return pltpu.make_async_copy(done.at[rows, :], out.at[rows, :], sems.at[t, 4])

    for t in range(3):
        for copy in fetch(t):
            copy.start()
    for t in range(3):
        for copy in fetch(t):
            copy.wait()
        for chunk in range(t * tile // LANES, (t + 1) * tile // LANES):
            zero, one = marks_of(marks, where[8], cols, chunk)
            keep = wide(jnp.where(second, one, zero))
            rows = slice(chunk * LANES, (chunk + 1) * LANES)
            total = own[rows, :] + wide(held[0, rows, :])
            total += wide(held[1, rows, :]) + wide(held[2, rows, :])
            done[rows, :] = low(total * keep)
        give(t).start()
    for t in range(3):
        give(t).wait()


def finish(block, where, marks, group, kept, third, cross, last):
    return call(
        functools.partial(finish_kernel, block),
        pltpu.HBM(kept.shape, jnp.bfloat16),
        [SMEM, SMEM, VMEM] + [HBM] * 4,
        HBM,
        "finish",
        [
            pltpu.VMEM((3, *kept.shape), jnp.bfloat16),
            pltpu.VMEM(kept.shape, jnp.float32),
            pltpu.VMEM(kept.shape, jnp.bfloat16),
            pltpu.SemaphoreType.DMA((3, 5)),
        ],
    )(where, marks, group, *[in_hbm(x) for x in (kept, third, cross, last)])


def pack_kernel(where, p0, p1, p2, p3, dz, sums, given, out, sems):
    rows, units = dz.shape
    cols = p0.shape[1]
    for q in range(4):
        block = out.at[q, pl.ds(0, rows), pl.ds(0, cols)]
        for index, piece in enumerate((p0, p1, p2, p3)):
            start = pltpu.make_async_copy(piece, block, sems.at[q]).start
            pl.when(where[0] ^ q == index)(start)
    extra = jnp.zeros((EXTRA, cols + units), jnp.bfloat16)
    for q in range(4):
        out[q, rows : rows + EXTRA, :] = extra
        out[q, 0:rows, cols : cols + units] = dz[...]
    for k in range(3):
        rest = sums[k : k + 1, :]
        for term in range(3):
            piece = low(rest)
            row = rows + 3 * k + term
            for q in range(4):
                out[q, row : row + 1, cols : cols + units] = piece
            rest = rest - wide(piece)
    gives = [pltpu.make_async_copy(out.at[q], given.at[q], sems.at[4 + q]) for q in range(4)]
    for q in range(4):
        block = out.at[q, pl.ds(0, rows), pl.ds(0, cols)]
        pltpu.make_async_copy(p0, block, sems.at[q]).wait()
        gives[q].start()
    for give in gives:
        give.wait()


def pack(where, pieces, dz, sums):
    rows, units = dz.shape
    cols = pieces[0].shape[1]
    return call(
        pack_kernel,
        pltpu.HBM((4, rows + EXTRA, cols + units), jnp.bfloat16),
        [SMEM] + [ANY] * 4 + [VMEM] * 2,
        HBM,
        "pack",
        [
            pltpu.VMEM((4, rows + EXTRA, cols + units), jnp.bfloat16),
            pltpu.SemaphoreType.DMA((8,)),
        ],
    )(where, *pieces, dz, sums)


def weight_kernel(sides, where, *refs):
    n = len(sides)
    images_of, dz_of = refs[:n], refs[n]
    *outs, images, dzs, tiles, sems = refs[n + 1 + (sides == (1,)) :]
    out = outs[0]
    rows, units = dzs.shape[1:]
    cols = images.shape[3]
    tile = tiles.shape[1]
    steps = cols // tile

    def fetch(q):
        source = dz_of.at[q, pl.ds(0, rows), pl.ds(cols, units)]
        return pltpu.make_async_copy(source, dzs.at[q], sems.at[q])

    def block(i, q):
        image = images_of[i].at[q, pl.ds(0, rows), pl.ds(0, cols)]
        return pltpu.make_async_copy(image, images.at[i, q], sems.at[4 + 4 * i + q])

    def give(i, t):
        at = pl.multiple_of((where[1] ^ sides[i]) * cols + t * tile, tile)
        slot = i * steps + t
        return pltpu.make_async_copy(
            tiles.at[slot], out.at[pl.ds(at, tile), :], sems.at[12 + slot]
        )

    for q in range(4):
        fetch(q).start()
    for i in range(n):
        for q in range(4):
            block(i, q).start()
    for q in range(4):
        fetch(q).wait()
    for i in range(n):
        for q in range(4):
            block(i, q).wait()
        if len(outs) > 1:
            for q in range(4):
                pltpu.make_async_copy(images.at[i, q], outs[1].at[q], sems.at[4 + q]).start()
        for t in range(steps):
            total = None
            for q in range(4):
                term = lax.dot_general(
                    images[i, q, :, t * tile : (t + 1) * tile],
                    dzs[q],
                    (((0,), (0,)), ((), ())),
                    preferred_element_type=jnp.float32,
                )
                total = term if total is None else total + term
            tiles[i * steps + t] = total
            give(i, t).start()
    for i in range(n):
        for t in range(steps):
            give(i, t).wait()
    if len(outs) > 1:
        for q in range(4):
            pltpu.make_async_copy(images.at[0, q], outs[1].at[q], sems.at[4 + q]).wait()


def weight_grad(sides, rows, cols, where, images, dz, *before):
    units = dz.shape[2] - cols
    tile = cols // 3
    n = len(sides)
    outs = [pltpu.HBM((2 * cols, units), jnp.float32)]
    if sides == (0,):
        outs.append(pltpu.HBM((4, rows, cols), jnp.bfloat16))
    return call(
        functools.partial(weight_kernel, sides),
        outs if len(outs) > 1 else outs[0],
        [SMEM] + [ANY] * (n + 1) + [HBM] * len(before),
        [HBM] * len(outs) if len(outs) > 1 else HBM,
        "weight_grad",
        [
            pltpu.VMEM((n, 4, rows, cols), jnp.bfloat16),
            pltpu.VMEM((4, rows, units), jnp.bfloat16),
            pltpu.VMEM((3 * n, tile, units), jnp.float32),
            pltpu.SemaphoreType.DMA((18,)),
        ],
        {n + 2: 0} if before else {},
    )(where, *images, dz, *before)


def sums_kernel(rows, cols, got_a, got_b, bias, stitch, terms, sems):
    units = bias.shape[1]
    copies = [
        pltpu.make_async_copy(
            got.at[:, pl.ds(rows, EXTRA), pl.ds(cols, units)], terms.at[side], sems.at[side]
        )
        for side, got in enumerate((got_a, got_b))
    ]
    for copy in copies:
        copy.start()
    for copy in copies:
        copy.wait()
    for side in range(2):
        totals = []
        for k in range(3):
            each = [
                (
                    wide(terms[side, q, 3 * k + 2 : 3 * k + 3, :])
                    + wide(terms[side, q, 3 * k + 1 : 3 * k + 2, :])
                )
                + wide(terms[side, q, 3 * k : 3 * k + 1, :])
                for q in range(4)
            ]
            totals.append((each[0] + each[1]) + (each[2] + each[3]))
        bias[side : side + 1, :] = totals[0]
        stitch[side : side + 1, :] = totals[1]
        stitch[2 + side : 3 + side, :] = totals[2]


def total_sums(rows, cols, got_a, got_b):
    units = got_a.shape[2] - cols
    return call(
        functools.partial(sums_kernel, rows, cols),
        [array((2, units), jnp.float32), array((4, units), jnp.float32)],
        [ANY, ANY],
        [VMEM, VMEM],
        "total_sums",
        [pltpu.VMEM((2, 4, EXTRA, units), jnp.bfloat16), pltpu.SemaphoreType.DMA((2,))],
    )(got_a, got_b)


def swap(x):
    return lax.ppermute(x, "mp", SWAP_CORE)


def along(x):
    return lax.ppermute(x, "mp", NEAR_Z)


def across(x):
    return lax.ppermute(x, "mp", FAR_Z)


def inward(x):
    return lax.ppermute(x, "mp", ENDS_IN)


def between(x):
    return lax.ppermute(x, "mp", MIDS)


def outward(x):
    return lax.ppermute(x, "mp", ENDS_OUT)


def exchange(x):
    return lax.all_to_all(x, "dp", 0, 0)


def fast_shards(
    image_a,
    image_b,
    image_group,
    position_mask,
    weight_a,
    weight_b,
    tower_bias,
    stitch,
    cotan_a,
    cotan_b,
):
    rows, cols = image_a.shape
    units = weight_a.shape[1]
    place = lax.axis_index("mp").astype(jnp.int32)
    z = place // 2
    core = place % 2
    quarter = lax.axis_index("dp").astype(jnp.int32)
    middle = ((z == 1) | (z == 2)).astype(jnp.int32)
    slots = jnp.take(jnp.asarray(SLOTS, jnp.int32), z, axis=0) ^ z
    where = jnp.concatenate(
        [jnp.stack([z, core, middle]), slots, jnp.stack([quarter, place])]
    ).astype(jnp.int32)
    group = image_group[None, :]
    line.token = None
    bf16, f32 = jnp.bfloat16, jnp.float32
    send, wait = line.send, line.wait

    whole_a = swap(weight_a)
    whole_b = swap(weight_b)
    def masked(k, image):
        spot = (2 * (z ^ k) + core)[None]
        return mask_image(spot, position_mask, group, image)

    raw2 = across(image_a)
    raw1 = along(image_a)
    b0 = masked(0, in_hbm(image_b))
    a0 = masked(0, in_hbm(image_a))
    raw1, raw2 = wait(raw1, raw2)
    raw3 = send(along, raw2)
    b_mid = send(between, b0)
    b1 = send(along, b0)
    a1 = masked(1, raw1)
    a2 = masked(2, raw2)
    whole_a, whole_b = wait(whole_a, whole_b)
    keep_a, give_a, last_a, slot_a = forward_open(where, a0, a1, a2, weight_a, whole_a)
    a3 = masked(3, wait(raw3))
    own_a, sent_a = forward_close(a3, last_a, keep_a, give_a)
    got_sum = wait(send(swap, sent_a))
    dz_a, dzt_a, sums_a, hidden_a = tower(
        first_kernel,
        "tower_a",
        far_array((rows, units), f32),
        own_a,
        got_sum,
        tower_bias,
        stitch,
        cotan_a,
        cotan_b,
    )
    dzo_a = send(swap, dzt_a)
    packed_a = pack(where, (a0, a1, a2, a3), dz_a, sums_a)
    b1, b_mid = wait(b1, b_mid)
    got_a = send(exchange, packed_a)
    b_end = send(outward, b_mid)
    b_mid2 = send(between, b1)
    dzo_a = wait(dzo_a)
    first_a = first_slot(slot_a, dzt_a, dzo_a)
    in1_a = send(inward, first_a)
    second_a, third_a, kept_a = parts(
        ((1, 0, 0), (2, 1, 0), (3, 2, 0)),
        [(1, bf16), (1, bf16), (1, f32)],
        where,
        weight_a,
        whole_a,
        dzt_a,
        dzo_a,
    )
    in2_a = send(inward, second_a)
    b_mid2 = wait(b_mid2)
    b_end2 = send(outward, b_mid2)
    b_end = wait(b_end)
    b2 = choose(where, b_end, b_mid2)
    keep_b, give_b, last_b, slot_b = forward_open(where, b0, b1, b2, weight_b, whole_b)
    in1_a = wait(in1_a)
    cross1_a = send(between, add(first_a, in1_a))
    b_end2 = wait(b_end2)
    b3 = choose(where, b_end2, b_mid)
    own_b, sent_b = forward_close(b3, last_b, keep_b, give_b)
    got_sum = send(swap, sent_b)
    in2_a = wait(in2_a)
    sum2_a = add(second_a, in2_a)
    got_sum = wait(got_sum)
    dz_b, dzt_b, sums_b, local = tower(
        second_kernel,
        "tower_b",
        far_array((2 * rows, units), bf16),
        own_b,
        got_sum,
        hidden_a,
        tower_bias,
        stitch,
        cotan_a,
        cotan_b,
    )
    dzo_b = send(swap, dzt_b)
    packed_b = pack(where, (b0, b1, b2, b3), dz_b, sums_b)
    cross1_a = wait(cross1_a)
    sum3_a = add(third_a, cross1_a)
    got_a = wait(got_a)
    far_a = send(swap, got_a)
    got_b = send(exchange, packed_b)
    cross2_a = send(between, sum2_a)
    dzo_b, far_a = wait(dzo_b, far_a)
    first_b = first_slot(slot_b, dzt_b, dzo_b)
    in1_b = send(inward, first_b)
    out_a = send(outward, sum3_a)
    s1 = send(along, local)
    s_mid = send(between, local)
    second_b, third_b, kept_b = parts(
        ((1, 0, 0), (2, 1, 0), (3, 2, 0)),
        [(1, bf16), (1, bf16), (1, f32)],
        where,
        weight_b,
        whole_b,
        dzt_b,
        dzo_b,
    )
    thirds = join(where, third_b, third_a, third_a)
    grad_weight_a = weight_grad((0, 1), rows, cols, where, (got_a, far_a), got_a)
    cross2_a, out_a = wait(cross2_a, out_a)
    in1_b = wait(in1_b)
    cross1_b = send(between, add(first_b, in1_b))
    in2_b = send(inward, second_b)
    in3 = send(inward, thirds)
    s1, s_mid = wait(s1, s_mid)
    s_end = send(outward, s_mid)
    s_mid2 = send(between, s1)
    low_half = join(where, local, s1, s1)
    cross1_b = wait(cross1_b)
    out_b = send(outward, add(third_b, cross1_b))
    in2_b = wait(in2_b)
    cross2_b = send(between, add(second_b, in2_b))
    s_end, s_mid2 = wait(s_end, s_mid2)
    s_end2 = send(outward, s_mid2)
    s2 = choose(where, s_end, s_mid2)
    got_b = wait(got_b)
    grad_bias, grad_stitch = total_sums(rows, cols, got_a, got_b)
    half_b, block_b = weight_grad((0,), rows, cols, where, (got_b,), got_b)
    in3, out_b, cross2_b = wait(in3, out_b, cross2_b)
    grad_image_b = finish(0, where, position_mask, group, kept_b, in3, cross2_b, out_b)
    s_end2 = wait(s_end2)
    high = join(where, s2, s_end2, s_mid)
    far_high = send(swap, high)
    far_low = send(swap, low_half)
    far_b = send(swap, block_b)
    grad_image_a = finish(1, where, position_mask, group, kept_a, in3, cross2_a, out_a)
    grad_weight_b = weight_grad((1,), rows, cols, where, (far_b,), got_b, half_b)
    stitched_a, stitched_b = lay_out(where, low_half, high, far_low, far_high)
    return (
        stitched_a,
        stitched_b,
        grad_image_a,
        grad_image_b,
        grad_weight_a,
        grad_weight_b,
        grad_bias,
        grad_stitch,
    )


def solution(mesh):
    placed = (
        P("dp", "mp"),
        P("dp", "mp"),
        P("dp"),
        P(),
        P(None, "mp"),
        P(None, "mp"),
        P(None, "mp"),
        P(None, "mp"),
        P("dp", "mp"),
        P("dp", "mp"),
    )
    fits = mesh.shape["dp"] == 4 and mesh.shape["mp"] == 8
    return jax.shard_map(
        fast_shards if fits else general_shards,
        mesh=mesh,
        in_specs=placed,
        out_specs=(
            P("dp", None),
            P("dp", None),
            P("mp", "dp"),
            P("mp", "dp"),
            P("dp", "mp"),
            P("dp", "mp"),
            P(None, "mp"),
            P(None, "mp"),
        ),
        check_vma=False,
    )
```

```python
import functools

import jax
import jax.numpy as jnp
from jax import lax
from jax.experimental import pallas as pl
from jax.experimental.pallas import tpu as pltpu
from jax.sharding import PartitionSpec as P

CH = 256
POS = 36


def keep_block(image_group, position_mask, first_col, cols):
    positions = (first_col + lax.iota(jnp.int32, cols)) // CH
    onehot = (positions[:, None] == lax.iota(jnp.int32, POS)[None, :]).astype(jnp.float32)
    per_position = jnp.dot(onehot, position_mask.astype(jnp.float32).T)
    return jnp.where(
        image_group[:, None] == 1, per_position[:, 1][None, :], per_position[:, 0][None, :]
    )


def general_shards(
    image_a,
    image_b,
    image_group,
    position_mask,
    weight_a,
    weight_b,
    tower_bias,
    stitch,
    cotan_a,
    cotan_b,
):
    batch_rows = image_a.shape[0]
    shard_cols = image_a.shape[1]
    first_col = lax.axis_index("mp") * shard_cols
    keep_mask = keep_block(image_group, position_mask, first_col, shard_cols)
    keep_low = keep_mask.astype(jnp.bfloat16)
    contract_rows = (((0,), (0,)), ((), ()))
    contract_units = (((1,), (1,)), ((), ()))
    full_a = lax.all_gather(image_a * keep_low, "mp", axis=1, tiled=True)
    full_b = lax.all_gather(image_b * keep_low, "mp", axis=1, tiled=True)
    pre_a = jnp.dot(full_a, weight_a, preferred_element_type=jnp.float32) + tower_bias[0][None, :]
    pre_b = jnp.dot(full_b, weight_b, preferred_element_type=jnp.float32) + tower_bias[1][None, :]
    sigma_a = jax.nn.sigmoid(pre_a)
    sigma_b = jax.nn.sigmoid(pre_b)
    hidden_a = pre_a * sigma_a
    hidden_b = pre_b * sigma_b
    local_a = (stitch[0][None, :] * hidden_a + stitch[1][None, :] * hidden_b).astype(jnp.bfloat16)
    local_b = (stitch[2][None, :] * hidden_a + stitch[3][None, :] * hidden_b).astype(jnp.bfloat16)
    stitched_a = lax.all_gather(local_a, "mp", axis=1, tiled=True)
    stitched_b = lax.all_gather(local_b, "mp", axis=1, tiled=True)
    upper_a = cotan_a.astype(jnp.float32)
    upper_b = cotan_b.astype(jnp.float32)
    dhid_a = stitch[0][None, :] * upper_a + stitch[2][None, :] * upper_b
    dhid_b = stitch[1][None, :] * upper_a + stitch[3][None, :] * upper_b
    dpre_a = dhid_a * (sigma_a * (1.0 + pre_a * (1.0 - sigma_a)))
    dpre_b = dhid_b * (sigma_b * (1.0 + pre_b * (1.0 - sigma_b)))
    bias_terms = jnp.stack([jnp.sum(dpre_a, axis=0), jnp.sum(dpre_b, axis=0)])
    stitch_terms = jnp.stack(
        [
            jnp.sum(upper_a * hidden_a, axis=0),
            jnp.sum(upper_a * hidden_b, axis=0),
            jnp.sum(upper_b * hidden_a, axis=0),
            jnp.sum(upper_b * hidden_b, axis=0),
        ]
    )
    grad_bias, grad_stitch = lax.psum((bias_terms, stitch_terms), "dp")
    dlow_a = dpre_a.astype(jnp.bfloat16)
    dlow_b = dpre_b.astype(jnp.bfloat16)
    block_a = lax.dot_general(full_a, dlow_a, contract_rows, preferred_element_type=jnp.float32)
    block_b = lax.dot_general(full_b, dlow_b, contract_rows, preferred_element_type=jnp.float32)
    grad_weight_a = lax.psum_scatter(block_a, "dp", scatter_dimension=0, tiled=True)
    grad_weight_b = lax.psum_scatter(block_b, "dp", scatter_dimension=0, tiled=True)
    part_a = lax.dot_general(weight_a, dlow_a, contract_units, preferred_element_type=jnp.float32)
    part_b = lax.dot_general(weight_b, dlow_b, contract_units, preferred_element_type=jnp.float32)
    summed = lax.psum_scatter(
        jnp.concatenate([part_a, part_b], axis=1), "mp", scatter_dimension=0, tiled=True
    )
    keep_cols = keep_mask.T
    grad_image_a = (summed[:, :batch_rows] * keep_cols).astype(jnp.bfloat16)
    grad_image_b = (summed[:, batch_rows:] * keep_cols).astype(jnp.bfloat16)
    return (
        stitched_a,
        stitched_b,
        grad_image_a,
        grad_image_b,
        grad_weight_a,
        grad_weight_b,
        grad_bias,
        grad_stitch,
    )


SWAP_CORE = [(d, d ^ 1) for d in range(8)]
NEAR_Z = [(d, d ^ 2) for d in range(8)]
FAR_Z = [(d, d ^ 4) for d in range(8)]
ENDS_IN = [(0, 2), (1, 3), (6, 4), (7, 5)]
MIDS = [(2, 4), (3, 5), (4, 2), (5, 3)]
ENDS_OUT = [(2, 0), (3, 1), (4, 6), (5, 7)]
SLOTS = ((3, 2, 1, 0), (3, 2, 0, 1), (0, 1, 3, 2), (0, 1, 2, 3))
LANES = 128
EXTRA = 16
VMEM_LIMIT = 22 * 1024 * 1024
SMEM = pl.BlockSpec(memory_space=pltpu.SMEM)
VMEM = pl.BlockSpec(memory_space=pltpu.VMEM)
HBM = pl.BlockSpec(memory_space=pltpu.HBM)
ANY = pl.BlockSpec(memory_space=pl.ANY)
LITTLE = pl.CostEstimate(flops=1, bytes_accessed=1, transcendentals=0)


def low(x):
    return x.astype(jnp.bfloat16)


def wide(x):
    return x.astype(jnp.float32)


def array(shape, dtype):
    return jax.ShapeDtypeStruct(shape, dtype)


def far_array(shape, dtype):
    return pltpu.HBM(shape, dtype)


class Line:
    def __init__(self):
        self.token = None

    def tie(self, *xs):
        if self.token is None:
            return xs
        *xs, self.token = lax.optimization_barrier((*xs, self.token))
        return xs

    def wait(self, *arrived):
        arrived = self.tie(*arrived)
        return arrived if len(arrived) > 1 else arrived[0]

    def send(self, move, x):
        return move(*self.tie(x))


line = Line()


def call(kernel, out_shape, in_specs, out_specs, name, scratch=(), aliases={}):
    single = not isinstance(out_shape, list)
    outs = [out_shape] if single else out_shape
    places = [out_specs] if single else out_specs
    n_in, n_out = len(in_specs), len(outs)
    before = () if line.token is None else (line.token,)

    def body(*refs):
        start = n_in + len(before)
        refs[start + n_out][...] = jnp.zeros((8, LANES), jnp.float32)
        kernel(*refs[:n_in], *refs[start : start + n_out], *refs[start + n_out + 1 :])

    run = pl.pallas_call(
        body,
        out_shape=[*outs, array((8, LANES), jnp.float32)],
        in_specs=[*in_specs, *[HBM] * len(before)],
        out_specs=[*places, VMEM],
        scratch_shapes=scratch,
        input_output_aliases=aliases,
        compiler_params=pltpu.CompilerParams(vmem_limit_bytes=VMEM_LIMIT),
        cost_estimate=LITTLE,
        name=name,
    )

    def go(*operands):
        *results, line.token = run(*operands, *before)
        return results[0] if single else results

    return go


def marks_of(marks, place, cols, chunk):
    position = (place * cols + chunk * LANES) // CH
    return marks[0, position], marks[1, position]


def mask_kernel(place, marks, group, image, out, held, sem):
    rows, cols = image.shape
    copy = pltpu.make_async_copy(image, held, sem)
    copy.start()
    second = jnp.broadcast_to(jnp.where(group[...] == 1, 1.0, 0.0), (8, rows)).T[:, 0:1] > 0.5
    copy.wait()
    for chunk in range(cols // LANES):
        zero, one = marks_of(marks, place[0], cols, chunk)
        keep = wide(jnp.where(second, one, zero))
        lanes = slice(chunk * LANES, (chunk + 1) * LANES)
        out[:, lanes] = low(wide(held[:, lanes]) * keep)


def mask_image(place, marks, group, image):
    return call(
        mask_kernel,
        array(image.shape, jnp.bfloat16),
        [SMEM, SMEM, VMEM, ANY],
        VMEM,
        "mask_image",
        [pltpu.VMEM(image.shape, jnp.bfloat16), pltpu.SemaphoreType.DMA],
    )(place, marks, group, image)


def in_hbm(x):
    return pltpu.with_memory_space_constraint(x, pltpu.HBM)


def dot(x, y):
    return jnp.dot(x, y, preferred_element_type=jnp.float32)


def products(where, ks, mine, other, held, sems, emit):
    cols = held.shape[2]

    def copies(i):
        block = 2 * (where[0] ^ ks[i]) + where[1]
        rows = pl.ds(pl.multiple_of(block * cols, cols), cols)
        return [
            pltpu.make_async_copy(weight.at[rows, :], held.at[i, side], sems.at[i, side])
            for side, weight in enumerate((mine, other))
        ]

    for i in range(len(ks)):
        for copy in copies(i):
            copy.start()
    for i in range(len(ks)):
        for copy in copies(i):
            copy.wait()
        emit(i, held[i, 0], held[i, 1])


def open_kernel(where, p0, p1, p2, mine, other, keep, send, last, slot, held, sems):
    pieces = (p0, p1, p2)
    cols = p0.shape[1]
    ahead = []
    for at, (k, out) in enumerate(((3, last), (where[3], slot))):
        block = 2 * (where[0] ^ k) + where[1]
        rows = pl.ds(pl.multiple_of(block * cols, cols), cols)
        for side, weight in enumerate((mine, other)):
            ahead.append(
                pltpu.make_async_copy(weight.at[rows, :], out.at[side], sems.at[3 + at, side])
            )

    def emit(i, own_block, other_block):
        if i == 0:
            for copy in ahead:
                copy.start()
            keep[...] = dot(p0[...], own_block)
            send[...] = dot(p0[...], other_block)
        else:
            keep[...] += dot(pieces[i][...], own_block)
            send[...] += dot(pieces[i][...], other_block)

    products(where, (0, 1, 2), mine, other, held, sems, emit)
    for copy in ahead:
        copy.wait()


def forward_open(where, p0, p1, p2, mine, other):
    rows, cols = p0.shape
    units = mine.shape[1]
    blocks = pltpu.VMEM((2, cols, units), jnp.bfloat16)
    return call(
        open_kernel,
        [array((rows, units), jnp.float32)] * 2 + [blocks] * 2,
        [SMEM] + [VMEM] * 3 + [HBM] * 2,
        [VMEM] * 4,
        "forward_open",
        [pltpu.VMEM((3, 2, cols, units), jnp.bfloat16), pltpu.SemaphoreType.DMA((5, 2))],
    )(where, p0, p1, p2, in_hbm(mine), in_hbm(other))


def close_kernel(p3, weights, keep, send, out, sent):
    sent[...] = send[...] + dot(p3[...], weights[1])
    out[...] = keep[...] + dot(p3[...], weights[0])


def forward_close(p3, weights, keep, send):
    return call(
        close_kernel,
        [array(keep.shape, jnp.float32)] * 2,
        [VMEM] * 4,
        [VMEM] * 2,
        "forward_close",
    )(p3, weights, keep, send)


def slot_kernel(weights, dz_t, dzo_t, out):
    out[...] = low(dot(weights[0], dz_t[...]) + dot(weights[1], dzo_t[...]))


def first_slot(weights, dz_t, dzo_t):
    return call(
        slot_kernel,
        array((weights.shape[1], dz_t.shape[1]), jnp.bfloat16),
        [VMEM] * 3,
        VMEM,
        "first_slot",
    )(weights, dz_t, dzo_t)


def tower_math(pre, bias, unit_a, unit_b, upper_a, upper_b, dz, dz_t, sums):
    pre = pre + bias[...]
    sigma = jax.nn.sigmoid(pre)
    hidden = pre * sigma
    cot_a = wide(upper_a[...])
    cot_b = wide(upper_b[...])
    dhid = unit_a[...] * cot_a + unit_b[...] * cot_b
    dpre = dhid * (sigma * (1.0 + pre * (1.0 - sigma)))
    dz[...] = low(dpre)
    dz_t[...] = low(dpre).T
    sums[0:1, :] = jnp.sum(dpre, axis=0, keepdims=True)
    sums[1:2, :] = jnp.sum(cot_a * hidden, axis=0, keepdims=True)
    sums[2:3, :] = jnp.sum(cot_b * hidden, axis=0, keepdims=True)
    sums[3:4, :] = jnp.zeros_like(sums[3:4, :])
    return hidden


def first_kernel(own, got, bias, stitch, upper_a, upper_b, dz, dz_t, sums, hidden):
    hidden[...] = tower_math(
        own[...] + got[...],
        bias[0:1, :],
        stitch[0:1, :],
        stitch[2:3, :],
        upper_a,
        upper_b,
        dz,
        dz_t,
        sums,
    )


def second_kernel(own, got, earlier, bias, stitch, upper_a, upper_b, dz, dz_t, sums, local):
    hidden = tower_math(
        own[...] + got[...],
        bias[1:2, :],
        stitch[1:2, :],
        stitch[3:4, :],
        upper_a,
        upper_b,
        dz,
        dz_t,
        sums,
    )
    rows = hidden.shape[0]
    before = earlier[...]
    local[0:rows, :] = low(stitch[0:1, :] * before + stitch[1:2, :] * hidden)
    local[rows : 2 * rows, :] = low(stitch[2:3, :] * before + stitch[3:4, :] * hidden)


def tower(kernel, name, last, *operands):
    rows, units = operands[0].shape
    return call(
        kernel,
        [
            array((rows, units), jnp.bfloat16),
            far_array((units, rows), jnp.bfloat16),
            array((4, units), jnp.float32),
            last,
        ],
        [VMEM] * len(operands),
        [VMEM] * 4,
        name,
    )(*operands)


def part_kernel(slots, where, mine, other, dz_t, dzo_t, *refs):
    *outs, held, sems = refs
    cols = held.shape[2]

    def emit(i, own_block, other_block):
        _, at, block = slots[i]
        total = dot(own_block, dz_t[...]) + dot(other_block, dzo_t[...])
        outs[at][block * cols : (block + 1) * cols, :] = total.astype(outs[at].dtype)

    products(where, [where[3 + slot] for slot, _, _ in slots], mine, other, held, sems, emit)


def parts(slots, outs, where, mine, other, dz_t, dzo_t):
    units, rows = dz_t.shape
    cols = mine.shape[0] // 8
    return call(
        functools.partial(part_kernel, slots),
        [far_array((blocks * cols, rows), dtype) for blocks, dtype in outs],
        [SMEM, HBM, HBM, VMEM, VMEM],
        [VMEM] * len(outs),
        "parts",
        [
            pltpu.VMEM((len(slots), 2, cols, units), jnp.bfloat16),
            pltpu.SemaphoreType.DMA((len(slots), 2)),
        ],
    )(where, in_hbm(mine), in_hbm(other), dz_t, dzo_t)


def choose_kernel(where, at_end, in_middle, out, sem):
    for flag, source in enumerate((at_end, in_middle)):
        pl.when(where[2] == flag)(pltpu.make_async_copy(source, out, sem).start)
    pltpu.make_async_copy(at_end, out, sem).wait()


def choose(where, at_end, in_middle):
    return call(
        choose_kernel,
        array(at_end.shape, at_end.dtype),
        [SMEM, ANY, ANY],
        VMEM,
        "choose",
        [pltpu.SemaphoreType.DMA],
    )(where, at_end, in_middle)


def join_kernel(where, one, at_end, in_middle, out, sems):
    rows = one.shape[0]
    copies = [pltpu.make_async_copy(one, out.at[pl.ds(0, rows), :], sems.at[0])]
    copies[0].start()
    rest = out.at[pl.ds(rows, rows), :]
    for flag, source in enumerate((at_end, in_middle)):
        pl.when(where[2] == flag)(pltpu.make_async_copy(source, rest, sems.at[1]).start)
    copies[0].wait()
    pltpu.make_async_copy(at_end, rest, sems.at[1]).wait()


def join(where, one, at_end, in_middle):
    rows, cols = one.shape
    return call(
        join_kernel,
        array((2 * rows, cols), one.dtype),
        [SMEM] + [ANY] * 3,
        VMEM,
        "join",
        [pltpu.SemaphoreType.DMA((2,))],
    )(where, one, at_end, in_middle)


def lay_kernel(where, low, high, far_low, far_high, out_a, out_b, stage, sems):
    rows = out_a.shape[0]
    units = low.shape[1]
    pieces = []
    for side, (first, second) in enumerate(((low, high), (far_low, far_high))):
        for k in range(4):
            block = 2 * (where[0] ^ k) + (where[1] ^ side)
            lanes = pl.ds(pl.multiple_of(block * units, units), units)
            source = (first, second)[k // 2]
            for half in range(2):
                at = pl.ds((2 * (k % 2) + half) * rows, rows)
                sem = sems.at[half, 4 * side + k]
                pieces.append(
                    pltpu.make_async_copy(source.at[at, :], stage.at[half, :, lanes], sem)
                )
    gives = [
        pltpu.make_async_copy(stage.at[half], out, sems.at[half, 8])
        for half, out in enumerate((out_a, out_b))
    ]
    for copy in pieces:
        copy.start()
    for half in range(2):
        for copy in pieces[half::2]:
            copy.wait()
        gives[half].start()
    for give in gives:
        give.wait()


def lay_out(where, low, high, far_low, far_high):
    rows, units = low.shape[0] // 4, low.shape[1]
    stitched = pltpu.HBM((rows, 8 * units), jnp.bfloat16)
    return call(
        lay_kernel,
        [stitched, stitched],
        [SMEM] + [ANY] * 4,
        [HBM] * 2,
        "lay_out",
        [
            pltpu.VMEM((2, rows, 8 * units), jnp.bfloat16),
            pltpu.SemaphoreType.DMA((2, 9)),
        ],
    )(where, low, high, far_low, far_high)


def add_kernel(at, one, two, out):
    rows = out.shape[0]
    out[...] = low(wide(one[at : at + rows, :]) + wide(two[0:rows, :]))


def add(one, two, block=0, rows=None):
    rows = rows or min(one.shape[0], two.shape[0])
    return call(
        functools.partial(add_kernel, block * rows),
        far_array((rows, one.shape[1]), jnp.bfloat16),
        [VMEM, VMEM],
        VMEM,
        "add",
    )(one, two)


def finish_kernel(
    block, where, marks, group, kept, third, cross, last, out, held, own, done, sems
):
    second = group[...] == 1
    cols = own.shape[0]
    tile = cols // 3

    def fetch(t):
        rows = pl.ds(t * tile, tile)
        copies = [pltpu.make_async_copy(kept.at[rows, :], own.at[rows, :], sems.at[t, 3])]
        for n, source in enumerate((third, cross, last)):
            start = block * cols + t * tile if n == 0 else t * tile
            part = source.at[pl.ds(start, tile), :]
            copies.append(pltpu.make_async_copy(part, held.at[n, rows, :], sems.at[t, n]))
        return copies

    def give(t):
        rows = pl.ds(t * tile, tile)
        return pltpu.make_async_copy(done.at[rows, :], out.at[rows, :], sems.at[t, 4])

    for t in range(3):
        for copy in fetch(t):
            copy.start()
    for t in range(3):
        for copy in fetch(t):
            copy.wait()
        for chunk in range(t * tile // LANES, (t + 1) * tile // LANES):
            zero, one = marks_of(marks, where[8], cols, chunk)
            keep = wide(jnp.where(second, one, zero))
            rows = slice(chunk * LANES, (chunk + 1) * LANES)
            total = own[rows, :] + wide(held[0, rows, :])
            total += wide(held[1, rows, :]) + wide(held[2, rows, :])
            done[rows, :] = low(total * keep)
        give(t).start()
    for t in range(3):
        give(t).wait()


def finish(block, where, marks, group, kept, third, cross, last):
    return call(
        functools.partial(finish_kernel, block),
        pltpu.HBM(kept.shape, jnp.bfloat16),
        [SMEM, SMEM, VMEM] + [HBM] * 4,
        HBM,
        "finish",
        [
            pltpu.VMEM((3, *kept.shape), jnp.bfloat16),
            pltpu.VMEM(kept.shape, jnp.float32),
            pltpu.VMEM(kept.shape, jnp.bfloat16),
            pltpu.SemaphoreType.DMA((3, 5)),
        ],
    )(where, marks, group, *[in_hbm(x) for x in (kept, third, cross, last)])


def pack_kernel(where, p0, p1, p2, p3, dz, sums, given, out, sems):
    rows, units = dz.shape
    cols = p0.shape[1]
    for q in range(4):
        block = out.at[q, pl.ds(0, rows), pl.ds(0, cols)]
        for index, piece in enumerate((p0, p1, p2, p3)):
            start = pltpu.make_async_copy(piece, block, sems.at[q]).start
            pl.when(where[0] ^ q == index)(start)
    extra = jnp.zeros((EXTRA, cols + units), jnp.bfloat16)
    for q in range(4):
        out[q, rows : rows + EXTRA, :] = extra
        out[q, 0:rows, cols : cols + units] = dz[...]
    for k in range(3):
        rest = sums[k : k + 1, :]
        for term in range(3):
            piece = low(rest)
            row = rows + 3 * k + term
            for q in range(4):
                out[q, row : row + 1, cols : cols + units] = piece
            rest = rest - wide(piece)
    gives = [pltpu.make_async_copy(out.at[q], given.at[q], sems.at[4 + q]) for q in range(4)]
    for q in range(4):
        block = out.at[q, pl.ds(0, rows), pl.ds(0, cols)]
        pltpu.make_async_copy(p0, block, sems.at[q]).wait()
        gives[q].start()
    for give in gives:
        give.wait()


def pack(where, pieces, dz, sums):
    rows, units = dz.shape
    cols = pieces[0].shape[1]
    return call(
        pack_kernel,
        pltpu.HBM((4, rows + EXTRA, cols + units), jnp.bfloat16),
        [SMEM] + [ANY] * 4 + [VMEM] * 2,
        HBM,
        "pack",
        [
            pltpu.VMEM((4, rows + EXTRA, cols + units), jnp.bfloat16),
            pltpu.SemaphoreType.DMA((8,)),
        ],
    )(where, *pieces, dz, sums)


def weight_kernel(sides, where, *refs):
    n = len(sides)
    images_of, dz_of = refs[:n], refs[n]
    *outs, images, dzs, tiles, sems = refs[n + 1 + (sides == (1,)) :]
    out = outs[0]
    rows, units = dzs.shape[1:]
    cols = images.shape[3]
    tile = tiles.shape[1]
    steps = cols // tile

    def fetch(q):
        source = dz_of.at[q, pl.ds(0, rows), pl.ds(cols, units)]
        return pltpu.make_async_copy(source, dzs.at[q], sems.at[q])

    def block(i, q):
        image = images_of[i].at[q, pl.ds(0, rows), pl.ds(0, cols)]
        return pltpu.make_async_copy(image, images.at[i, q], sems.at[4 + 4 * i + q])

    def give(i, t):
        at = pl.multiple_of((where[1] ^ sides[i]) * cols + t * tile, tile)
        slot = i * steps + t
        return pltpu.make_async_copy(
            tiles.at[slot], out.at[pl.ds(at, tile), :], sems.at[12 + slot]
        )

    for q in range(4):
        fetch(q).start()
    for i in range(n):
        for q in range(4):
            block(i, q).start()
    for q in range(4):
        fetch(q).wait()
    for i in range(n):
        for q in range(4):
            block(i, q).wait()
        if len(outs) > 1:
            for q in range(4):
                pltpu.make_async_copy(images.at[i, q], outs[1].at[q], sems.at[4 + q]).start()
        for t in range(steps):
            total = None
            for q in range(4):
                term = lax.dot_general(
                    images[i, q, :, t * tile : (t + 1) * tile],
                    dzs[q],
                    (((0,), (0,)), ((), ())),
                    preferred_element_type=jnp.float32,
                )
                total = term if total is None else total + term
            tiles[i * steps + t] = total
            give(i, t).start()
    for i in range(n):
        for t in range(steps):
            give(i, t).wait()
    if len(outs) > 1:
        for q in range(4):
            pltpu.make_async_copy(images.at[0, q], outs[1].at[q], sems.at[4 + q]).wait()


def weight_grad(sides, rows, cols, where, images, dz, *before):
    units = dz.shape[2] - cols
    tile = cols // 3
    n = len(sides)
    outs = [pltpu.HBM((2 * cols, units), jnp.float32)]
    if sides == (0,):
        outs.append(pltpu.HBM((4, rows, cols), jnp.bfloat16))
    return call(
        functools.partial(weight_kernel, sides),
        outs if len(outs) > 1 else outs[0],
        [SMEM] + [ANY] * (n + 1) + [HBM] * len(before),
        [HBM] * len(outs) if len(outs) > 1 else HBM,
        "weight_grad",
        [
            pltpu.VMEM((n, 4, rows, cols), jnp.bfloat16),
            pltpu.VMEM((4, rows, units), jnp.bfloat16),
            pltpu.VMEM((3 * n, tile, units), jnp.float32),
            pltpu.SemaphoreType.DMA((18,)),
        ],
        {n + 2: 0} if before else {},
    )(where, *images, dz, *before)


def sums_kernel(rows, cols, got_a, got_b, bias, stitch, terms, sems):
    units = bias.shape[1]
    copies = [
        pltpu.make_async_copy(
            got.at[:, pl.ds(rows, EXTRA), pl.ds(cols, units)], terms.at[side], sems.at[side]
        )
        for side, got in enumerate((got_a, got_b))
    ]
    for copy in copies:
        copy.start()
    for copy in copies:
        copy.wait()
    for side in range(2):
        totals = []
        for k in range(3):
            each = [
                (
                    wide(terms[side, q, 3 * k + 2 : 3 * k + 3, :])
                    + wide(terms[side, q, 3 * k + 1 : 3 * k + 2, :])
                )
                + wide(terms[side, q, 3 * k : 3 * k + 1, :])
                for q in range(4)
            ]
            totals.append((each[0] + each[1]) + (each[2] + each[3]))
        bias[side : side + 1, :] = totals[0]
        stitch[side : side + 1, :] = totals[1]
        stitch[2 + side : 3 + side, :] = totals[2]


def total_sums(rows, cols, got_a, got_b):
    units = got_a.shape[2] - cols
    return call(
        functools.partial(sums_kernel, rows, cols),
        [array((2, units), jnp.float32), array((4, units), jnp.float32)],
        [ANY, ANY],
        [VMEM, VMEM],
        "total_sums",
        [pltpu.VMEM((2, 4, EXTRA, units), jnp.bfloat16), pltpu.SemaphoreType.DMA((2,))],
    )(got_a, got_b)


def swap(x):
    return lax.ppermute(x, "mp", SWAP_CORE)


def along(x):
    return lax.ppermute(x, "mp", NEAR_Z)


def across(x):
    return lax.ppermute(x, "mp", FAR_Z)


def inward(x):
    return lax.ppermute(x, "mp", ENDS_IN)


def between(x):
    return lax.ppermute(x, "mp", MIDS)


def outward(x):
    return lax.ppermute(x, "mp", ENDS_OUT)


def exchange(x):
    return lax.all_to_all(x, "dp", 0, 0)


def fast_shards(
    image_a,
    image_b,
    image_group,
    position_mask,
    weight_a,
    weight_b,
    tower_bias,
    stitch,
    cotan_a,
    cotan_b,
):
    rows, cols = image_a.shape
    units = weight_a.shape[1]
    place = lax.axis_index("mp").astype(jnp.int32)
    z = place // 2
    core = place % 2
    quarter = lax.axis_index("dp").astype(jnp.int32)
    middle = ((z == 1) | (z == 2)).astype(jnp.int32)
    slots = jnp.take(jnp.asarray(SLOTS, jnp.int32), z, axis=0) ^ z
    where = jnp.concatenate(
        [jnp.stack([z, core, middle]), slots, jnp.stack([quarter, place])]
    ).astype(jnp.int32)
    group = image_group[None, :]
    line.token = None
    bf16, f32 = jnp.bfloat16, jnp.float32
    send, wait = line.send, line.wait

    whole_a = swap(weight_a)
    whole_b = swap(weight_b)
    def masked(k, image):
        spot = (2 * (z ^ k) + core)[None]
        return mask_image(spot, position_mask, group, image)

    raw2 = across(image_a)
    raw1 = along(image_a)
    b0 = masked(0, in_hbm(image_b))
    a0 = masked(0, in_hbm(image_a))
    raw1, raw2 = wait(raw1, raw2)
    raw3 = send(along, raw2)
    b_mid = send(between, b0)
    b1 = send(along, b0)
    a1 = masked(1, raw1)
    a2 = masked(2, raw2)
    whole_a, whole_b = wait(whole_a, whole_b)
    keep_a, give_a, last_a, slot_a = forward_open(where, a0, a1, a2, weight_a, whole_a)
    a3 = masked(3, wait(raw3))
    own_a, sent_a = forward_close(a3, last_a, keep_a, give_a)
    got_sum = wait(send(swap, sent_a))
    dz_a, dzt_a, sums_a, hidden_a = tower(
        first_kernel,
        "tower_a",
        far_array((rows, units), f32),
        own_a,
        got_sum,
        tower_bias,
        stitch,
        cotan_a,
        cotan_b,
    )
    dzo_a = send(swap, dzt_a)
    packed_a = pack(where, (a0, a1, a2, a3), dz_a, sums_a)
    b1, b_mid = wait(b1, b_mid)
    got_a = send(exchange, packed_a)
    b_end = send(outward, b_mid)
    b_mid2 = send(between, b1)
    dzo_a = wait(dzo_a)
    first_a = first_slot(slot_a, dzt_a, dzo_a)
    in1_a = send(inward, first_a)
    second_a, third_a, kept_a = parts(
        ((1, 0, 0), (2, 1, 0), (3, 2, 0)),
        [(1, bf16), (1, bf16), (1, f32)],
        where,
        weight_a,
        whole_a,
        dzt_a,
        dzo_a,
    )
    in2_a = send(inward, second_a)
    b_mid2 = wait(b_mid2)
    b_end2 = send(outward, b_mid2)
    b_end = wait(b_end)
    b2 = choose(where, b_end, b_mid2)
    keep_b, give_b, last_b, slot_b = forward_open(where, b0, b1, b2, weight_b, whole_b)
    in1_a = wait(in1_a)
    cross1_a = send(between, add(first_a, in1_a))
    b_end2 = wait(b_end2)
    b3 = choose(where, b_end2, b_mid)
    own_b, sent_b = forward_close(b3, last_b, keep_b, give_b)
    got_sum = send(swap, sent_b)
    in2_a = wait(in2_a)
    sum2_a = add(second_a, in2_a)
    got_sum = wait(got_sum)
    dz_b, dzt_b, sums_b, local = tower(
        second_kernel,
        "tower_b",
        far_array((2 * rows, units), bf16),
        own_b,
        got_sum,
        hidden_a,
        tower_bias,
        stitch,
        cotan_a,
        cotan_b,
    )
    dzo_b = send(swap, dzt_b)
    packed_b = pack(where, (b0, b1, b2, b3), dz_b, sums_b)
    cross1_a = wait(cross1_a)
    sum3_a = add(third_a, cross1_a)
    got_a = wait(got_a)
    far_a = send(swap, got_a)
    got_b = send(exchange, packed_b)
    cross2_a = send(between, sum2_a)
    dzo_b, far_a = wait(dzo_b, far_a)
    first_b = first_slot(slot_b, dzt_b, dzo_b)
    in1_b = send(inward, first_b)
    out_a = send(outward, sum3_a)
    s1 = send(along, local)
    s_mid = send(between, local)
    second_b, third_b, kept_b = parts(
        ((1, 0, 0), (2, 1, 0), (3, 2, 0)),
        [(1, bf16), (1, bf16), (1, f32)],
        where,
        weight_b,
        whole_b,
        dzt_b,
        dzo_b,
    )
    grad_weight_a = weight_grad((0, 1), rows, cols, where, (got_a, far_a), got_a)
    cross2_a, out_a = wait(cross2_a, out_a)
    in1_b = wait(in1_b)
    cross1_b = send(between, add(first_b, in1_b))
    thirds = join(where, third_b, third_a, third_a)
    in2_b = send(inward, second_b)
    in3 = send(inward, thirds)
    s1, s_mid = wait(s1, s_mid)
    s_end = send(outward, s_mid)
    s_mid2 = send(between, s1)
    low_half = join(where, local, s1, s1)
    cross1_b = wait(cross1_b)
    out_b = send(outward, add(third_b, cross1_b))
    in2_b = wait(in2_b)
    cross2_b = send(between, add(second_b, in2_b))
    s_end, s_mid2 = wait(s_end, s_mid2)
    s_end2 = send(outward, s_mid2)
    s2 = choose(where, s_end, s_mid2)
    got_b = wait(got_b)
    grad_bias, grad_stitch = total_sums(rows, cols, got_a, got_b)
    half_b, block_b = weight_grad((0,), rows, cols, where, (got_b,), got_b)
    in3, out_b, cross2_b = wait(in3, out_b, cross2_b)
    grad_image_b = finish(0, where, position_mask, group, kept_b, in3, cross2_b, out_b)
    s_end2 = wait(s_end2)
    high = join(where, s2, s_end2, s_mid)
    far_high = send(swap, high)
    far_low = send(swap, low_half)
    far_b = send(swap, block_b)
    grad_image_a = finish(1, where, position_mask, group, kept_a, in3, cross2_a, out_a)
    grad_weight_b = weight_grad((1,), rows, cols, where, (far_b,), got_b, half_b)
    stitched_a, stitched_b = lay_out(where, low_half, high, far_low, far_high)
    return (
        stitched_a,
        stitched_b,
        grad_image_a,
        grad_image_b,
        grad_weight_a,
        grad_weight_b,
        grad_bias,
        grad_stitch,
    )


def solution(mesh):
    placed = (
        P("dp", "mp"),
        P("dp", "mp"),
        P("dp"),
        P(),
        P(None, "mp"),
        P(None, "mp"),
        P(None, "mp"),
        P(None, "mp"),
        P("dp", "mp"),
        P("dp", "mp"),
    )
    fits = mesh.shape["dp"] == 4 and mesh.shape["mp"] == 8
    return jax.shard_map(
        fast_shards if fits else general_shards,
        mesh=mesh,
        in_specs=placed,
        out_specs=(
            P("dp", None),
            P("dp", None),
            P("mp", "dp"),
            P("mp", "dp"),
            P("dp", "mp"),
            P("dp", "mp"),
            P(None, "mp"),
            P(None, "mp"),
        ),
        check_vma=False,
    )
```
